32 devices in a mesh: plane: 4 (over x, core), tile: 8 (over z, y).
Axes of the slice: x: 2, y: 2, z: 4, core: 2. Of those that a mesh axis runs over, the one named last changes fastest.
Arguments:
- primal: float32 [5, 8, 32, 512], P(None, 'plane', 'tile'), may hold values from -6 to 6
- dual: float32 [5, 8, 8, 1024], P(None, 'plane', 'tile'), may hold values from -6 to 6
- measured: float32 [8, 8, 1024], P('plane', 'tile'), may hold values from -6 to 6
- footprint_weights: float32 [8, 8, 12, 128, 128], P('tile'), may hold values from -0.21875 to 0.21875
- pixel_index: int32 [8, 8, 12], P('tile'), may hold values from 0 to 15
- bin_index: int32 [8, 8, 12], replicated, may hold values from 0 to 7
- slot_count: int32 [8, 8], P('tile'), may hold values from 6 to 12, as said below
- dual_kernel: float32 [32, 7, 3, 3, 3], replicated, may hold values from -0.4375 to 0.4375
- dual_bias: float32 [32], replicated, may hold values from -1.5 to 1.5
- dual_slope: float32 [32], replicated, may hold values from 0.05 to 0.8
- dual_mixing: float32 [5, 32], replicated, may hold values from -1 to 1
- dual_shift: float32 [5], replicated, may hold values from -1.5 to 1.5
- primal_kernel: float32 [32, 6, 3, 3, 3], replicated, may hold values from -0.5 to 0.5
- primal_bias: float32 [32], replicated, may hold values from -1.5 to 1.5
- primal_slope: float32 [32], replicated, may hold values from 0.05 to 0.8
- primal_mixing: float32 [5, 32], replicated, may hold values from -1 to 1
- primal_shift: float32 [5], replicated, may hold values from -1.5 to 1.5
Outputs:
- new_primal: float32 [5, 8, 32, 512], P(None, 'plane', 'tile')
- new_dual: float32 [5, 8, 8, 1024], P(None, 'plane', 'tile')
The draws below stay inside these ranges and needn't reach their ends.
Inputs may be any that keep to these rules, and one draw needn't show every extreme that they name: slot_count is at least 6 everywhere, and equals 12 for some strip and angle in every draw.
All inputs are finite; a program needn't handle non-finite values.
Results may differ from the reference program's by a relative error of at most 0.0003.
Values sent between devices are 32-bit elements; how exact they have to be, the bound alone decides.
A program may use at most 64 MiB of HBM per device.

```python
import math
import jax
import jax.numpy as jnp
from jax import lax

NCOL = 512
BINS = 1024
BLK = 128
SLOTS = 12
CH = 32
MEM = 5
ANGLES = 8
STRIPS = 8
PLANES = 8
NROW = 32
PIXBLK = 16
BINBLK = 8


def draw_slot_count(key, part):
    key_counts, key_strip, key_angle = jax.random.split(jax.random.fold_in(key, 17), 3)
    counts = jax.random.randint(key_counts, (STRIPS, ANGLES), SLOTS // 2, SLOTS + 1)
    strip_pick = jax.random.randint(key_strip, (), 0, STRIPS)
    angle_pick = jax.random.randint(key_angle, (), 0, ANGLES)
    return counts.at[strip_pick, angle_pick].set(SLOTS).astype(jnp.int32)


def touch_ends(drawn, own_key, low, high):
    place = [jax.random.randint(jax.random.fold_in(own_key, axis), (), 0, length) for axis, length in enumerate(drawn.shape)]
    main_axis = drawn.shape.index(max(drawn.shape))
    next_to = place[:main_axis] + [(place[main_axis] + 1) % drawn.shape[main_axis]] + place[main_axis + 1:]
    return drawn.at[tuple(place)].set(low).at[tuple(next_to)].set(high)


def raised(entries, rng, source, target, blocks, factor):
    owner, partner = [(jnp.arange(entries.shape[dim]) // (entries.shape[dim] // blocks)).reshape([-1 if axis == dim else 1 for axis in range(entries.ndim)]) for dim in (source, target)]
    chosen = jax.random.permutation(rng, blocks)[partner]
    strong = (owner == chosen) | (owner == (partner + blocks // 2) % blocks)
    return jnp.where(strong, factor * entries, entries)


def shard_levels(stream_key, shape, cuts, smallest, largest):
    factor_of = 1.0
    for dim, blocks in cuts:
        steps = jax.random.uniform(jax.random.fold_in(jax.random.fold_in(stream_key, 6), dim), (blocks,), jnp.float32, smallest / len(cuts), largest / len(cuts))
        factor_of = factor_of * jnp.repeat(jnp.exp(steps), shape[dim] // blocks).reshape((-1,) + (1,) * (len(shape) - 1 - dim))
    return factor_of


def scatter_about(own_key, dims, scale, reach, cuts=(), kind=jnp.bfloat16):
    drawn = jax.random.normal(own_key, dims, jnp.float32) * scale
    if len(cuts) > 0:
        drawn = shard_levels(own_key, dims, cuts, -0.22, 0.18) * drawn
    return jnp.clip(drawn, min=-reach, max=reach).astype(kind)


def noise_with(stream_key, dims, width, reach, shards, heavy, kind=jnp.bfloat16):
    values = width * jax.random.normal(stream_key, dims, jnp.float32)
    if shards:
        values = values * shard_levels(stream_key, dims, shards, -0.22, 0.18)
    return jnp.clip(raised(values, jax.random.fold_in(stream_key, 3), *heavy), -reach, reach).astype(kind)


def setup_inputs(seed: int = 0) -> dict:
    arg_keys = jax.random.split(jax.random.key(seed), 18)
    primal = scatter_about(arg_keys[0], (MEM, PLANES, NROW, NCOL), 1.0, 6.0, ((1, 4), (2, 8)), jnp.float32)
    dual = scatter_about(arg_keys[1], (MEM, PLANES, ANGLES, BINS), 1.0, 6.0, ((1, 4), (2, 8)), jnp.float32)
    measured = scatter_about(arg_keys[2], (PLANES, ANGLES, BINS), 1.0, 6.0, ((0, 4), (1, 8)), jnp.float32)
    footprint_weights = noise_with(arg_keys[3], (STRIPS, ANGLES, SLOTS, BLK, BLK), (SLOTS * STRIPS * BLK * BLK // BINS) ** -0.5, 0.21875, ((0, 8),), (0, 1, 8, 2.0), jnp.float32)
    pixel_index = touch_ends(jax.random.randint(arg_keys[4], (STRIPS, ANGLES, SLOTS), 0, PIXBLK), jax.random.fold_in(arg_keys[4], 1), 0, PIXBLK - 1).astype(jnp.int32)
    bin_index = touch_ends(jax.random.randint(arg_keys[5], (STRIPS, ANGLES, SLOTS), 0, BINBLK), jax.random.fold_in(arg_keys[5], 1), 0, BINBLK - 1).astype(jnp.int32)
    slot_count = draw_slot_count(jax.random.fold_in(arg_keys[17], 71), 0)
    dual_kernel = scatter_about(arg_keys[7], (CH, MEM + 2, 3, 3, 3), (27 * (MEM + 2)) ** -0.5, 0.4375, (), jnp.float32)
    dual_bias = scatter_about(arg_keys[8], (CH,), 0.3, 1.5, (), jnp.float32)
    dual_slope = jnp.clip(jnp.exp(jax.random.uniform(arg_keys[9], (CH,), jnp.float32, math.log(0.05), math.log(0.8))), 0.05, 0.8)
    dual_mixing = scatter_about(arg_keys[10], (MEM, CH), CH ** -0.5, 1.0, (), jnp.float32)
    dual_shift = scatter_about(arg_keys[11], (MEM,), 0.3, 1.5, (), jnp.float32)
    primal_kernel = scatter_about(arg_keys[12], (CH, MEM + 1, 3, 3, 3), (27 * (MEM + 1)) ** -0.5, 0.5, (), jnp.float32)
    primal_bias = scatter_about(arg_keys[13], (CH,), 0.3, 1.5, (), jnp.float32)
    primal_slope = jnp.clip(jnp.exp(jax.random.uniform(arg_keys[14], (CH,), jnp.float32, math.log(0.05), math.log(0.8))), 0.05, 0.8)
    primal_mixing = scatter_about(arg_keys[15], (MEM, CH), CH ** -0.5, 1.0, (), jnp.float32)
    primal_shift = scatter_about(arg_keys[16], (MEM,), 0.3, 1.5, (), jnp.float32)
    return dict(primal=primal, dual=dual, measured=measured, footprint_weights=footprint_weights, pixel_index=pixel_index, bin_index=bin_index, slot_count=slot_count, dual_kernel=dual_kernel, dual_bias=dual_bias, dual_slope=dual_slope, dual_mixing=dual_mixing, dual_shift=dual_shift, primal_kernel=primal_kernel, primal_bias=primal_bias, primal_slope=primal_slope, primal_mixing=primal_mixing, primal_shift=primal_shift)


HIGHEST = lax.Precision.HIGHEST


def indicator(indices, total_count):
    return (indices[..., None] == jnp.arange(total_count, dtype=jnp.int32)).astype(jnp.float32)


def network(inputs, kernel, bias_first, leak_slope, mixing, bias_last):
    padded = jnp.pad(inputs, ((0, 0), (1, 1), (1, 1), (1, 1)))
    hidden = lax.conv_general_dilated(padded[None], kernel, (1, 1, 1), "VALID", dimension_numbers=("NCDHW", "OIDHW", "NCDHW"), precision=HIGHEST)[0]
    hidden = hidden + bias_first[:, None, None, None]
    hidden = jnp.where(hidden > 0, hidden, leak_slope[:, None, None, None] * hidden)
    return jnp.einsum("oc,czyx->ozyx", mixing, hidden, precision=HIGHEST) + bias_last[:, None, None, None]


def reference(primal, dual, measured, footprint_weights, pixel_index, bin_index, slot_count, dual_kernel, dual_bias, dual_slope, dual_mixing, dual_shift, primal_kernel, primal_bias, primal_slope, primal_mixing, primal_shift):
    live_slots = (jnp.arange(SLOTS, dtype=jnp.int32) < slot_count[..., None]).astype(jnp.float32)
    source = primal[1].reshape(PLANES, STRIPS, PIXBLK, BLK).transpose(1, 0, 2, 3)

    def forward_strip(running, strip_items):
        blocks_here, weights_here, pixels_here, bins_here, live_here = strip_items
        picked = blocks_here[:, pixels_here, :]
        products = jnp.einsum("zasj,asjk->zask", picked, weights_here, precision=HIGHEST) * live_here[None, :, :, None]
        added = jnp.einsum("zask,asb->zabk", products, indicator(bins_here, BINBLK), precision=HIGHEST)
        return running + added, None

    start_sum = jnp.zeros((PLANES, ANGLES, BINBLK, BLK), jnp.float32)
    summed, _ = lax.scan(forward_strip, start_sum, (source, footprint_weights, pixel_index, bin_index, live_slots))
    projected = summed.reshape(PLANES, ANGLES, BINS)
    dual_input = jnp.concatenate([dual, projected[None], measured[None]], 0)
    new_dual = dual + network(dual_input, dual_kernel, dual_bias, dual_slope, dual_mixing, dual_shift)

    dual_blocks = new_dual[0].reshape(PLANES, ANGLES, BINBLK, BLK)
    angle_ids = jnp.arange(ANGLES, dtype=jnp.int32)[:, None]

    def backward_strip(strip_items):
        weights_here, pixels_here, bins_here, live_here = strip_items
        picked = dual_blocks[:, angle_ids, bins_here, :]
        spread = jnp.einsum("zask,asjk->zasj", picked, weights_here, precision=HIGHEST) * live_here[None, :, :, None]
        return jnp.einsum("zasj,asq->zqj", spread, indicator(pixels_here, PIXBLK), precision=HIGHEST)

    back = lax.map(backward_strip, (footprint_weights, pixel_index, bin_index, live_slots))
    back = back.transpose(1, 0, 2, 3).reshape(PLANES, NROW, NCOL)
    primal_input = jnp.concatenate([primal, back[None]], 0)
    new_primal = primal + network(primal_input, primal_kernel, primal_bias, primal_slope, primal_mixing, primal_shift)
    return new_primal, new_dual
```

```python
import functools

import jax
import jax.numpy as jnp
from jax import lax
from jax.experimental import pallas as pl
from jax.experimental.pallas import tpu as pltpu
from jax.sharding import PartitionSpec as P

F32 = jnp.float32
BF16 = jnp.bfloat16
MESH = pl.DeviceIdType.MESH
NEIGHBOURS = [(dp, dt) for dp in (-1, 0, 1) for dt in (-1, 0, 1)]
CENTRE = 4
NEW = 5


def split(x):
    high = x.astype(BF16)
    return high, (x - high.astype(F32)).astype(BF16)


def dot(a, b):
    return jnp.dot(a, b, preferred_element_type=F32)


def iota(shape, dim):
    return lax.broadcasted_iota(jnp.int32, shape, dim)


def shifted_sum(y, hidden):
    width = y.shape[1]
    lane = iota((hidden, width), 1)
    left = jnp.where(lane == 0, 0.0, pltpu.roll(y[:hidden], 1, 1))
    right = jnp.where(lane == width - 1, 0.0, pltpu.roll(y[2 * hidden :], width - 1, 1))
    return left + y[hidden : 2 * hidden] + right


def column(row, rows, repeat):
    shape = (rows, row.shape[1])
    low = iota(shape, 1) * repeat
    at = iota(shape, 0)
    hit = (at >= low) & (at < low + repeat)
    return jnp.sum(jnp.where(hit, row, 0.0), axis=1, keepdims=True)


def row_code(rows, lanes, step_rows):
    at = iota((rows, lanes), 0)
    tap = lax.shift_right_logical(at, 3)
    kz = (tap >= 3).astype(jnp.int32) + (tap >= 6).astype(jnp.int32)
    return kz * step_rows + (tap - 3 * kz), at & 7


def expand_new(kern_ref, out_ref, zs, rs, span):
    kern = kern_ref[...]
    taps = kern.shape[0]
    hidden = taps // 3
    high, low = split(kern)
    lanes = out_ref.shape[1]
    code, chan = row_code(kern.shape[1], lanes, rs + 2)
    lane = iota((kern.shape[1], lanes), 1)
    keep = lax.rem(iota((hidden, lanes), 1), 3 * span) < 2 * span
    for i in range(zs * rs):
        spread = 0.0
        for kx in range(3):
            place = code + ((i // rs) * (rs + 2) + i % rs + 3 * kx * span)
            hit = (lane == place) | (lane == place + span) | (lane == place + 2 * span)
            own = slice(kx * hidden, (kx + 1) * hidden)
            spread += dot(
                jnp.concatenate([high[own], low[own]], 0),
                jnp.where(hit & (chan == NEW), 1.0, 0.0).astype(BF16),
            )
        out_ref[i * hidden : (i + 1) * hidden, :] = jnp.where(
            keep, spread[:hidden], spread[hidden:]
        ).astype(BF16)


def known_part(kern_ref, bias_ref, cells, known_ref, zs, rs):
    hidden = bias_ref.shape[1]
    kern = kern_ref[...]
    taps = kern.shape[0]
    depth = cells.shape[0]
    lanes = -(-depth // 128) * 128
    both = jnp.concatenate(split(kern), 0)
    code, chan = row_code(kern.shape[1], lanes, rs + 2)
    base = code * 8 + chan
    lane = iota((kern.shape[1], lanes), 1)
    high, low = split(cells)
    bias = column(bias_ref[...], hidden, 1)
    for i in range(zs * rs):
        place = base + ((i // rs) * (rs + 2) + i % rs) * 8
        a = dot(both, jnp.where(lane == place, 1.0, 0.0).astype(BF16))[:, :depth].astype(BF16)
        y = dot(a, high)
        y = y[:taps] + y[taps:] + dot(a[:taps], low)
        known_ref[i * hidden : (i + 1) * hidden, :] = shifted_sum(y, hidden) + bias


def mixing_matrix(mix_ref, rows, cells):
    outs, hidden = mix_ref.shape
    lanes = cells * hidden
    mix = jnp.concatenate([mix_ref[...], jnp.zeros((8 - outs, hidden), F32)], 0)
    both = jnp.concatenate(split(mix), 0)
    at = iota((hidden, lanes), 1)
    rep = jnp.where(lax.rem(at, hidden) == iota((hidden, lanes), 0), 1.0, 0.0).astype(BF16)
    wide = dot(both, rep)
    low_row = iota((rows, 8), 1) * cells
    at_row = iota((rows, 8), 0)
    pick = jnp.where((at_row >= low_row) & (at_row < low_row + cells), 1.0, 0.0).astype(BF16)
    cell_of_lane = lax.div(iota((rows, lanes), 1), hidden)
    own = lax.rem(iota((rows, lanes), 0), cells) == cell_of_lane
    high = jnp.where(own, dot(pick, wide[:8].astype(BF16)), 0.0).astype(BF16)
    low = jnp.where(own, dot(pick, wide[8:].astype(BF16)), 0.0).astype(BF16)
    return jnp.concatenate([high, low], 0)


def finish(new_ref, a_ref, known_ref, slope_ref, mix, shift_ref, hid_high, hid_low, cells, span):
    hidden = slope_ref.shape[1]
    high, low = split(new_ref[...])
    high, low = high.astype(F32), low.astype(F32)
    stack = jnp.concatenate([high, low, high], 0)
    width = stack.shape[1]
    lane = iota(stack.shape, 1)
    left = jnp.where(lane == 0, 0.0, pltpu.roll(stack, 1, 1))
    right = jnp.where(lane == width - 1, 0.0, pltpu.roll(stack, width - 1, 1))
    stack = jnp.concatenate([left, stack, right], 0).astype(BF16)
    y = dot(a_ref[:, : 9 * span], stack)
    slope = column(slope_ref[...], hidden, 1)
    for i in range(cells):
        h = known_ref[i * hidden : (i + 1) * hidden, :] + y[i * hidden : (i + 1) * hidden]
        h = jnp.where(h > 0, h, slope * h)
        hh, hl = split(h)
        hid_high[i * hidden : (i + 1) * hidden, :] = hh
        hid_low[i * hidden : (i + 1) * hidden, :] = hl
    rows = mix.shape[0] // 2
    first = dot(mix, hid_high[...])
    out = first[:rows] + first[rows:] + dot(mix[:rows], hid_low[...])
    return out + column(shift_ref[...], rows, cells)


def body(
    plane_count,
    tile_count,
    primal_hbm,
    dual_hbm,
    measured_hbm,
    w_hbm,
    pix_hbm,
    bin_hbm,
    cnt_hbm,
    dk_hbm,
    db_hbm,
    ds_hbm,
    dm_hbm,
    dh_hbm,
    pk_hbm,
    pb_hbm,
    ps_hbm,
    pm_hbm,
    ph_hbm,
    out_primal,
    out_dual,
    primal_ref,
    dual_ref,
    measured_ref,
    pix_ref,
    bin_ref,
    cnt_ref,
    dk_ref,
    db_ref,
    ds_ref,
    dm_ref,
    dh_ref,
    pk_ref,
    pb_ref,
    ps_ref,
    pm_ref,
    ph_ref,
    dkern,
    pkern,
    moved,
    in_sem,
    wbuf,
    whigh,
    wlow,
    src_pat,
    nd_pat,
    part,
    got,
    size_ref,
    nd,
    xd,
    xp,
    proj,
    back,
    proj_rows,
    back_rows,
    ad,
    ap,
    known_d,
    known_p,
    hd_high,
    hd_low,
    hp_high,
    hp_low,
    w_sem,
    part_send,
    part_recv,
    nd_send,
    nd_recv,
    xd_send,
    xd_recv,
    xp_send,
    xp_recv,
    proj_send,
    proj_recv,
    back_send,
    back_recv,
):
    mems, zs, rs, cols = primal_hbm.shape
    bins = dual_hbm.shape[3]
    angles, slots, blk = w_hbm.shape[1], w_hbm.shape[2], w_hbm.shape[3]
    pix_blocks = rs * cols // blk
    bin_blocks = bins // blk
    col_blocks = cols // blk
    p = lax.axis_index("plane")
    t = lax.axis_index("tile")

    def angle_at(n):
        return lax.rem(t + n, tile_count)

    def near(n):
        inner = jnp.minimum(t, tile_count - 1 - t)
        away = lax.div(n + 1, 2)
        either = jnp.where(lax.rem(n, 2) == 1, t + away, t - away)
        beyond = jnp.where(t < tile_count - 1 - t, t + n - inner, t - n + inner)
        return jnp.where(n <= 2 * inner, either, beyond)

    def far(n):
        return near(tile_count - 1 - n)

    def w_copy(a):
        return pltpu.make_async_copy(w_hbm.at[0, a], wbuf.at[a], w_sem.at[a])

    inputs = (
        (primal_hbm, primal_ref),
        (pix_hbm, pix_ref),
        (bin_hbm, bin_ref),
        (cnt_hbm, cnt_ref),
        (dual_hbm, dual_ref),
        (measured_hbm, measured_ref),
        (dk_hbm, dk_ref),
        (db_hbm, db_ref),
        (ds_hbm, ds_ref),
        (dm_hbm, dm_ref),
        (dh_hbm, dh_ref),
        (pk_hbm, pk_ref),
        (pb_hbm, pb_ref),
        (ps_hbm, ps_ref),
        (pm_hbm, pm_ref),
        (ph_hbm, ph_ref),
    )
    loads = [pltpu.make_async_copy(a, b, in_sem.at[i]) for i, (a, b) in enumerate(inputs)]
    for load in loads[:4]:
        load.start()
    w_copy(far(0)).start()
    for load in loads[4:6]:
        load.start()

    @pl.loop(1, angles)
    def _(n):
        w_copy(far(n)).start()

    for load in loads[6:]:
        load.start()

    xd[...] = jnp.zeros_like(xd)
    xp[...] = jnp.zeros_like(xp)
    proj[...] = jnp.zeros_like(proj)
    back[...] = jnp.zeros_like(back)
    def exists(dp, dt):
        there = None
        for step, at, count in ((dp, p, plane_count), (dt, t, tile_count)):
            if step:
                ok = at > 0 if step < 0 else at < count - 1
                there = ok if there is None else there & ok
        return there

    barrier = pltpu.get_barrier_semaphore()

    @pl.loop(1, tile_count)
    def _(n):
        pl.semaphore_signal(barrier, inc=1, device_id=(p, angle_at(n)), device_id_type=MESH)

    for dp, dt in NEIGHBOURS:
        if dp:

            @pl.when(exists(dp, dt))
            def _():
                pl.semaphore_signal(
                    barrier, inc=1, device_id=(p + dp, t + dt), device_id_type=MESH
                )

    planes_near = (p > 0).astype(jnp.int32) + (p < plane_count - 1).astype(jnp.int32)
    tiles_near = 1 + (t > 0).astype(jnp.int32) + (t < tile_count - 1).astype(jnp.int32)
    for load in loads[:6]:
        load.wait()
    for z in range(zs):
        for c in range(mems):
            xd[1 + z, 1, c : c + 1, :] = dual_ref[c, z]
        xd[1 + z, 1, NEW + 1 : NEW + 2, :] = measured_ref[z]
        for r in range(rs):
            for c in range(mems):
                xp[1 + z, 1 + r, c : c + 1, :] = primal_ref[c, z, r : r + 1, :]

    def z_part(step, sending):
        if step == 0:
            return pl.ds(1, zs)
        if sending:
            return 1 if step < 0 else zs
        return zs + 1 if step < 0 else 0

    def r_part(step, sending, rows):
        if step == 0:
            return pl.ds(1, rows)
        if sending:
            return 1 if step < 0 else rows
        return rows + 1 if step < 0 else 0

    def cell_copy(ref, send, recv, dp, dt, rows):
        return pltpu.make_async_remote_copy(
            src_ref=ref.at[z_part(dp, True), r_part(dt, True, rows)],
            dst_ref=ref.at[z_part(dp, False), r_part(dt, False, rows)],
            send_sem=send.at[0],
            recv_sem=recv.at[0],
            device_id=(p + dp, t + dt),
            device_id_type=MESH,
        )

    def block_copy(ref, send, recv, dp, dt, span):
        k = (dp + 1) * 3 + dt + 1
        return pltpu.make_async_remote_copy(
            src_ref=ref.at[CENTRE, span(dt, True)],
            dst_ref=ref.at[8 - k, span(dt, True)],
            send_sem=send.at[0],
            recv_sem=recv.at[0],
            device_id=(p + dp, t + dt),
            device_id_type=MESH,
        )

    def all_copy(size, send, recv):
        return pltpu.make_async_remote_copy(
            src_ref=size,
            dst_ref=size,
            send_sem=send.at[0],
            recv_sem=recv.at[0],
            device_id=(p, angle_at(1)),
            device_id_type=MESH,
        )

    def each_count(act):
        for i in range(min(plane_count, 3)):
            for j in range(min(tile_count, 3)):
                if (i or plane_count == 1) and (j or tile_count == 1):
                    pl.when((planes_near == i) & (tiles_near == j + 1))(
                        functools.partial(act, i, j)
                    )

    def cells_of(ref, rows, i, j):
        units = i * rows + j * zs + i * j
        return size_ref.at[pl.ds(0, units * ref.shape[3] // blk)]

    def blocks_of(along, side, i, j):
        return size_ref.at[pl.ds(0, (i * along + (i + 1) * j * side) // 8)]

    proj_len = bin_blocks * zs
    back_len = pix_blocks * zs
    edge_len = col_blocks * zs

    def proj_span(dt, sending):
        return pl.ds(0, proj_len)

    def back_span(dt, sending):
        if dt == 0:
            return pl.ds(0, back_len)
        first = (dt < 0) == sending
        return pl.ds(0 if first else back_len - edge_len, edge_len)

    def each_neighbour(act):
        for dp, dt in NEIGHBOURS:
            if (dp, dt) != (0, 0):
                pl.when(exists(dp, dt))(functools.partial(act, dp, dt))


    row8 = iota((8, blk), 0)
    group = 8 // zs
    of_row = lax.div(row8, zs)
    z_row = lax.rem(row8, zs)

    def pattern(rows):
        out = jnp.broadcast_to(rows[0], (8, blk))
        for z in range(1, zs):
            out = jnp.where(z_row == z, jnp.broadcast_to(rows[z], (8, blk)), out)
        high, low = split(out)
        return jnp.concatenate([high.astype(F32), low.astype(F32)], 0)

    for q in range(pix_blocks):
        r, b = q // col_blocks, q % col_blocks
        src_pat[q] = pattern(
            [primal_ref[1, z, r : r + 1, b * blk : (b + 1) * blk] for z in range(zs)]
        )

    def masked(pat, target, total):
        pieces = []
        for half in (pat[:8], pat[8:]):
            for g in range(total // 8):
                pieces.append(jnp.where(of_row + g * group == target, half, 0.0))
        return jnp.concatenate(pieces, 0).astype(BF16)

    def part_copy(a):
        return pltpu.make_async_remote_copy(
            src_ref=part.at[a],
            dst_ref=got.at[lax.rem(t - a - 1 + 2 * tile_count, tile_count)],
            send_sem=part_send.at[0],
            recv_sem=part_recv.at[0],
            device_id=(p, a),
            device_id_type=MESH,
        )

    def forward(n, carry):
        a = far(n)
        w_copy(a).wait()
        high, low = split(wbuf[a].reshape(slots * blk, blk))
        whigh[a] = high
        wlow[a] = low
        left = []
        for s in range(slots):
            target = jnp.where(s < cnt_ref[0, a], bin_ref[t, a, s], -1)
            left.append(masked(src_pat[pix_ref[0, a, s]], target, proj_len))
        o = dot(jnp.concatenate(left, 1), jnp.concatenate([high, low], 1))
        part[a] = o[:proj_len, :blk] + o[proj_len:, :blk] + o[:proj_len, blk:]

        @pl.when(n == ahead)
        def _():
            pl.semaphore_wait(barrier, tile_count - 1 + planes_near * tiles_near)
            for m in range(ahead):
                part_copy(far(m)).start()

        @pl.when((n >= ahead) & (n < tile_count - 1))
        def _():
            part_copy(a).start()

        return carry

    ahead = 5
    lax.fori_loop(0, angles, forward, 0)

    each_neighbour(lambda dp, dt: cell_copy(xd, xd_send, xd_recv, dp, dt, 1).start())

    for load in loads[6:]:
        load.wait()
    hidden = db_ref.shape[1]
    moved[...] = jnp.zeros_like(moved)

    def flatten(kern):
        for kx in range(3):
            kern[kx * hidden : (kx + 1) * hidden, :] = moved[kx].T[:hidden, :]

    for kz in range(3):
        for ky in range(3):
            for kx in range(3):
                at = (kz * 3 + ky) * 8
                moved[kx, at : at + mems + 2, :hidden] = dk_ref[kz, ky, kx]
    flatten(dkern)
    d_span = -(-(zs + 2) * 3 // 8) * 8
    p_span = -(-(zs + 2) * (rs + 2) // 8) * 8
    proj_rows[...] = jnp.zeros_like(proj_rows)
    back_rows[...] = jnp.zeros_like(back_rows)
    expand_new(dkern, ad, zs, 1, d_span)
    d_rows = -(-mems * zs // 8) * 8
    p_rows = -(-mems * zs * rs // 8) * 8
    d_mix = mixing_matrix(dm_ref, d_rows, zs)
    for c in range(mems + 1):
        for kz in range(3):
            for ky in range(3):
                at = (kz * 3 + ky) * 8 + c
                taps = pk_ref[c, kz, ky]
                for kx in range(3):
                    moved[kx, at : at + 1, :hidden] = taps[kx : kx + 1]
    flatten(pkern)
    expand_new(pkern, ap, zs, rs, p_span)
    p_mix = mixing_matrix(pm_ref, p_rows, zs * rs)

    total = part[t]
    all_copy(got, part_send, part_recv).wait_recv()
    for n in range(tile_count - 1):
        total = total + got[n]
    proj[CENTRE] = total
    each_neighbour(lambda dp, dt: block_copy(proj, proj_send, proj_recv, dp, dt, proj_span).start())
    each_neighbour(lambda dp, dt: cell_copy(xp, xp_send, xp_recv, dp, dt, rs).start())
    each_count(lambda i, j: all_copy(cells_of(xd, 1, i, j), xd_send, xd_recv).wait_recv())
    known_part(dkern, db_ref, xd[...].reshape((zs + 2) * 3 * 8, bins), known_d, zs, 1)
    proj_all = functools.partial(blocks_of, proj_len, proj_len)
    back_all = functools.partial(blocks_of, back_len, edge_len)
    each_count(lambda i, j: all_copy(proj_all(i, j), proj_send, proj_recv).wait_recv())

    def source_of(at, count):
        if at == 0:
            return -1, count - 1
        if at == count + 1:
            return 1, 0
        return 0, at - 1

    for zz in range(zs + 2):
        dp, z = source_of(zz, zs)
        for aa in range(3):
            dt, _ = source_of(aa, 1)
            k = (dp + 1) * 3 + dt + 1
            at = zz * 3 + aa
            for b in range(bin_blocks):
                row = b * zs + z
                proj_rows[at : at + 1, b * blk : (b + 1) * blk] = proj[k, row : row + 1, :]

    res = finish(
        proj_rows, ad, known_d, ds_ref, d_mix, dh_ref, hd_high, hd_low, zs, d_span
    )
    lead = [res[z : z + 1] + dual_ref[0, z] for z in range(zs)]
    for b in range(bin_blocks):
        for z in range(zs):
            row = b * zs + z
            nd[t, row : row + 1, :] = lead[z][:, b * blk : (b + 1) * blk]

    def nd_copy(a):
        return pltpu.make_async_remote_copy(
            src_ref=nd.at[t],
            dst_ref=nd.at[t],
            send_sem=nd_send.at[0],
            recv_sem=nd_recv.at[t],
            device_id=(p, a),
            device_id_type=MESH,
        )

    def nd_arrival(a):
        return pltpu.make_async_remote_copy(
            src_ref=nd.at[a],
            dst_ref=nd.at[a],
            send_sem=nd_send.at[0],
            recv_sem=nd_recv.at[a],
            device_id=(p, a),
            device_id_type=MESH,
        )

    @pl.loop(1, tile_count)
    def _(n):
        nd_copy(near(tile_count - n)).start()

    for c in range(mems):
        for z in range(zs):
            at = c * zs + z
            out_dual[c, z] = res[at : at + 1] + dual_ref[c, z]

    each_count(lambda i, j: all_copy(cells_of(xp, rs, i, j), xp_send, xp_recv).wait_recv())
    known_part(
        pkern, pb_ref, xp[...].reshape((zs + 2) * (rs + 2) * 8, cols), known_p, zs, rs
    )

    def backward(n, acc):
        a = near(n)

        @pl.when(n > 0)
        def _():
            nd_arrival(a).wait_recv()

        for b in range(bin_blocks):
            nd_pat[b] = pattern([nd[a, b * zs + z : b * zs + z + 1, :] for z in range(zs)])
        for s in range(slots):
            target = jnp.where(s < cnt_ref[0, a], pix_ref[0, a, s], -1)
            left = masked(nd_pat[bin_ref[t, a, s]], target, back_len)
            rows = slice(s * blk, (s + 1) * blk)
            right = jnp.concatenate([whigh[a, rows, :], wlow[a, rows, :]], 0)
            o = lax.dot_general(
                left, right, (((1,), (1,)), ((), ())), preferred_element_type=F32
            )
            acc = acc + o
        return acc

    acc = lax.fori_loop(0, tile_count, backward, jnp.zeros((2 * back_len, 2 * blk), F32))
    back[CENTRE] = acc[:back_len, :blk] + acc[back_len:, :blk] + acc[:back_len, blk:]
    each_neighbour(lambda dp, dt: block_copy(back, back_send, back_recv, dp, dt, back_span).start())
    each_count(lambda i, j: all_copy(back_all(i, j), back_send, back_recv).wait_recv())
    for zz in range(zs + 2):
        dp, z = source_of(zz, zs)
        for rr in range(rs + 2):
            dt, r = source_of(rr, rs)
            k = (dp + 1) * 3 + dt + 1
            at = zz * (rs + 2) + rr
            for b in range(col_blocks):
                row = (r * col_blocks + b) * zs + z
                back_rows[at : at + 1, b * blk : (b + 1) * blk] = back[k, row : row + 1, :]

    res = finish(
        back_rows, ap, known_p, ps_ref, p_mix, ph_ref, hp_high, hp_low, zs * rs, p_span
    )
    for c in range(mems):
        for z in range(zs):
            at = (c * zs + z) * rs
            out_primal[c, z] = res[at : at + rs] + primal_ref[c, z]

    each_count(lambda i, j: all_copy(cells_of(xd, 1, i, j), xd_send, xd_recv).wait_send())
    each_count(lambda i, j: all_copy(cells_of(xp, rs, i, j), xp_send, xp_recv).wait_send())
    each_count(lambda i, j: all_copy(proj_all(i, j), proj_send, proj_recv).wait_send())
    each_count(lambda i, j: all_copy(back_all(i, j), back_send, back_recv).wait_send())
    all_copy(got, part_send, part_recv).wait_send()
    all_copy(got, nd_send, part_recv).wait_send()


def store(a_ref, b_ref, a_hbm, b_hbm, sem):
    copies = [
        pltpu.make_async_copy(x, y, sem.at[i])
        for i, (x, y) in enumerate(((a_ref, a_hbm), (b_ref, b_hbm)))
    ]
    for copy in copies:
        copy.start()
    for copy in copies:
        copy.wait()


def per_device(plane_count, tile_count, *args):
    (primal, dual, measured, weights, pix, bins_of, count, dk, db, ds, dm, dh, pk, pb, ps, pm, ph) = args
    mems, zs, rs, cols = primal.shape
    bins = dual.shape[3]
    angles, slots, blk = weights.shape[1:4]
    assert dual.shape[2] == 1 and angles == tile_count and 8 % zs == 0 and mems == NEW
    hidden = db.shape[0]
    proj_len = bins // blk * zs
    back_len = rs * cols // blk * zs
    d_span = -(-(zs + 2) * 3 // 8) * 8
    p_span = -(-(zs + 2) * (rs + 2) // 8) * 8
    cells = zs * rs
    most = max((6 + 2 * zs) * bins, (2 * rs + 2 * zs + 4) * cols, 9 * bins, 9 * blk) // blk
    most = max(most, 8 * proj_len // 8, (2 * back_len + 6 * rs * cols) // 8)
    vmem = pl.BlockSpec(memory_space=pltpu.VMEM)
    dma = pltpu.SemaphoreType.DMA
    operands = (
        primal, dual, measured, weights, pix, bins_of, count,
        jnp.transpose(dk, (2, 3, 4, 1, 0)), db[None], ds[None], dm, dh[None],
        jnp.transpose(pk, (1, 2, 3, 4, 0)), pb[None], ps[None], pm, ph[None],
    )
    held = pl.pallas_call(
        functools.partial(body, plane_count, tile_count),
        out_shape=(
            pltpu.VMEM(primal.shape, F32),
            pltpu.VMEM(dual.shape, F32),
        ),
        in_specs=[pl.BlockSpec(memory_space=pl.ANY)] * len(operands),
        out_specs=(vmem, vmem),
        scratch_shapes=[
            (pltpu.SMEM if x.dtype == jnp.int32 else pltpu.VMEM)(x.shape, x.dtype)
            for x in operands
            if x is not weights
        ]
        + [
            pltpu.VMEM((3 * hidden, 72), F32),
            pltpu.VMEM((3 * hidden, 72), F32),
            pltpu.VMEM((3, 72, 128), F32),
            dma((len(operands) - 1,)),
            pltpu.VMEM((angles, slots, blk, blk), F32),
            pltpu.VMEM((angles, slots * blk, blk), BF16),
            pltpu.VMEM((angles, slots * blk, blk), BF16),
            pltpu.VMEM((rs * cols // blk, 16, blk), F32),
            pltpu.VMEM((bins // blk, 16, blk), F32),
            pltpu.VMEM((tile_count, proj_len, blk), F32),
            pltpu.VMEM((tile_count - 1, proj_len, blk), F32),
            pltpu.VMEM((most, 8, blk), F32),
            pltpu.VMEM((tile_count, proj_len, blk), F32),
            pltpu.VMEM((zs + 2, 3, 8, bins), F32),
            pltpu.VMEM((zs + 2, rs + 2, 8, cols), F32),
            pltpu.VMEM((9, proj_len, blk), F32),
            pltpu.VMEM((9, back_len, blk), F32),
            pltpu.VMEM((d_span, bins), F32),
            pltpu.VMEM((p_span, cols), F32),
            pltpu.VMEM((zs * hidden, -(-9 * d_span // 128) * 128), BF16),
            pltpu.VMEM((cells * hidden, -(-9 * p_span // 128) * 128), BF16),
            pltpu.VMEM((zs * hidden, bins), F32),
            pltpu.VMEM((cells * hidden, cols), F32),
            pltpu.VMEM((zs * hidden, bins), BF16),
            pltpu.VMEM((zs * hidden, bins), BF16),
            pltpu.VMEM((cells * hidden, cols), BF16),
            pltpu.VMEM((cells * hidden, cols), BF16),
            dma((angles,)),
            dma((1,)),
            dma((1,)),
            dma((1,)),
            dma((tile_count,)),
        ]
        + [dma((1,))] * 8,
        compiler_params=pltpu.CompilerParams(
            collective_id=0, has_side_effects=True, vmem_limit_bytes=60 * 2**20
        ),
    )(*operands)
    hbm = pl.BlockSpec(memory_space=pl.ANY)
    return pl.pallas_call(
        store,
        out_shape=[jax.ShapeDtypeStruct(x.shape, F32) for x in held],
        in_specs=[vmem] * 2,
        out_specs=[hbm] * 2,
        scratch_shapes=[dma((2,))],
    )(*[pltpu.with_memory_space_constraint(x, pltpu.VMEM) for x in held])


def solution(mesh):
    in_specs = (
        P(None, "plane", "tile", None),
        P(None, "plane", "tile", None),
        P("plane", "tile", None),
        P("tile", None, None, None, None),
        P("tile", None, None),
        P(),
        P("tile", None),
    ) + (P(),) * 10
    out_specs = (P(None, "plane", "tile", None), P(None, "plane", "tile", None))
    return jax.shard_map(
        functools.partial(per_device, mesh.shape["plane"], mesh.shape["tile"]),
        mesh=mesh,
        in_specs=in_specs,
        out_specs=out_specs,
        check_vma=False,
    )
```

```python
import functools

import jax
import jax.numpy as jnp
from jax import lax
from jax.experimental import pallas as pl
from jax.experimental.pallas import tpu as pltpu
from jax.sharding import PartitionSpec as P

F32 = jnp.float32
BF16 = jnp.bfloat16
MESH = pl.DeviceIdType.MESH
NEIGHBOURS = [(dp, dt) for dp in (-1, 0, 1) for dt in (-1, 0, 1)]
CENTRE = 4
NEW = 5


def split(x):
    high = x.astype(BF16)
    return high, (x - high.astype(F32)).astype(BF16)


def dot(a, b):
    return jnp.dot(a, b, preferred_element_type=F32)


def iota(shape, dim):
    return lax.broadcasted_iota(jnp.int32, shape, dim)


def shifted_sum(y, hidden):
    width = y.shape[1]
    lane = iota((hidden, width), 1)
    left = jnp.where(lane == 0, 0.0, pltpu.roll(y[:hidden], 1, 1))
    right = jnp.where(lane == width - 1, 0.0, pltpu.roll(y[2 * hidden :], width - 1, 1))
    return left + y[hidden : 2 * hidden] + right


def column(row, rows, repeat):
    shape = (rows, row.shape[1])
    low = iota(shape, 1) * repeat
    at = iota(shape, 0)
    hit = (at >= low) & (at < low + repeat)
    return jnp.sum(jnp.where(hit, row, 0.0), axis=1, keepdims=True)


def row_code(rows, lanes, step_rows):
    at = iota((rows, lanes), 0)
    tap = lax.shift_right_logical(at, 3)
    kz = (tap >= 3).astype(jnp.int32) + (tap >= 6).astype(jnp.int32)
    return kz * step_rows + (tap - 3 * kz), at & 7


def expand_new(kern_ref, out_ref, zs, rs, span):
    kern = kern_ref[...]
    taps = kern.shape[0]
    hidden = taps // 3
    high, low = split(kern)
    lanes = out_ref.shape[1]
    code, chan = row_code(kern.shape[1], lanes, rs + 2)
    lane = iota((kern.shape[1], lanes), 1)
    keep = lax.rem(iota((hidden, lanes), 1), 3 * span) < 2 * span
    for i in range(zs * rs):
        spread = 0.0
        for kx in range(3):
            place = code + ((i // rs) * (rs + 2) + i % rs + 3 * kx * span)
            hit = (lane == place) | (lane == place + span) | (lane == place + 2 * span)
            own = slice(kx * hidden, (kx + 1) * hidden)
            spread += dot(
                jnp.concatenate([high[own], low[own]], 0),
                jnp.where(hit & (chan == NEW), 1.0, 0.0).astype(BF16),
            )
        out_ref[i * hidden : (i + 1) * hidden, :] = jnp.where(
            keep, spread[:hidden], spread[hidden:]
        ).astype(BF16)


def known_part(kern_ref, bias_ref, cells, known_ref, zs, rs):
    hidden = bias_ref.shape[1]
    kern = kern_ref[...]
    taps = kern.shape[0]
    depth = cells.shape[0]
    lanes = -(-depth // 128) * 128
    both = jnp.concatenate(split(kern), 0)
    code, chan = row_code(kern.shape[1], lanes, rs + 2)
    base = code * 8 + chan
    lane = iota((kern.shape[1], lanes), 1)
    high, low = split(cells)
    bias = column(bias_ref[...], hidden, 1)
    for i in range(zs * rs):
        place = base + ((i // rs) * (rs + 2) + i % rs) * 8
        a = dot(both, jnp.where(lane == place, 1.0, 0.0).astype(BF16))[:, :depth].astype(BF16)
        y = dot(a, high)
        y = y[:taps] + y[taps:] + dot(a[:taps], low)
        known_ref[i * hidden : (i + 1) * hidden, :] = shifted_sum(y, hidden) + bias


def mixing_matrix(mix_ref, rows, cells):
    outs, hidden = mix_ref.shape
    lanes = cells * hidden
    mix = jnp.concatenate([mix_ref[...], jnp.zeros((8 - outs, hidden), F32)], 0)
    both = jnp.concatenate(split(mix), 0)
    at = iota((hidden, lanes), 1)
    rep = jnp.where(lax.rem(at, hidden) == iota((hidden, lanes), 0), 1.0, 0.0).astype(BF16)
    wide = dot(both, rep)
    low_row = iota((rows, 8), 1) * cells
    at_row = iota((rows, 8), 0)
    pick = jnp.where((at_row >= low_row) & (at_row < low_row + cells), 1.0, 0.0).astype(BF16)
    cell_of_lane = lax.div(iota((rows, lanes), 1), hidden)
    own = lax.rem(iota((rows, lanes), 0), cells) == cell_of_lane
    high = jnp.where(own, dot(pick, wide[:8].astype(BF16)), 0.0).astype(BF16)
    low = jnp.where(own, dot(pick, wide[8:].astype(BF16)), 0.0).astype(BF16)
    return jnp.concatenate([high, low], 0)


def finish(new_ref, a_ref, known_ref, slope_ref, mix, shift_ref, hid_high, hid_low, cells, span):
    hidden = slope_ref.shape[1]
    high, low = split(new_ref[...])
    high, low = high.astype(F32), low.astype(F32)
    stack = jnp.concatenate([high, low, high], 0)
    width = stack.shape[1]
    lane = iota(stack.shape, 1)
    left = jnp.where(lane == 0, 0.0, pltpu.roll(stack, 1, 1))
    right = jnp.where(lane == width - 1, 0.0, pltpu.roll(stack, width - 1, 1))
    stack = jnp.concatenate([left, stack, right], 0).astype(BF16)
    y = dot(a_ref[:, : 9 * span], stack)
    slope = column(slope_ref[...], hidden, 1)
    for i in range(cells):
        h = known_ref[i * hidden : (i + 1) * hidden, :] + y[i * hidden : (i + 1) * hidden]
        h = jnp.where(h > 0, h, slope * h)
        hh, hl = split(h)
        hid_high[i * hidden : (i + 1) * hidden, :] = hh
        hid_low[i * hidden : (i + 1) * hidden, :] = hl
    rows = mix.shape[0] // 2
    first = dot(mix, hid_high[...])
    out = first[:rows] + first[rows:] + dot(mix[:rows], hid_low[...])
    return out + column(shift_ref[...], rows, cells)


def body(
    plane_count,
    tile_count,
    primal_hbm,
    dual_hbm,
    measured_hbm,
    w_hbm,
    pix_hbm,
    bin_hbm,
    cnt_hbm,
    dk_hbm,
    db_hbm,
    ds_hbm,
    dm_hbm,
    dh_hbm,
    pk_hbm,
    pb_hbm,
    ps_hbm,
    pm_hbm,
    ph_hbm,
    out_primal,
    out_dual,
    primal_ref,
    pix_ref,
    bin_ref,
    cnt_ref,
    dk_ref,
    db_ref,
    ds_ref,
    dm_ref,
    dh_ref,
    pk_ref,
    pb_ref,
    ps_ref,
    pm_ref,
    ph_ref,
    dkern,
    pkern,
    moved,
    in_sem,
    wbuf,
    whigh,
    wlow,
    src_pat,
    nd_pat,
    part,
    got,
    size_ref,
    nd,
    xraw,
    xside,
    prow_out,
    prow_in,
    pplane,
    pprow,
    xd,
    xp,
    proj,
    back,
    proj_rows,
    back_rows,
    ad,
    ap,
    known_d,
    known_p,
    hd_high,
    hd_low,
    hp_high,
    hp_low,
    w_sem,
    part_send,
    part_recv,
    nd_send,
    nd_recv,
    xd_send,
    xd_recv,
    near_send,
    near_recv,
    row_send,
    row_recv,
    xp_send,
    xp_recv,
    proj_send,
    proj_recv,
    back_send,
    back_recv,
):
    mems, zs, rs, cols = primal_hbm.shape
    bins = dual_hbm.shape[3]
    angles, slots, blk = w_hbm.shape[1], w_hbm.shape[2], w_hbm.shape[3]
    pix_blocks = rs * cols // blk
    bin_blocks = bins // blk
    col_blocks = cols // blk
    p = lax.axis_index("plane")
    t = lax.axis_index("tile")

    def angle_at(n):
        return lax.rem(t + n, tile_count)

    def near(n):
        inner = jnp.minimum(t, tile_count - 1 - t)
        away = lax.div(n + 1, 2)
        either = jnp.where(lax.rem(n, 2) == 1, t + away, t - away)
        beyond = jnp.where(t < tile_count - 1 - t, t + n - inner, t - n + inner)
        return jnp.where(n <= 2 * inner, either, beyond)

    def far(n):
        return near(tile_count - 1 - n)

    def w_copy(a):
        return pltpu.make_async_copy(w_hbm.at[0, a], wbuf.at[a], w_sem.at[a])

    inputs = (
        (primal_hbm, primal_ref),
        (pix_hbm, pix_ref),
        (bin_hbm, bin_ref),
        (cnt_hbm, cnt_ref),
        (dual_hbm, xraw.at[1, pl.ds(0, mems)]),
        (measured_hbm, xraw.at[1, mems]),
        (dk_hbm, dk_ref),
        (db_hbm, db_ref),
        (ds_hbm, ds_ref),
        (dm_hbm, dm_ref),
        (dh_hbm, dh_ref),
        (pk_hbm, pk_ref),
        (pb_hbm, pb_ref),
        (ps_hbm, ps_ref),
        (pm_hbm, pm_ref),
        (ph_hbm, ph_ref),
    )
    loads = [pltpu.make_async_copy(a, b, in_sem.at[i]) for i, (a, b) in enumerate(inputs)]
    for load in loads[:4]:
        load.start()
    w_copy(far(0)).start()
    for load in loads[4:6]:
        load.start()

    @pl.loop(1, angles)
    def _(n):
        w_copy(far(n)).start()

    for load in loads[6:]:
        load.start()

    for side in (0, 2):
        xraw[side] = jnp.zeros(xraw.shape[1:], F32)
    for ref in (xside, prow_in, pplane, pprow, xd, xp):
        ref[...] = jnp.zeros_like(ref)
    proj[...] = jnp.zeros_like(proj)
    back[...] = jnp.zeros_like(back)
    def exists(dp, dt):
        there = None
        for step, at, count in ((dp, p, plane_count), (dt, t, tile_count)):
            if step:
                ok = at > 0 if step < 0 else at < count - 1
                there = ok if there is None else there & ok
        return there

    barrier = pltpu.get_barrier_semaphore()

    @pl.loop(1, tile_count)
    def _(n):
        pl.semaphore_signal(barrier, inc=1, device_id=(p, angle_at(n)), device_id_type=MESH)

    for dp, dt in NEIGHBOURS:
        if dp:

            @pl.when(exists(dp, dt))
            def _():
                pl.semaphore_signal(
                    barrier, inc=1, device_id=(p + dp, t + dt), device_id_type=MESH
                )

    planes_near = (p > 0).astype(jnp.int32) + (p < plane_count - 1).astype(jnp.int32)
    tiles_near = 1 + (t > 0).astype(jnp.int32) + (t < tile_count - 1).astype(jnp.int32)
    for load in loads[:6]:
        load.wait()
    for z in range(zs):
        for c in range(mems):
            prow_out[0, c, z] = primal_ref[c, z, 0:1, :]
            prow_out[1, c, z] = primal_ref[c, z, rs - 1 : rs, :]

    odd = lax.rem(p, 2) == 1
    far_step = jnp.where(odd, 1, -1)
    far_edge = jnp.where(odd, zs - 1, 0)
    near_edge = jnp.where(odd, 0, zs - 1)
    far_there = (p + far_step >= 0) & (p + far_step < plane_count)

    def remote(src, dst, send, recv, device):
        return pltpu.make_async_remote_copy(
            src_ref=src,
            dst_ref=dst,
            send_sem=send.at[0],
            recv_sem=recv.at[0],
            device_id=device,
            device_id_type=MESH,
        )

    def dual_tile(dt):
        return remote(xraw.at[1], xraw.at[1 - dt], xd_send, xd_recv, (p, t + dt))

    def dual_far(dt):
        return remote(
            xraw.at[1, :, far_edge], xside.at[1, 1 - dt], xd_send, xd_recv, (p + far_step, t + dt)
        )

    def dual_near():
        return remote(
            xraw.at[:, :, near_edge], xside.at[0], near_send, near_recv, (p - far_step, t)
        )

    def row_tile(dt):
        side = (dt + 1) // 2
        return remote(prow_out.at[side], prow_in.at[1 - side], row_send, row_recv, (p, t + dt))

    def plane_copies(dp):
        z, side = (0, 1) if dp < 0 else (zs - 1, 0)
        to = (p + dp, t)
        return (
            remote(primal_ref.at[:, z], pplane.at[side], xp_send, xp_recv, to),
            remote(prow_in.at[:, :, z], pprow.at[side], xp_send, xp_recv, to),
        )

    def send_known():
        for dt in (-1, 1):
            pl.when(exists(0, dt))(lambda dt=dt: dual_tile(dt).start())
        pl.when(far_there)(lambda: dual_far(0).start())
        for dt in (-1, 1):
            pl.when(far_there & exists(0, dt))(lambda dt=dt: dual_far(dt).start())
        for dt in (-1, 1):
            pl.when(exists(0, dt))(lambda dt=dt: row_tile(dt).start())

    def send_planes():
        for dp in (-1, 1):

            @pl.when(exists(dp, 0))
            def _():
                for copy in plane_copies(dp):
                    copy.start()

    def block_copy(ref, send, recv, dp, dt, span):
        k = (dp + 1) * 3 + dt + 1
        return pltpu.make_async_remote_copy(
            src_ref=ref.at[CENTRE, span(dt, True)],
            dst_ref=ref.at[8 - k, span(dt, True)],
            send_sem=send.at[0],
            recv_sem=recv.at[0],
            device_id=(p + dp, t + dt),
            device_id_type=MESH,
        )

    def all_copy(size, send, recv):
        return pltpu.make_async_remote_copy(
            src_ref=size,
            dst_ref=size,
            send_sem=send.at[0],
            recv_sem=recv.at[0],
            device_id=(p, angle_at(1)),
            device_id_type=MESH,
        )

    def each_count(act):
        for i in range(min(plane_count, 3)):
            for j in range(min(tile_count, 3)):
                if (i or plane_count == 1) and (j or tile_count == 1):
                    pl.when((planes_near == i) & (tiles_near == j + 1))(
                        functools.partial(act, i, j)
                    )

    def tiles(n):
        return size_ref.at[pl.ds(0, n // (8 * blk))]

    def dual_all(act):
        for far in range(2):
            for j in range(1, min(tile_count, 3)):
                count = j * zs + far * (1 + j)
                pl.when((far_there == (far == 1)) & (tiles_near == j + 1))(
                    functools.partial(act, tiles(count * (mems + 1) * bins))
                )

    def rows_all(act):
        for j in range(1, min(tile_count, 3)):
            pl.when(tiles_near == j + 1)(functools.partial(act, tiles(j * mems * zs * cols)))

    def planes_all(act):
        for i in range(1, min(plane_count, 3)):
            pl.when(planes_near == i)(functools.partial(act, tiles(i * mems * (rs + 2) * cols)))

    def blocks_of(along, side, i, j):
        return size_ref.at[pl.ds(0, (i * along + (i + 1) * j * side) // 8)]

    proj_len = bin_blocks * zs
    back_len = pix_blocks * zs
    edge_len = col_blocks * zs

    def proj_span(dt, sending):
        return pl.ds(0, proj_len)

    def back_span(dt, sending):
        if dt == 0:
            return pl.ds(0, back_len)
        first = (dt < 0) == sending
        return pl.ds(0 if first else back_len - edge_len, edge_len)

    def each_neighbour(act):
        for dp, dt in NEIGHBOURS:
            if (dp, dt) != (0, 0):
                pl.when(exists(dp, dt))(functools.partial(act, dp, dt))


    row8 = iota((8, blk), 0)
    group = 8 // zs
    of_row = lax.div(row8, zs)
    z_row = lax.rem(row8, zs)

    def pattern(rows):
        out = jnp.broadcast_to(rows[0], (8, blk))
        for z in range(1, zs):
            out = jnp.where(z_row == z, jnp.broadcast_to(rows[z], (8, blk)), out)
        high, low = split(out)
        return jnp.concatenate([high.astype(F32), low.astype(F32)], 0)

    for q in range(pix_blocks):
        r, b = q // col_blocks, q % col_blocks
        src_pat[q] = pattern(
            [primal_ref[1, z, r : r + 1, b * blk : (b + 1) * blk] for z in range(zs)]
        )

    def masked(pat, target, total):
        pieces = []
        for half in (pat[:8], pat[8:]):
            for g in range(total // 8):
                pieces.append(jnp.where(of_row + g * group == target, half, 0.0))
        return jnp.concatenate(pieces, 0).astype(BF16)

    def part_copy(a):
        return pltpu.make_async_remote_copy(
            src_ref=part.at[a],
            dst_ref=got.at[lax.rem(t - a - 1 + 2 * tile_count, tile_count)],
            send_sem=part_send.at[0],
            recv_sem=part_recv.at[0],
            device_id=(p, a),
            device_id_type=MESH,
        )

    def forward(n, carry):
        a = far(n)
        w_copy(a).wait()
        high, low = split(wbuf[a].reshape(slots * blk, blk))
        whigh[a] = high
        wlow[a] = low
        left = []
        for s in range(slots):
            target = jnp.where(s < cnt_ref[0, a], bin_ref[t, a, s], -1)
            left.append(masked(src_pat[pix_ref[0, a, s]], target, proj_len))
        o = dot(jnp.concatenate(left, 1), jnp.concatenate([high, low], 1))
        part[a] = o[:proj_len, :blk] + o[proj_len:, :blk] + o[:proj_len, blk:]

        @pl.when(n == ahead)
        def _():
            pl.semaphore_wait(barrier, tile_count - 1 + planes_near * tiles_near)
            for m in range(ahead):
                part_copy(far(m)).start()

        @pl.when((n >= ahead) & (n < tile_count - 1))
        def _():
            part_copy(a).start()

        return carry

    ahead = angles - 1
    lax.fori_loop(0, angles, forward, 0)

    send_known()

    for load in loads[6:]:
        load.wait()
    hidden = db_ref.shape[1]
    moved[...] = jnp.zeros_like(moved)

    def flatten(kern):
        for kx in range(3):
            kern[kx * hidden : (kx + 1) * hidden, :] = moved[kx].T[:hidden, :]

    for kz in range(3):
        for ky in range(3):
            for kx in range(3):
                at = (kz * 3 + ky) * 8
                moved[kx, at : at + mems + 2, :hidden] = dk_ref[kz, ky, kx]
    flatten(dkern)
    d_span = -(-(zs + 2) * 3 // 8) * 8
    p_span = -(-(zs + 2) * (rs + 2) // 8) * 8
    proj_rows[...] = jnp.zeros_like(proj_rows)
    back_rows[...] = jnp.zeros_like(back_rows)
    expand_new(dkern, ad, zs, 1, d_span)
    d_rows = -(-mems * zs // 8) * 8
    p_rows = -(-mems * zs * rs // 8) * 8
    d_mix = mixing_matrix(dm_ref, d_rows, zs)
    for c in range(mems + 1):
        for kz in range(3):
            for ky in range(3):
                at = (kz * 3 + ky) * 8 + c
                taps = pk_ref[c, kz, ky]
                for kx in range(3):
                    moved[kx, at : at + 1, :hidden] = taps[kx : kx + 1]
    flatten(pkern)
    expand_new(pkern, ap, zs, rs, p_span)
    p_mix = mixing_matrix(pm_ref, p_rows, zs * rs)

    total = part[t]
    all_copy(got, part_send, part_recv).wait_recv()
    for n in range(tile_count - 1):
        total = total + got[n]
    proj[CENTRE] = total
    each_neighbour(lambda dp, dt: block_copy(proj, proj_send, proj_recv, dp, dt, proj_span).start())
    dual_all(lambda size: all_copy(size, xd_send, xd_recv).wait_recv())
    dual_near().start()
    for z in range(zs):
        for aa in range(3):
            for c in range(mems + 1):
                at = c if c < mems else NEW + 1
                xd[1 + z, aa, at : at + 1, :] = xraw[aa, c, z]
    low_side = jnp.where(odd, 0, 1)
    dual_near().wait_recv()
    for zz, side in ((0, low_side), (zs + 1, 1 - low_side)):
        for aa in range(3):
            for c in range(mems + 1):
                at = c if c < mems else NEW + 1
                xd[zz, aa, at : at + 1, :] = xside[side, aa, c]
    known_part(dkern, db_ref, xd[...].reshape((zs + 2) * 3 * 8, bins), known_d, zs, 1)
    proj_all = functools.partial(blocks_of, proj_len, proj_len)
    back_all = functools.partial(blocks_of, back_len, edge_len)
    each_count(lambda i, j: all_copy(proj_all(i, j), proj_send, proj_recv).wait_recv())

    def source_of(at, count):
        if at == 0:
            return -1, count - 1
        if at == count + 1:
            return 1, 0
        return 0, at - 1

    for zz in range(zs + 2):
        dp, z = source_of(zz, zs)
        for aa in range(3):
            dt, _ = source_of(aa, 1)
            k = (dp + 1) * 3 + dt + 1
            at = zz * 3 + aa
            for b in range(bin_blocks):
                row = b * zs + z
                proj_rows[at : at + 1, b * blk : (b + 1) * blk] = proj[k, row : row + 1, :]

    res = finish(
        proj_rows, ad, known_d, ds_ref, d_mix, dh_ref, hd_high, hd_low, zs, d_span
    )
    lead = [res[z : z + 1] + xraw[1, 0, z] for z in range(zs)]
    for b in range(bin_blocks):
        for z in range(zs):
            row = b * zs + z
            nd[t, row : row + 1, :] = lead[z][:, b * blk : (b + 1) * blk]

    def nd_copy(a):
        return pltpu.make_async_remote_copy(
            src_ref=nd.at[t],
            dst_ref=nd.at[t],
            send_sem=nd_send.at[0],
            recv_sem=nd_recv.at[t],
            device_id=(p, a),
            device_id_type=MESH,
        )

    def nd_arrival(a):
        return pltpu.make_async_remote_copy(
            src_ref=nd.at[a],
            dst_ref=nd.at[a],
            send_sem=nd_send.at[0],
            recv_sem=nd_recv.at[a],
            device_id=(p, a),
            device_id_type=MESH,
        )

    @pl.loop(1, tile_count)
    def _(n):
        nd_copy(near(tile_count - n)).start()

    for c in range(mems):
        for z in range(zs):
            at = c * zs + z
            out_dual[c, z] = res[at : at + 1] + xraw[1, c, z]

    rows_all(lambda size: all_copy(size, row_send, row_recv).wait_recv())
    send_planes()

    def backward(n, acc):
        a = near(n)

        @pl.when(n > 0)
        def _():
            nd_arrival(a).wait_recv()

        for b in range(bin_blocks):
            nd_pat[b] = pattern([nd[a, b * zs + z : b * zs + z + 1, :] for z in range(zs)])
        for s in range(slots):
            target = jnp.where(s < cnt_ref[0, a], pix_ref[0, a, s], -1)
            left = masked(nd_pat[bin_ref[t, a, s]], target, back_len)
            rows = slice(s * blk, (s + 1) * blk)
            right = jnp.concatenate([whigh[a, rows, :], wlow[a, rows, :]], 0)
            o = lax.dot_general(
                left, right, (((1,), (1,)), ((), ())), preferred_element_type=F32
            )
            acc = acc + o
        return acc

    acc = lax.fori_loop(0, tile_count, backward, jnp.zeros((2 * back_len, 2 * blk), F32))
    back[CENTRE] = acc[:back_len, :blk] + acc[back_len:, :blk] + acc[:back_len, blk:]
    each_neighbour(lambda dp, dt: block_copy(back, back_send, back_recv, dp, dt, back_span).start())
    planes_all(lambda size: all_copy(size, xp_send, xp_recv).wait_recv())
    for c in range(mems):
        for zz in range(zs + 2):
            for rr in range(rs + 2):
                if 0 < rr <= rs:
                    r = slice(rr - 1, rr)
                    row = primal_ref[c, zz - 1, r, :] if 0 < zz <= zs else pplane[min(zz, 1), c, r, :]
                else:
                    side = 0 if rr == 0 else 1
                    row = prow_in[side, c, zz - 1] if 0 < zz <= zs else pprow[min(zz, 1), side, c]
                xp[zz, rr, c : c + 1, :] = row
    known_part(
        pkern, pb_ref, xp[...].reshape((zs + 2) * (rs + 2) * 8, cols), known_p, zs, rs
    )
    each_count(lambda i, j: all_copy(back_all(i, j), back_send, back_recv).wait_recv())
    for zz in range(zs + 2):
        dp, z = source_of(zz, zs)
        for rr in range(rs + 2):
            dt, r = source_of(rr, rs)
            k = (dp + 1) * 3 + dt + 1
            at = zz * (rs + 2) + rr
            for b in range(col_blocks):
                row = (r * col_blocks + b) * zs + z
                back_rows[at : at + 1, b * blk : (b + 1) * blk] = back[k, row : row + 1, :]

    res = finish(
        back_rows, ap, known_p, ps_ref, p_mix, ph_ref, hp_high, hp_low, zs * rs, p_span
    )
    for c in range(mems):
        for z in range(zs):
            at = (c * zs + z) * rs
            out_primal[c, z] = res[at : at + rs] + primal_ref[c, z]

    dual_all(lambda size: all_copy(size, xd_send, xd_recv).wait_send())
    dual_near().wait_send()
    rows_all(lambda size: all_copy(size, row_send, row_recv).wait_send())
    planes_all(lambda size: all_copy(size, xp_send, xp_recv).wait_send())
    each_count(lambda i, j: all_copy(proj_all(i, j), proj_send, proj_recv).wait_send())
    each_count(lambda i, j: all_copy(back_all(i, j), back_send, back_recv).wait_send())
    all_copy(got, part_send, part_recv).wait_send()
    all_copy(got, nd_send, part_recv).wait_send()


def store(a_ref, b_ref, a_hbm, b_hbm, sem):
    copies = [
        pltpu.make_async_copy(x, y, sem.at[i])
        for i, (x, y) in enumerate(((a_ref, a_hbm), (b_ref, b_hbm)))
    ]
    for copy in copies:
        copy.start()
    for copy in copies:
        copy.wait()


def per_device(plane_count, tile_count, *args):
    (primal, dual, measured, weights, pix, bins_of, count, dk, db, ds, dm, dh, pk, pb, ps, pm, ph) = args
    mems, zs, rs, cols = primal.shape
    bins = dual.shape[3]
    angles, slots, blk = weights.shape[1:4]
    assert dual.shape[2] == 1 and angles == tile_count and 8 % zs == 0 and mems == NEW
    assert plane_count % 2 == 0
    hidden = db.shape[0]
    proj_len = bins // blk * zs
    back_len = rs * cols // blk * zs
    d_span = -(-(zs + 2) * 3 // 8) * 8
    p_span = -(-(zs + 2) * (rs + 2) // 8) * 8
    cells = zs * rs
    most = max(
        (2 * zs + 3) * (mems + 1) * bins,
        2 * mems * (rs + 2) * cols,
        2 * mems * zs * cols,
        8 * proj_len * blk,
        (2 * back_len + 6 * cols // blk * zs) * blk,
    )
    vmem = pl.BlockSpec(memory_space=pltpu.VMEM)
    dma = pltpu.SemaphoreType.DMA
    operands = (
        primal, dual, measured, weights, pix, bins_of, count,
        jnp.transpose(dk, (2, 3, 4, 1, 0)), db[None], ds[None], dm, dh[None],
        jnp.transpose(pk, (1, 2, 3, 4, 0)), pb[None], ps[None], pm, ph[None],
    )
    held = pl.pallas_call(
        functools.partial(body, plane_count, tile_count),
        out_shape=(
            pltpu.VMEM(primal.shape, F32),
            pltpu.VMEM(dual.shape, F32),
        ),
        in_specs=[pl.BlockSpec(memory_space=pl.ANY)] * len(operands),
        out_specs=(vmem, vmem),
        scratch_shapes=[
            (pltpu.SMEM if x.dtype == jnp.int32 else pltpu.VMEM)(x.shape, x.dtype)
            for x in operands
            if not any(x is y for y in (weights, dual, measured))
        ]
        + [
            pltpu.VMEM((3 * hidden, 72), F32),
            pltpu.VMEM((3 * hidden, 72), F32),
            pltpu.VMEM((3, 72, 128), F32),
            dma((len(operands) - 1,)),
            pltpu.VMEM((angles, slots, blk, blk), F32),
            pltpu.VMEM((angles, slots * blk, blk), BF16),
            pltpu.VMEM((angles, slots * blk, blk), BF16),
            pltpu.VMEM((rs * cols // blk, 16, blk), F32),
            pltpu.VMEM((bins // blk, 16, blk), F32),
            pltpu.VMEM((tile_count, proj_len, blk), F32),
            pltpu.VMEM((tile_count - 1, proj_len, blk), F32),
            pltpu.VMEM((-(-most // (8 * blk)), 8, blk), F32),
            pltpu.VMEM((tile_count, proj_len, blk), F32),
            pltpu.VMEM((3, mems + 1, zs, 1, bins), F32),
            pltpu.VMEM((2, 3, mems + 1, 1, bins), F32),
            pltpu.VMEM((2, mems, zs, 1, cols), F32),
            pltpu.VMEM((2, mems, zs, 1, cols), F32),
            pltpu.VMEM((2, mems, rs, cols), F32),
            pltpu.VMEM((2, 2, mems, 1, cols), F32),
            pltpu.VMEM((zs + 2, 3, 8, bins), F32),
            pltpu.VMEM((zs + 2, rs + 2, 8, cols), F32),
            pltpu.VMEM((9, proj_len, blk), F32),
            pltpu.VMEM((9, back_len, blk), F32),
            pltpu.VMEM((d_span, bins), F32),
            pltpu.VMEM((p_span, cols), F32),
            pltpu.VMEM((zs * hidden, -(-9 * d_span // 128) * 128), BF16),
            pltpu.VMEM((cells * hidden, -(-9 * p_span // 128) * 128), BF16),
            pltpu.VMEM((zs * hidden, bins), F32),
            pltpu.VMEM((cells * hidden, cols), F32),
            pltpu.VMEM((zs * hidden, bins), BF16),
            pltpu.VMEM((zs * hidden, bins), BF16),
            pltpu.VMEM((cells * hidden, cols), BF16),
            pltpu.VMEM((cells * hidden, cols), BF16),
            dma((angles,)),
            dma((1,)),
            dma((1,)),
            dma((1,)),
            dma((tile_count,)),
        ]
        + [dma((1,))] * 12,
        compiler_params=pltpu.CompilerParams(
            collective_id=0, has_side_effects=True, vmem_limit_bytes=60 * 2**20
        ),
    )(*operands)
    hbm = pl.BlockSpec(memory_space=pl.ANY)
    return pl.pallas_call(
        store,
        out_shape=[jax.ShapeDtypeStruct(x.shape, F32) for x in held],
        in_specs=[vmem] * 2,
        out_specs=[hbm] * 2,
        scratch_shapes=[dma((2,))],
    )(*[pltpu.with_memory_space_constraint(x, pltpu.VMEM) for x in held])


def solution(mesh):
    in_specs = (
        P(None, "plane", "tile", None),
        P(None, "plane", "tile", None),
        P("plane", "tile", None),
        P("tile", None, None, None, None),
        P("tile", None, None),
        P(),
        P("tile", None),
    ) + (P(),) * 10
    out_specs = (P(None, "plane", "tile", None), P(None, "plane", "tile", None))
    return jax.shard_map(
        functools.partial(per_device, mesh.shape["plane"], mesh.shape["tile"]),
        mesh=mesh,
        in_specs=in_specs,
        out_specs=out_specs,
        check_vma=False,
    )
```

```python
import functools

import jax
import jax.numpy as jnp
from jax import lax
from jax.experimental import pallas as pl
from jax.experimental.pallas import tpu as pltpu
from jax.sharding import PartitionSpec as P

F32 = jnp.float32
BF16 = jnp.bfloat16
MESH = pl.DeviceIdType.MESH
NEIGHBOURS = [(dp, dt) for dp in (-1, 0, 1) for dt in (-1, 0, 1)]
CENTRE = 4
NEW = 5


def split(x):
    high = x.astype(BF16)
    return high, (x - high.astype(F32)).astype(BF16)


def dot(a, b):
    return jnp.dot(a, b, preferred_element_type=F32)


def iota(shape, dim):
    return lax.broadcasted_iota(jnp.int32, shape, dim)


def shifted_sum(y, hidden):
    width = y.shape[1]
    lane = iota((hidden, width), 1)
    left = jnp.where(lane == 0, 0.0, pltpu.roll(y[:hidden], 1, 1))
    right = jnp.where(lane == width - 1, 0.0, pltpu.roll(y[2 * hidden :], width - 1, 1))
    return left + y[hidden : 2 * hidden] + right


def column(row, rows, repeat):
    shape = (rows, row.shape[1])
    low = iota(shape, 1) * repeat
    at = iota(shape, 0)
    hit = (at >= low) & (at < low + repeat)
    return jnp.sum(jnp.where(hit, row, 0.0), axis=1, keepdims=True)


def row_code(rows, lanes, step_rows):
    at = iota((rows, lanes), 0)
    tap = lax.shift_right_logical(at, 3)
    kz = (tap >= 3).astype(jnp.int32) + (tap >= 6).astype(jnp.int32)
    return kz * step_rows + (tap - 3 * kz), at & 7


def expand_new(kern_ref, out_ref, zs, rs, span):
    kern = kern_ref[...]
    taps = kern.shape[0]
    hidden = taps // 3
    high, low = split(kern)
    lanes = out_ref.shape[1]
    code, chan = row_code(kern.shape[1], lanes, rs + 2)
    lane = iota((kern.shape[1], lanes), 1)
    keep = lax.rem(iota((hidden, lanes), 1), 3 * span) < 2 * span
    for i in range(zs * rs):
        spread = 0.0
        for kx in range(3):
            place = code + ((i // rs) * (rs + 2) + i % rs + 3 * kx * span)
            hit = (lane == place) | (lane == place + span) | (lane == place + 2 * span)
            own = slice(kx * hidden, (kx + 1) * hidden)
            spread += dot(
                jnp.concatenate([high[own], low[own]], 0),
                jnp.where(hit & (chan == NEW), 1.0, 0.0).astype(BF16),
            )
        out_ref[i * hidden : (i + 1) * hidden, :] = jnp.where(
            keep, spread[:hidden], spread[hidden:]
        ).astype(BF16)


def known_part(kern_ref, bias_ref, cells, known_ref, zs, rs):
    hidden = bias_ref.shape[1]
    kern = kern_ref[...]
    taps = kern.shape[0]
    depth = cells.shape[0]
    lanes = -(-depth // 128) * 128
    both = jnp.concatenate(split(kern), 0)
    code, chan = row_code(kern.shape[1], lanes, rs + 2)
    base = code * 8 + chan
    lane = iota((kern.shape[1], lanes), 1)
    high, low = split(cells)
    bias = column(bias_ref[...], hidden, 1)
    for i in range(zs * rs):
        place = base + ((i // rs) * (rs + 2) + i % rs) * 8
        a = dot(both, jnp.where(lane == place, 1.0, 0.0).astype(BF16))[:, :depth].astype(BF16)
        y = dot(a, high)
        y = y[:taps] + y[taps:] + dot(a[:taps], low)
        known_ref[i * hidden : (i + 1) * hidden, :] = shifted_sum(y, hidden) + bias


def mixing_matrix(mix_ref, rows, cells):
    outs, hidden = mix_ref.shape
    lanes = cells * hidden
    mix = jnp.concatenate([mix_ref[...], jnp.zeros((8 - outs, hidden), F32)], 0)
    both = jnp.concatenate(split(mix), 0)
    at = iota((hidden, lanes), 1)
    rep = jnp.where(lax.rem(at, hidden) == iota((hidden, lanes), 0), 1.0, 0.0).astype(BF16)
    wide = dot(both, rep)
    low_row = iota((rows, 8), 1) * cells
    at_row = iota((rows, 8), 0)
    pick = jnp.where((at_row >= low_row) & (at_row < low_row + cells), 1.0, 0.0).astype(BF16)
    cell_of_lane = lax.div(iota((rows, lanes), 1), hidden)
    own = lax.rem(iota((rows, lanes), 0), cells) == cell_of_lane
    high = jnp.where(own, dot(pick, wide[:8].astype(BF16)), 0.0).astype(BF16)
    low = jnp.where(own, dot(pick, wide[8:].astype(BF16)), 0.0).astype(BF16)
    return jnp.concatenate([high, low], 0)


def finish(new_ref, a_ref, known_ref, slope_ref, mix, shift_ref, hid_high, hid_low, cells, span):
    hidden = slope_ref.shape[1]
    high, low = split(new_ref[...])
    high, low = high.astype(F32), low.astype(F32)
    stack = jnp.concatenate([high, low, high], 0)
    width = stack.shape[1]
    lane = iota(stack.shape, 1)
    left = jnp.where(lane == 0, 0.0, pltpu.roll(stack, 1, 1))
    right = jnp.where(lane == width - 1, 0.0, pltpu.roll(stack, width - 1, 1))
    stack = jnp.concatenate([left, stack, right], 0).astype(BF16)
    y = dot(a_ref[:, : 9 * span], stack)
    slope = column(slope_ref[...], hidden, 1)
    for i in range(cells):
        h = known_ref[i * hidden : (i + 1) * hidden, :] + y[i * hidden : (i + 1) * hidden]
        h = jnp.where(h > 0, h, slope * h)
        hh, hl = split(h)
        hid_high[i * hidden : (i + 1) * hidden, :] = hh
        hid_low[i * hidden : (i + 1) * hidden, :] = hl
    rows = mix.shape[0] // 2
    first = dot(mix, hid_high[...])
    out = first[:rows] + first[rows:] + dot(mix[:rows], hid_low[...])
    return out + column(shift_ref[...], rows, cells)


def body(
    plane_count,
    tile_count,
    primal_hbm,
    dual_hbm,
    measured_hbm,
    w_hbm,
    pix_hbm,
    bin_hbm,
    cnt_hbm,
    dk_hbm,
    db_hbm,
    ds_hbm,
    dm_hbm,
    dh_hbm,
    pk_hbm,
    pb_hbm,
    ps_hbm,
    pm_hbm,
    ph_hbm,
    out_primal,
    out_dual,
    primal_ref,
    pix_ref,
    bin_ref,
    cnt_ref,
    dk_ref,
    db_ref,
    ds_ref,
    dm_ref,
    dh_ref,
    pk_ref,
    pb_ref,
    ps_ref,
    pm_ref,
    ph_ref,
    dkern,
    pkern,
    moved,
    in_sem,
    wbuf,
    wback,
    src_pat,
    nd_pat,
    part,
    got,
    size_ref,
    nd,
    xraw,
    xside,
    prow_out,
    prow_in,
    pplane,
    pprow,
    xd,
    xp,
    proj,
    back,
    proj_rows,
    back_rows,
    ad,
    ap,
    known_d,
    known_p,
    hd_high,
    hd_low,
    hp_high,
    hp_low,
    w_sem,
    part_send,
    part_recv,
    nd_send,
    nd_recv,
    xd_send,
    xd_recv,
    near_send,
    near_recv,
    row_send,
    row_recv,
    xp_send,
    xp_recv,
    proj_send,
    proj_recv,
    back_send,
    back_recv,
):
    mems, zs, rs, cols = primal_hbm.shape
    bins = dual_hbm.shape[3]
    angles, slots, blk = w_hbm.shape[1], w_hbm.shape[2], w_hbm.shape[3]
    pix_blocks = rs * cols // blk
    bin_blocks = bins // blk
    col_blocks = cols // blk
    p = lax.axis_index("plane")
    t = lax.axis_index("tile")

    def angle_at(n):
        return lax.rem(t + n, tile_count)

    def near(n):
        inner = jnp.minimum(t, tile_count - 1 - t)
        away = lax.div(n + 1, 2)
        either = jnp.where(lax.rem(n, 2) == 1, t + away, t - away)
        beyond = jnp.where(t < tile_count - 1 - t, t + n - inner, t - n + inner)
        return jnp.where(n <= 2 * inner, either, beyond)

    def far(n):
        return near(tile_count - 1 - n)

    def w_copy(a):
        return pltpu.make_async_copy(w_hbm.at[0, a], wbuf.at[a], w_sem.at[a])

    inputs = (
        (primal_hbm, primal_ref),
        (pix_hbm, pix_ref),
        (bin_hbm, bin_ref),
        (cnt_hbm, cnt_ref),
        (dual_hbm, xraw.at[1, pl.ds(0, mems)]),
        (measured_hbm, xraw.at[1, mems]),
        (dk_hbm, dk_ref),
        (db_hbm, db_ref),
        (ds_hbm, ds_ref),
        (dm_hbm, dm_ref),
        (dh_hbm, dh_ref),
        (pk_hbm, pk_ref),
        (pb_hbm, pb_ref),
        (ps_hbm, ps_ref),
        (pm_hbm, pm_ref),
        (ph_hbm, ph_ref),
    )
    loads = [pltpu.make_async_copy(a, b, in_sem.at[i]) for i, (a, b) in enumerate(inputs)]
    for load in loads[:4]:
        load.start()
    w_copy(far(0)).start()
    def exists(dp, dt):
        there = None
        for step, at, count in ((dp, p, plane_count), (dt, t, tile_count)):
            if step:
                ok = at > 0 if step < 0 else at < count - 1
                there = ok if there is None else there & ok
        return there

    barrier = pltpu.get_barrier_semaphore()

    @pl.loop(1, tile_count)
    def _(n):
        pl.semaphore_signal(barrier, inc=1, device_id=(p, near(tile_count - n)), device_id_type=MESH)

    for dp, dt in NEIGHBOURS:
        if dp:

            @pl.when(exists(dp, dt))
            def _():
                pl.semaphore_signal(
                    barrier, inc=1, device_id=(p + dp, t + dt), device_id_type=MESH
                )

    for load in loads[4:6]:
        load.start()

    @pl.loop(1, angles)
    def _(n):
        w_copy(far(n)).start()

    for load in loads[6:]:
        load.start()

    for ref in (xd, xp):
        ref[...] = jnp.zeros_like(ref)

    def clear(ref):
        ref[...] = jnp.zeros_like(ref)

    planes_near = (p > 0).astype(jnp.int32) + (p < plane_count - 1).astype(jnp.int32)
    tiles_near = 1 + (t > 0).astype(jnp.int32) + (t < tile_count - 1).astype(jnp.int32)
    odd = lax.rem(p, 2) == 1
    far_step = jnp.where(odd, 1, -1)
    far_edge = jnp.where(odd, zs - 1, 0)
    near_edge = jnp.where(odd, 0, zs - 1)
    far_there = (p + far_step >= 0) & (p + far_step < plane_count)

    def missing(there, *refs):
        @pl.when(jnp.logical_not(there))
        def _():
            for ref in refs:
                clear(ref)

    for dt in (-1, 1):
        missing(exists(0, dt), xraw.at[1 + dt], prow_in.at[(dt + 1) // 2])
        missing(far_there & exists(0, dt), xside.at[1, 1 + dt])
    missing(far_there, xside.at[1, 1])
    for dp in (-1, 1):
        missing(exists(dp, 0), pplane.at[(dp + 1) // 2], pprow.at[(dp + 1) // 2])
    for dp, dt in [x for x in NEIGHBOURS if x != (0, 0)]:
        k = (dp + 1) * 3 + dt + 1
        missing(exists(dp, dt), proj.at[k], back.at[k])

    for load in loads[:6]:
        load.wait()
    for z in range(zs):
        for c in range(mems):
            prow_out[0, c, z] = primal_ref[c, z, 0:1, :]
            prow_out[1, c, z] = primal_ref[c, z, rs - 1 : rs, :]

    def remote(src, dst, send, recv, device):
        return pltpu.make_async_remote_copy(
            src_ref=src,
            dst_ref=dst,
            send_sem=send.at[0],
            recv_sem=recv.at[0],
            device_id=device,
            device_id_type=MESH,
        )

    def dual_tile(dt):
        return remote(xraw.at[1], xraw.at[1 - dt], xd_send, xd_recv, (p, t + dt))

    def dual_far(dt):
        return remote(
            xraw.at[1, :, far_edge], xside.at[1, 1 - dt], xd_send, xd_recv, (p + far_step, t + dt)
        )

    def dual_near():
        return remote(
            xraw.at[:, :, near_edge], xside.at[0], near_send, near_recv, (p - far_step, t)
        )

    def row_tile(dt):
        side = (dt + 1) // 2
        return remote(prow_out.at[side], prow_in.at[1 - side], row_send, row_recv, (p, t + dt))

    def plane_copies(dp):
        z, side = (0, 1) if dp < 0 else (zs - 1, 0)
        to = (p + dp, t)
        return (
            remote(primal_ref.at[:, z], pplane.at[side], xp_send, xp_recv, to),
            remote(prow_in.at[:, :, z], pprow.at[side], xp_send, xp_recv, to),
        )

    def send_known():
        for dt in (-1, 1):
            pl.when(exists(0, dt))(lambda dt=dt: dual_tile(dt).start())
        pl.when(far_there)(lambda: dual_far(0).start())
        for dt in (-1, 1):
            pl.when(far_there & exists(0, dt))(lambda dt=dt: dual_far(dt).start())
        for dt in (-1, 1):
            pl.when(exists(0, dt))(lambda dt=dt: row_tile(dt).start())

    def send_planes():
        for dp in (-1, 1):

            @pl.when(exists(dp, 0))
            def _():
                for copy in plane_copies(dp):
                    copy.start()

    def block_copy(ref, send, recv, dp, dt, span):
        k = (dp + 1) * 3 + dt + 1
        return pltpu.make_async_remote_copy(
            src_ref=ref.at[CENTRE, span(dt, True)],
            dst_ref=ref.at[8 - k, span(dt, True)],
            send_sem=send.at[0],
            recv_sem=recv.at[0],
            device_id=(p + dp, t + dt),
            device_id_type=MESH,
        )

    def all_copy(size, send, recv):
        return pltpu.make_async_remote_copy(
            src_ref=size,
            dst_ref=size,
            send_sem=send.at[0],
            recv_sem=recv.at[0],
            device_id=(p, angle_at(1)),
            device_id_type=MESH,
        )

    def each_count(act):
        for i in range(min(plane_count, 3)):
            for j in range(min(tile_count, 3)):
                if (i or plane_count == 1) and (j or tile_count == 1):
                    pl.when((planes_near == i) & (tiles_near == j + 1))(
                        functools.partial(act, i, j)
                    )

    def tiles(n):
        return size_ref.at[pl.ds(0, n // (8 * blk))]

    def dual_all(act):
        for far in range(2):
            for j in range(1, min(tile_count, 3)):
                count = j * zs + far * (1 + j)
                pl.when((far_there == (far == 1)) & (tiles_near == j + 1))(
                    functools.partial(act, tiles(count * (mems + 1) * bins))
                )

    def rows_all(act):
        for j in range(1, min(tile_count, 3)):
            pl.when(tiles_near == j + 1)(functools.partial(act, tiles(j * mems * zs * cols)))

    def planes_all(act):
        for i in range(1, min(plane_count, 3)):
            pl.when(planes_near == i)(functools.partial(act, tiles(i * mems * (rs + 2) * cols)))

    def blocks_of(along, side, i, j):
        return size_ref.at[pl.ds(0, (i * along + (i + 1) * j * side) // 8)]

    proj_len = bin_blocks * zs
    back_len = pix_blocks * zs
    edge_len = col_blocks * zs

    def proj_span(dt, sending):
        return pl.ds(0, proj_len)

    def back_span(dt, sending):
        if dt == 0:
            return pl.ds(0, back_len)
        first = (dt < 0) == sending
        return pl.ds(0 if first else back_len - edge_len, edge_len)

    def each_neighbour(act):
        for dp, dt in NEIGHBOURS:
            if (dp, dt) != (0, 0):
                pl.when(exists(dp, dt))(functools.partial(act, dp, dt))


    row8 = iota((8, blk), 0)
    group = 8 // zs
    of_row = lax.div(row8, zs)
    z_row = lax.rem(row8, zs)

    def pattern(rows):
        out = jnp.broadcast_to(rows[0], (8, blk))
        for z in range(1, zs):
            out = jnp.where(z_row == z, jnp.broadcast_to(rows[z], (8, blk)), out)
        high, low = split(out)
        return jnp.concatenate([high.astype(F32), low.astype(F32)], 0)

    for q in range(pix_blocks):
        r, b = q // col_blocks, q % col_blocks
        src_pat[q] = pattern(
            [primal_ref[1, z, r : r + 1, b * blk : (b + 1) * blk] for z in range(zs)]
        )

    def masked(pat, target, total):
        pieces = []
        for half in (pat[:8], pat[8:]):
            for g in range(total // 8):
                pieces.append(jnp.where(of_row + g * group == target, half, 0.0))
        return jnp.concatenate(pieces, 0).astype(BF16)

    def part_copy(a):
        return pltpu.make_async_remote_copy(
            src_ref=part.at[a],
            dst_ref=got.at[lax.rem(t - a - 1 + 2 * tile_count, tile_count)],
            send_sem=part_send.at[0],
            recv_sem=part_recv.at[0],
            device_id=(p, a),
            device_id_type=MESH,
        )

    def forward(n, carry):
        a = far(n)
        w_copy(a).wait()
        high, low = split(wbuf[a].reshape(slots * blk, blk))
        for s in range(slots):
            rows = slice(s * blk, (s + 1) * blk)
            wback[a, :blk, rows] = high[rows]
            wback[a, blk:, rows] = low[rows]
        left = []
        for s in range(slots):
            target = jnp.where(s < cnt_ref[0, a], bin_ref[t, a, s], -1)
            left.append(masked(src_pat[pix_ref[0, a, s]], target, proj_len))
        o = dot(jnp.concatenate(left, 1), jnp.concatenate([high, low], 1))
        part[a] = o[:proj_len, :blk] + o[proj_len:, :blk] + o[:proj_len, blk:]

        @pl.when(n == ahead)
        def _():
            pl.semaphore_wait(barrier, tile_count - 1 + planes_near * tiles_near)
            for m in range(ahead):
                part_copy(far(m)).start()

        @pl.when((n >= ahead) & (n < tile_count - 1))
        def _():
            part_copy(a).start()

        return carry

    ahead = angles - 2
    lax.fori_loop(0, angles, forward, 0)

    send_known()

    for load in loads[6:]:
        load.wait()
    hidden = db_ref.shape[1]
    moved[...] = jnp.zeros_like(moved)

    def flatten(kern):
        for kx in range(3):
            kern[kx * hidden : (kx + 1) * hidden, :] = moved[kx].T[:hidden, :]

    for kz in range(3):
        for ky in range(3):
            for kx in range(3):
                at = (kz * 3 + ky) * 8
                moved[kx, at : at + mems + 2, :hidden] = dk_ref[kz, ky, kx]
    flatten(dkern)
    d_span = -(-(zs + 2) * 3 // 8) * 8
    p_span = -(-(zs + 2) * (rs + 2) // 8) * 8
    proj_rows[...] = jnp.zeros_like(proj_rows)
    back_rows[...] = jnp.zeros_like(back_rows)
    expand_new(dkern, ad, zs, 1, d_span)
    d_rows = -(-mems * zs // 8) * 8
    p_rows = -(-mems * zs * rs // 8) * 8
    d_mix = mixing_matrix(dm_ref, d_rows, zs)
    total = part[t]
    all_copy(got, part_send, part_recv).wait_recv()
    for n in range(tile_count - 1):
        total = total + got[n]
    proj[CENTRE] = total
    each_neighbour(lambda dp, dt: block_copy(proj, proj_send, proj_recv, dp, dt, proj_span).start())
    dual_all(lambda size: all_copy(size, xd_send, xd_recv).wait_recv())
    dual_near().start()
    for z in range(zs):
        for aa in range(3):
            for c in range(mems + 1):
                at = c if c < mems else NEW + 1
                xd[1 + z, aa, at : at + 1, :] = xraw[aa, c, z]
    low_side = jnp.where(odd, 0, 1)
    dual_near().wait_recv()
    for zz, side in ((0, low_side), (zs + 1, 1 - low_side)):
        for aa in range(3):
            for c in range(mems + 1):
                at = c if c < mems else NEW + 1
                xd[zz, aa, at : at + 1, :] = xside[side, aa, c]
    known_part(dkern, db_ref, xd[...].reshape((zs + 2) * 3 * 8, bins), known_d, zs, 1)
    proj_all = functools.partial(blocks_of, proj_len, proj_len)
    back_all = functools.partial(blocks_of, back_len, edge_len)
    each_count(lambda i, j: all_copy(proj_all(i, j), proj_send, proj_recv).wait_recv())

    def source_of(at, count):
        if at == 0:
            return -1, count - 1
        if at == count + 1:
            return 1, 0
        return 0, at - 1

    for zz in range(zs + 2):
        dp, z = source_of(zz, zs)
        for aa in range(3):
            dt, _ = source_of(aa, 1)
            k = (dp + 1) * 3 + dt + 1
            at = zz * 3 + aa
            for b in range(bin_blocks):
                row = b * zs + z
                proj_rows[at : at + 1, b * blk : (b + 1) * blk] = proj[k, row : row + 1, :]

    res = finish(
        proj_rows, ad, known_d, ds_ref, d_mix, dh_ref, hd_high, hd_low, zs, d_span
    )
    lead = [res[z : z + 1] + xraw[1, 0, z] for z in range(zs)]
    for b in range(bin_blocks):
        for z in range(zs):
            row = b * zs + z
            nd[t, row : row + 1, :] = lead[z][:, b * blk : (b + 1) * blk]

    def nd_copy(a):
        return pltpu.make_async_remote_copy(
            src_ref=nd.at[t],
            dst_ref=nd.at[t],
            send_sem=nd_send.at[0],
            recv_sem=nd_recv.at[t],
            device_id=(p, a),
            device_id_type=MESH,
        )

    def nd_arrival(a):
        return pltpu.make_async_remote_copy(
            src_ref=nd.at[a],
            dst_ref=nd.at[a],
            send_sem=nd_send.at[0],
            recv_sem=nd_recv.at[a],
            device_id=(p, a),
            device_id_type=MESH,
        )

    @pl.loop(1, tile_count)
    def _(n):
        nd_copy(near(tile_count - n)).start()

    for c in range(mems):
        for z in range(zs):
            at = c * zs + z
            out_dual[c, z] = res[at : at + 1] + xraw[1, c, z]

    rows_all(lambda size: all_copy(size, row_send, row_recv).wait_recv())
    send_planes()
    for c in range(mems + 1):
        for kz in range(3):
            for ky in range(3):
                at = (kz * 3 + ky) * 8 + c
                taps = pk_ref[c, kz, ky]
                for kx in range(3):
                    moved[kx, at : at + 1, :hidden] = taps[kx : kx + 1]
    flatten(pkern)
    expand_new(pkern, ap, zs, rs, p_span)
    p_mix = mixing_matrix(pm_ref, p_rows, zs * rs)


    together = 2

    def backward(m, acc):
        picks = [near(m * together + i) for i in range(together)]
        for i, a in enumerate(picks):

            @pl.when(m * together + i > 0)
            def _():
                nd_arrival(a).wait_recv()

        for i, a in enumerate(picks):
            for b in range(bin_blocks):
                nd_pat[i, b] = pattern([nd[a, b * zs + z : b * zs + z + 1, :] for z in range(zs)])
        for i, a in enumerate(picks):
            left = []
            for s in range(slots):
                target = jnp.where(s < cnt_ref[0, a], pix_ref[0, a, s], -1)
                left.append(masked(nd_pat[i, bin_ref[t, a, s]], target, back_len))
            acc = acc + lax.dot_general(
                jnp.concatenate(left, 1),
                wback[a],
                (((1,), (1,)), ((), ())),
                preferred_element_type=F32,
            )
        return acc

    acc = lax.fori_loop(0, tile_count // together, backward, jnp.zeros((2 * back_len, 2 * blk), F32))
    back[CENTRE] = acc[:back_len, :blk] + acc[back_len:, :blk] + acc[:back_len, blk:]
    each_neighbour(lambda dp, dt: block_copy(back, back_send, back_recv, dp, dt, back_span).start())
    planes_all(lambda size: all_copy(size, xp_send, xp_recv).wait_recv())
    for c in range(mems):
        for zz in range(zs + 2):
            for rr in range(rs + 2):
                if 0 < rr <= rs:
                    r = slice(rr - 1, rr)
                    row = primal_ref[c, zz - 1, r, :] if 0 < zz <= zs else pplane[min(zz, 1), c, r, :]
                else:
                    side = 0 if rr == 0 else 1
                    row = prow_in[side, c, zz - 1] if 0 < zz <= zs else pprow[min(zz, 1), side, c]
                xp[zz, rr, c : c + 1, :] = row
    known_part(
        pkern, pb_ref, xp[...].reshape((zs + 2) * (rs + 2) * 8, cols), known_p, zs, rs
    )
    each_count(lambda i, j: all_copy(back_all(i, j), back_send, back_recv).wait_recv())
    for zz in range(zs + 2):
        dp, z = source_of(zz, zs)
        for rr in range(rs + 2):
            dt, r = source_of(rr, rs)
            k = (dp + 1) * 3 + dt + 1
            at = zz * (rs + 2) + rr
            for b in range(col_blocks):
                row = (r * col_blocks + b) * zs + z
                back_rows[at : at + 1, b * blk : (b + 1) * blk] = back[k, row : row + 1, :]

    res = finish(
        back_rows, ap, known_p, ps_ref, p_mix, ph_ref, hp_high, hp_low, zs * rs, p_span
    )
    for c in range(mems):
        for z in range(zs):
            at = (c * zs + z) * rs
            out_primal[c, z] = res[at : at + rs] + primal_ref[c, z]

    dual_all(lambda size: all_copy(size, xd_send, xd_recv).wait_send())
    dual_near().wait_send()
    rows_all(lambda size: all_copy(size, row_send, row_recv).wait_send())
    planes_all(lambda size: all_copy(size, xp_send, xp_recv).wait_send())
    each_count(lambda i, j: all_copy(proj_all(i, j), proj_send, proj_recv).wait_send())
    each_count(lambda i, j: all_copy(back_all(i, j), back_send, back_recv).wait_send())
    all_copy(got, part_send, part_recv).wait_send()
    all_copy(got, nd_send, part_recv).wait_send()


def store(a_ref, b_ref, a_hbm, b_hbm, sem):
    copies = [
        pltpu.make_async_copy(x, y, sem.at[i])
        for i, (x, y) in enumerate(((a_ref, a_hbm), (b_ref, b_hbm)))
    ]
    for copy in copies:
        copy.start()
    for copy in copies:
        copy.wait()


def per_device(plane_count, tile_count, *args):
    (primal, dual, measured, weights, pix, bins_of, count, dk, db, ds, dm, dh, pk, pb, ps, pm, ph) = args
    mems, zs, rs, cols = primal.shape
    bins = dual.shape[3]
    angles, slots, blk = weights.shape[1:4]
    assert dual.shape[2] == 1 and angles == tile_count and 8 % zs == 0 and mems == NEW
    assert plane_count % 2 == 0
    hidden = db.shape[0]
    proj_len = bins // blk * zs
    back_len = rs * cols // blk * zs
    d_span = -(-(zs + 2) * 3 // 8) * 8
    p_span = -(-(zs + 2) * (rs + 2) // 8) * 8
    cells = zs * rs
    most = max(
        (2 * zs + 3) * (mems + 1) * bins,
        2 * mems * (rs + 2) * cols,
        2 * mems * zs * cols,
        8 * proj_len * blk,
        (2 * back_len + 6 * cols // blk * zs) * blk,
    )
    vmem = pl.BlockSpec(memory_space=pltpu.VMEM)
    dma = pltpu.SemaphoreType.DMA
    operands = (
        primal, dual, measured, weights, pix, bins_of, count,
        jnp.transpose(dk, (2, 3, 4, 1, 0)), db[None], ds[None], dm, dh[None],
        jnp.transpose(pk, (1, 2, 3, 4, 0)), pb[None], ps[None], pm, ph[None],
    )
    held = pl.pallas_call(
        functools.partial(body, plane_count, tile_count),
        out_shape=(
            pltpu.VMEM(primal.shape, F32),
            pltpu.VMEM(dual.shape, F32),
        ),
        in_specs=[pl.BlockSpec(memory_space=pl.ANY)] * len(operands),
        out_specs=(vmem, vmem),
        scratch_shapes=[
            (pltpu.SMEM if x.dtype == jnp.int32 else pltpu.VMEM)(x.shape, x.dtype)
            for x in operands
            if not any(x is y for y in (weights, dual, measured))
        ]
        + [
            pltpu.VMEM((3 * hidden, 72), F32),
            pltpu.VMEM((3 * hidden, 72), F32),
            pltpu.VMEM((3, 72, 128), F32),
            dma((len(operands) - 1,)),
            pltpu.VMEM((angles, slots, blk, blk), F32),
            pltpu.VMEM((angles, 2 * blk, slots * blk), BF16),
            pltpu.VMEM((rs * cols // blk, 16, blk), F32),
            pltpu.VMEM((2, bins // blk, 16, blk), F32),
            pltpu.VMEM((tile_count, proj_len, blk), F32),
            pltpu.VMEM((tile_count - 1, proj_len, blk), F32),
            pltpu.VMEM((-(-most // (8 * blk)), 8, blk), F32),
            pltpu.VMEM((tile_count, proj_len, blk), F32),
            pltpu.VMEM((3, mems + 1, zs, 1, bins), F32),
            pltpu.VMEM((2, 3, mems + 1, 1, bins), F32),
            pltpu.VMEM((2, mems, zs, 1, cols), F32),
            pltpu.VMEM((2, mems, zs, 1, cols), F32),
            pltpu.VMEM((2, mems, rs, cols), F32),
            pltpu.VMEM((2, 2, mems, 1, cols), F32),
            pltpu.VMEM((zs + 2, 3, 8, bins), F32),
            pltpu.VMEM((zs + 2, rs + 2, 8, cols), F32),
            pltpu.VMEM((9, proj_len, blk), F32),
            pltpu.VMEM((9, back_len, blk), F32),
            pltpu.VMEM((d_span, bins), F32),
            pltpu.VMEM((p_span, cols), F32),
            pltpu.VMEM((zs * hidden, -(-9 * d_span // 128) * 128), BF16),
            pltpu.VMEM((cells * hidden, -(-9 * p_span // 128) * 128), BF16),
            pltpu.VMEM((zs * hidden, bins), F32),
            pltpu.VMEM((cells * hidden, cols), F32),
            pltpu.VMEM((zs * hidden, bins), BF16),
            pltpu.VMEM((zs * hidden, bins), BF16),
            pltpu.VMEM((cells * hidden, cols), BF16),
            pltpu.VMEM((cells * hidden, cols), BF16),
            dma((angles,)),
            dma((1,)),
            dma((1,)),
            dma((1,)),
            dma((tile_count,)),
        ]
        + [dma((1,))] * 12,
        compiler_params=pltpu.CompilerParams(
            collective_id=0, has_side_effects=True, vmem_limit_bytes=60 * 2**20
        ),
    )(*operands)
    hbm = pl.BlockSpec(memory_space=pl.ANY)
    return pl.pallas_call(
        store,
        out_shape=[jax.ShapeDtypeStruct(x.shape, F32) for x in held],
        in_specs=[vmem] * 2,
        out_specs=[hbm] * 2,
        scratch_shapes=[dma((2,))],
    )(*[pltpu.with_memory_space_constraint(x, pltpu.VMEM) for x in held])


def solution(mesh):
    in_specs = (
        P(None, "plane", "tile", None),
        P(None, "plane", "tile", None),
        P("plane", "tile", None),
        P("tile", None, None, None, None),
        P("tile", None, None),
        P(),
        P("tile", None),
    ) + (P(),) * 10
    out_specs = (P(None, "plane", "tile", None), P(None, "plane", "tile", None))
    return jax.shard_map(
        functools.partial(per_device, mesh.shape["plane"], mesh.shape["tile"]),
        mesh=mesh,
        in_specs=in_specs,
        out_specs=out_specs,
        check_vma=False,
    )
```

```python
import functools

import jax
import jax.numpy as jnp
from jax import lax
from jax.experimental import pallas as pl
from jax.experimental.pallas import tpu as pltpu
from jax.sharding import PartitionSpec as P

F32 = jnp.float32
BF16 = jnp.bfloat16
MESH = pl.DeviceIdType.MESH
NEIGHBOURS = [(dp, dt) for dp in (-1, 0, 1) for dt in (-1, 0, 1)]
CENTRE = 4
NEW = 5


def split(x):
    high = x.astype(BF16)
    return high, (x - high.astype(F32)).astype(BF16)


def dot(a, b):
    return jnp.dot(a, b, preferred_element_type=F32)


def iota(shape, dim):
    return lax.broadcasted_iota(jnp.int32, shape, dim)


def shifted_sum(y, hidden):
    width = y.shape[1]
    lane = iota((hidden, width), 1)
    left = jnp.where(lane == 0, 0.0, pltpu.roll(y[:hidden], 1, 1))
    right = jnp.where(lane == width - 1, 0.0, pltpu.roll(y[2 * hidden :], width - 1, 1))
    return left + y[hidden : 2 * hidden] + right


def column(row, rows, repeat):
    shape = (rows, row.shape[1])
    low = iota(shape, 1) * repeat
    at = iota(shape, 0)
    hit = (at >= low) & (at < low + repeat)
    return jnp.sum(jnp.where(hit, row, 0.0), axis=1, keepdims=True)


def row_code(rows, lanes, step_rows):
    at = iota((rows, lanes), 0)
    tap = lax.shift_right_logical(at, 3)
    kz = (tap >= 3).astype(jnp.int32) + (tap >= 6).astype(jnp.int32)
    return kz * step_rows + (tap - 3 * kz), at & 7


def expand_new(kern_ref, out_ref, zs, rs, span):
    kern = kern_ref[...]
    taps = kern.shape[0]
    hidden = taps // 3
    high, low = split(kern)
    lanes = out_ref.shape[1]
    code, chan = row_code(kern.shape[1], lanes, rs + 2)
    lane = iota((kern.shape[1], lanes), 1)
    keep = lax.rem(iota((hidden, lanes), 1), 3 * span) < 2 * span
    for i in range(zs * rs):
        spread = 0.0
        for kx in range(3):
            place = code + ((i // rs) * (rs + 2) + i % rs + 3 * kx * span)
            hit = (lane == place) | (lane == place + span) | (lane == place + 2 * span)
            own = slice(kx * hidden, (kx + 1) * hidden)
            spread += dot(
                jnp.concatenate([high[own], low[own]], 0),
                jnp.where(hit & (chan == NEW), 1.0, 0.0).astype(BF16),
            )
        out_ref[i * hidden : (i + 1) * hidden, :] = jnp.where(
            keep, spread[:hidden], spread[hidden:]
        ).astype(BF16)


def known_part(kern_ref, bias_ref, cells, known_ref, zs, rs):
    hidden = bias_ref.shape[1]
    kern = kern_ref[...]
    taps = kern.shape[0]
    depth = cells.shape[0]
    lanes = -(-depth // 128) * 128
    both = jnp.concatenate(split(kern), 0)
    code, chan = row_code(kern.shape[1], lanes, rs + 2)
    base = code * 8 + chan
    lane = iota((kern.shape[1], lanes), 1)
    high, low = split(cells)
    bias = column(bias_ref[...], hidden, 1)
    for i in range(zs * rs):
        place = base + ((i // rs) * (rs + 2) + i % rs) * 8
        a = dot(both, jnp.where(lane == place, 1.0, 0.0).astype(BF16))[:, :depth].astype(BF16)
        y = dot(a, high)
        y = y[:taps] + y[taps:] + dot(a[:taps], low)
        known_ref[i * hidden : (i + 1) * hidden, :] = shifted_sum(y, hidden) + bias


def mixing_matrix(mix_ref, rows, cells):
    outs, hidden = mix_ref.shape
    lanes = cells * hidden
    mix = jnp.concatenate([mix_ref[...], jnp.zeros((8 - outs, hidden), F32)], 0)
    both = jnp.concatenate(split(mix), 0)
    at = iota((hidden, lanes), 1)
    rep = jnp.where(lax.rem(at, hidden) == iota((hidden, lanes), 0), 1.0, 0.0).astype(BF16)
    wide = dot(both, rep)
    low_row = iota((rows, 8), 1) * cells
    at_row = iota((rows, 8), 0)
    pick = jnp.where((at_row >= low_row) & (at_row < low_row + cells), 1.0, 0.0).astype(BF16)
    cell_of_lane = lax.div(iota((rows, lanes), 1), hidden)
    own = lax.rem(iota((rows, lanes), 0), cells) == cell_of_lane
    high = jnp.where(own, dot(pick, wide[:8].astype(BF16)), 0.0).astype(BF16)
    low = jnp.where(own, dot(pick, wide[8:].astype(BF16)), 0.0).astype(BF16)
    return jnp.concatenate([high, low], 0)


def finish(new_ref, a_ref, known_ref, slope_ref, mix, shift_ref, hid_high, hid_low, cells, span):
    hidden = slope_ref.shape[1]
    new = new_ref[...]
    width = new.shape[1]
    lane = iota(new.shape, 1)
    left = jnp.where(lane == 0, 0.0, pltpu.roll(new, 1, 1))
    right = jnp.where(lane == width - 1, 0.0, pltpu.roll(new, width - 1, 1))
    pieces = []
    for piece in (left, new, right):
        high, low = split(piece)
        high, low = high.astype(F32), low.astype(F32)
        pieces += [high, low, high]
    stack = jnp.concatenate(pieces, 0).astype(BF16)
    y = dot(a_ref[:, : 9 * span], stack)
    slope = column(slope_ref[...], hidden, 1)
    for i in range(cells):
        h = known_ref[i * hidden : (i + 1) * hidden, :] + y[i * hidden : (i + 1) * hidden]
        h = jnp.where(h > 0, h, slope * h)
        hh, hl = split(h)
        hid_high[i * hidden : (i + 1) * hidden, :] = hh
        hid_low[i * hidden : (i + 1) * hidden, :] = hl
    rows = mix.shape[0] // 2
    first = dot(mix, hid_high[...])
    out = first[:rows] + first[rows:] + dot(mix[:rows], hid_low[...])
    return out + column(shift_ref[...], rows, cells)


def body(
    plane_count,
    tile_count,
    primal_hbm,
    dual_hbm,
    measured_hbm,
    w_hbm,
    pix_hbm,
    bin_hbm,
    cnt_hbm,
    dk_hbm,
    db_hbm,
    ds_hbm,
    dm_hbm,
    dh_hbm,
    pk_hbm,
    pb_hbm,
    ps_hbm,
    pm_hbm,
    ph_hbm,
    out_primal,
    out_dual,
    primal_ref,
    pix_ref,
    bin_ref,
    cnt_ref,
    dk_ref,
    db_ref,
    ds_ref,
    dm_ref,
    dh_ref,
    pk_ref,
    pb_ref,
    ps_ref,
    pm_ref,
    ph_ref,
    dkern,
    pkern,
    moved,
    in_sem,
    wbuf,
    wback,
    wturn,
    src_pat,
    nd_pat,
    part,
    got,
    size_ref,
    nd,
    xraw,
    xside,
    prow_out,
    prow_in,
    pplane,
    pprow,
    xd,
    xp,
    proj,
    back,
    proj_rows,
    back_rows,
    ad,
    ap,
    known_d,
    known_p,
    hd_high,
    hd_low,
    hp_high,
    hp_low,
    w_sem,
    part_send,
    part_recv,
    nd_send,
    nd_recv,
    xd_send,
    xd_recv,
    near_send,
    near_recv,
    row_send,
    row_recv,
    xp_send,
    xp_recv,
    proj_send,
    proj_recv,
    back_send,
    back_recv,
):
    mems, zs, rs, cols = primal_hbm.shape
    bins = dual_hbm.shape[3]
    angles, slots, blk = w_hbm.shape[1], w_hbm.shape[2], w_hbm.shape[3]
    pix_blocks = rs * cols // blk
    bin_blocks = bins // blk
    col_blocks = cols // blk
    p = lax.axis_index("plane")
    t = lax.axis_index("tile")

    def angle_at(n):
        return lax.rem(t + n, tile_count)

    def near(n):
        inner = jnp.minimum(t, tile_count - 1 - t)
        away = lax.div(n + 1, 2)
        either = jnp.where(lax.rem(n, 2) == 1, t + away, t - away)
        beyond = jnp.where(t < tile_count - 1 - t, t + n - inner, t - n + inner)
        return jnp.where(n <= 2 * inner, either, beyond)

    def far(n):
        return near(tile_count - 1 - n)

    def w_copy(a):
        return pltpu.make_async_copy(w_hbm.at[0, a], wbuf.at[a], w_sem.at[a])

    inputs = (
        (primal_hbm, primal_ref),
        (pix_hbm, pix_ref),
        (bin_hbm, bin_ref),
        (cnt_hbm, cnt_ref),
        (dual_hbm, xraw.at[1, pl.ds(0, mems)]),
        (measured_hbm, xraw.at[1, mems]),
        (dk_hbm, dk_ref),
        (db_hbm, db_ref),
        (ds_hbm, ds_ref),
        (dm_hbm, dm_ref),
        (dh_hbm, dh_ref),
        (pk_hbm, pk_ref),
        (pb_hbm, pb_ref),
        (ps_hbm, ps_ref),
        (pm_hbm, pm_ref),
        (ph_hbm, ph_ref),
    )
    loads = [pltpu.make_async_copy(a, b, in_sem.at[i]) for i, (a, b) in enumerate(inputs)]
    for load in loads[:4]:
        load.start()
    w_copy(far(0)).start()
    def exists(dp, dt):
        there = None
        for step, at, count in ((dp, p, plane_count), (dt, t, tile_count)):
            if step:
                ok = at > 0 if step < 0 else at < count - 1
                there = ok if there is None else there & ok
        return there

    barrier = pltpu.get_barrier_semaphore()

    @pl.loop(1, tile_count)
    def _(n):
        pl.semaphore_signal(barrier, inc=1, device_id=(p, near(tile_count - n)), device_id_type=MESH)

    for dp, dt in NEIGHBOURS:
        if dp:

            @pl.when(exists(dp, dt))
            def _():
                pl.semaphore_signal(
                    barrier, inc=1, device_id=(p + dp, t + dt), device_id_type=MESH
                )

    for load in loads[4:6]:
        load.start()

    @pl.loop(1, angles)
    def _(n):
        w_copy(far(n)).start()

    for load in loads[6:]:
        load.start()

    for ref in (xd, xp):
        ref[...] = jnp.zeros_like(ref)

    def clear(ref):
        ref[...] = jnp.zeros_like(ref)

    planes_near = (p > 0).astype(jnp.int32) + (p < plane_count - 1).astype(jnp.int32)
    tiles_near = 1 + (t > 0).astype(jnp.int32) + (t < tile_count - 1).astype(jnp.int32)
    odd = lax.rem(p, 2) == 1
    far_step = jnp.where(odd, 1, -1)
    far_edge = jnp.where(odd, zs - 1, 0)
    near_edge = jnp.where(odd, 0, zs - 1)
    far_there = (p + far_step >= 0) & (p + far_step < plane_count)

    def missing(there, *refs):
        @pl.when(jnp.logical_not(there))
        def _():
            for ref in refs:
                clear(ref)

    for dt in (-1, 1):
        missing(exists(0, dt), xraw.at[1 + dt], prow_in.at[(dt + 1) // 2])
        missing(far_there & exists(0, dt), xside.at[1, 1 + dt])
    missing(far_there, xside.at[1, 1])
    for dp in (-1, 1):
        missing(exists(dp, 0), pplane.at[(dp + 1) // 2], pprow.at[(dp + 1) // 2])
    for dp, dt in [x for x in NEIGHBOURS if x != (0, 0)]:
        k = (dp + 1) * 3 + dt + 1
        missing(exists(dp, dt), proj.at[k], back.at[k])

    for load in loads[:6]:
        load.wait()
    for z in range(zs):
        for c in range(mems):
            prow_out[0, c, z] = primal_ref[c, z, 0:1, :]
            prow_out[1, c, z] = primal_ref[c, z, rs - 1 : rs, :]

    def remote(src, dst, send, recv, device):
        return pltpu.make_async_remote_copy(
            src_ref=src,
            dst_ref=dst,
            send_sem=send.at[0],
            recv_sem=recv.at[0],
            device_id=device,
            device_id_type=MESH,
        )

    def dual_tile(dt):
        return remote(xraw.at[1], xraw.at[1 - dt], xd_send, xd_recv, (p, t + dt))

    def dual_far(dt):
        return remote(
            xraw.at[1, :, far_edge], xside.at[1, 1 - dt], xd_send, xd_recv, (p + far_step, t + dt)
        )

    def dual_near():
        return remote(
            xraw.at[:, :, near_edge], xside.at[0], near_send, near_recv, (p - far_step, t)
        )

    def row_tile(dt):
        side = (dt + 1) // 2
        return remote(prow_out.at[side], prow_in.at[1 - side], row_send, row_recv, (p, t + dt))

    def plane_copies(dp):
        z, side = (0, 1) if dp < 0 else (zs - 1, 0)
        to = (p + dp, t)
        return (
            remote(primal_ref.at[:, z], pplane.at[side], xp_send, xp_recv, to),
            remote(prow_in.at[:, :, z], pprow.at[side], xp_send, xp_recv, to),
        )

    def send_known():
        for dt in (-1, 1):
            pl.when(exists(0, dt))(lambda dt=dt: dual_tile(dt).start())
        pl.when(far_there)(lambda: dual_far(0).start())
        for dt in (-1, 1):
            pl.when(far_there & exists(0, dt))(lambda dt=dt: dual_far(dt).start())
        for dt in (-1, 1):
            pl.when(exists(0, dt))(lambda dt=dt: row_tile(dt).start())

    def send_planes():
        for dp in (-1, 1):

            @pl.when(exists(dp, 0))
            def _():
                for copy in plane_copies(dp):
                    copy.start()

    def block_copy(ref, send, recv, dp, dt, span):
        k = (dp + 1) * 3 + dt + 1
        return pltpu.make_async_remote_copy(
            src_ref=ref.at[CENTRE, span(dt, True)],
            dst_ref=ref.at[8 - k, span(dt, True)],
            send_sem=send.at[0],
            recv_sem=recv.at[0],
            device_id=(p + dp, t + dt),
            device_id_type=MESH,
        )

    def all_copy(size, send, recv):
        return pltpu.make_async_remote_copy(
            src_ref=size,
            dst_ref=size,
            send_sem=send.at[0],
            recv_sem=recv.at[0],
            device_id=(p, angle_at(1)),
            device_id_type=MESH,
        )

    def each_count(act):
        for i in range(min(plane_count, 3)):
            for j in range(min(tile_count, 3)):
                if (i or plane_count == 1) and (j or tile_count == 1):
                    pl.when((planes_near == i) & (tiles_near == j + 1))(
                        functools.partial(act, i, j)
                    )

    def tiles(n):
        return size_ref.at[pl.ds(0, n // (8 * blk))]

    def dual_all(act):
        for far in range(2):
            for j in range(1, min(tile_count, 3)):
                count = j * zs + far * (1 + j)
                pl.when((far_there == (far == 1)) & (tiles_near == j + 1))(
                    functools.partial(act, tiles(count * (mems + 1) * bins))
                )

    def rows_all(act):
        for j in range(1, min(tile_count, 3)):
            pl.when(tiles_near == j + 1)(functools.partial(act, tiles(j * mems * zs * cols)))

    def planes_all(act):
        for i in range(1, min(plane_count, 3)):
            pl.when(planes_near == i)(functools.partial(act, tiles(i * mems * (rs + 2) * cols)))

    def blocks_of(along, side, i, j):
        return size_ref.at[pl.ds(0, (i * along + (i + 1) * j * side) // 8)]

    proj_len = bin_blocks * zs
    back_len = pix_blocks * zs
    edge_len = col_blocks * zs

    def proj_span(dt, sending):
        return pl.ds(0, proj_len)

    def back_span(dt, sending):
        if dt == 0:
            return pl.ds(0, back_len)
        first = (dt < 0) == sending
        return pl.ds(0 if first else back_len - edge_len, edge_len)

    def each_neighbour(act):
        for dp, dt in NEIGHBOURS:
            if (dp, dt) != (0, 0):
                pl.when(exists(dp, dt))(functools.partial(act, dp, dt))


    row8 = iota((8, blk), 0)
    group = 8 // zs
    of_row = lax.div(row8, zs)
    z_row = lax.rem(row8, zs)

    def pattern(rows):
        out = jnp.broadcast_to(rows[0], (8, blk))
        for z in range(1, zs):
            out = jnp.where(z_row == z, jnp.broadcast_to(rows[z], (8, blk)), out)
        high, low = split(out)
        return jnp.concatenate([high.astype(F32), low.astype(F32)], 0)

    for q in range(pix_blocks):
        r, b = q // col_blocks, q % col_blocks
        src_pat[q] = pattern(
            [primal_ref[1, z, r : r + 1, b * blk : (b + 1) * blk] for z in range(zs)]
        )

    def masked(pat, target, total):
        pieces = []
        for half in (pat[:8], pat[8:]):
            for g in range(total // 8):
                pieces.append(jnp.where(of_row + g * group == target, half, 0.0))
        return jnp.concatenate(pieces, 0).astype(BF16)

    def part_copy(a):
        return pltpu.make_async_remote_copy(
            src_ref=part.at[a],
            dst_ref=got.at[lax.rem(t - a - 1 + 2 * tile_count, tile_count)],
            send_sem=part_send.at[0],
            recv_sem=part_recv.at[0],
            device_id=(p, a),
            device_id_type=MESH,
        )

    def forward(n, carry):
        a = far(n)
        w_copy(a).wait()
        high, low = split(wbuf[a].reshape(slots * blk, blk))
        for s in range(slots):
            rows = slice(s * blk, (s + 1) * blk)
            wback[a, :blk, rows] = high[rows]
            wback[a, blk:, rows] = low[rows]
        left = []
        for s in range(slots):
            target = jnp.where(s < cnt_ref[0, a], bin_ref[t, a, s], -1)
            left.append(masked(src_pat[pix_ref[0, a, s]], target, proj_len))
        o = dot(jnp.concatenate(left, 1), jnp.concatenate([high, low], 1))
        part[a] = o[:proj_len, :blk] + o[proj_len:, :blk] + o[:proj_len, blk:]

        @pl.when(n == ahead)
        def _():
            pl.semaphore_wait(barrier, tile_count - 1 + planes_near * tiles_near)
            for m in range(ahead):
                part_copy(far(m)).start()

        @pl.when((n >= ahead) & (n < tile_count - 1))
        def _():
            part_copy(a).start()

        return carry

    ahead = angles - 2
    lax.fori_loop(0, angles, forward, 0)

    send_known()

    for load in loads[6:]:
        load.wait()
    hidden = db_ref.shape[1]
    moved[...] = jnp.zeros_like(moved)

    def flatten(kern):
        for kx in range(3):
            kern[kx * hidden : (kx + 1) * hidden, :] = moved[kx].T[:hidden, :]

    for kz in range(3):
        for ky in range(3):
            for kx in range(3):
                at = (kz * 3 + ky) * 8
                moved[kx, at : at + mems + 2, :hidden] = dk_ref[kz, ky, kx]
    flatten(dkern)
    d_span = -(-(zs + 2) * 3 // 8) * 8
    p_span = -(-(zs + 2) * (rs + 2) // 8) * 8
    proj_rows[...] = jnp.zeros_like(proj_rows)
    back_rows[...] = jnp.zeros_like(back_rows)
    expand_new(dkern, ad, zs, 1, d_span)
    d_rows = -(-mems * zs // 8) * 8
    p_rows = -(-mems * zs * rs // 8) * 8
    d_mix = mixing_matrix(dm_ref, d_rows, zs)
    eye = jnp.where(iota((blk, blk), 0) == iota((blk, blk), 1), 1.0, 0.0).astype(BF16)

    def turn(first, last):
        @pl.loop(first, last)
        def _(n):
            a = near(n)
            for s in range(slots):
                rows = slice(s * blk, (s + 1) * blk)
                wturn[a, rows, :] = lax.dot_general(
                    eye, wback[a, :, rows], (((1,), (1,)), ((), ())), preferred_element_type=F32
                ).astype(BF16)

    turn(0, angles)
    total = part[t]
    all_copy(got, part_send, part_recv).wait_recv()
    for n in range(tile_count - 1):
        total = total + got[n]
    proj[CENTRE] = total
    each_neighbour(lambda dp, dt: block_copy(proj, proj_send, proj_recv, dp, dt, proj_span).start())
    dual_all(lambda size: all_copy(size, xd_send, xd_recv).wait_recv())
    dual_near().start()
    for z in range(zs):
        for aa in range(3):
            for c in range(mems + 1):
                at = c if c < mems else NEW + 1
                xd[1 + z, aa, at : at + 1, :] = xraw[aa, c, z]
    low_side = jnp.where(odd, 0, 1)
    dual_near().wait_recv()
    for zz, side in ((0, low_side), (zs + 1, 1 - low_side)):
        for aa in range(3):
            for c in range(mems + 1):
                at = c if c < mems else NEW + 1
                xd[zz, aa, at : at + 1, :] = xside[side, aa, c]
    known_part(dkern, db_ref, xd[...].reshape((zs + 2) * 3 * 8, bins), known_d, zs, 1)
    proj_all = functools.partial(blocks_of, proj_len, proj_len)
    back_all = functools.partial(blocks_of, back_len, edge_len)
    each_count(lambda i, j: all_copy(proj_all(i, j), proj_send, proj_recv).wait_recv())

    def source_of(at, count):
        if at == 0:
            return -1, count - 1
        if at == count + 1:
            return 1, 0
        return 0, at - 1

    for zz in range(zs + 2):
        dp, z = source_of(zz, zs)
        for aa in range(3):
            dt, _ = source_of(aa, 1)
            k = (dp + 1) * 3 + dt + 1
            at = zz * 3 + aa
            for b in range(bin_blocks):
                row = b * zs + z
                proj_rows[at : at + 1, b * blk : (b + 1) * blk] = proj[k, row : row + 1, :]

    res = finish(
        proj_rows, ad, known_d, ds_ref, d_mix, dh_ref, hd_high, hd_low, zs, d_span
    )
    lead = [res[z : z + 1] + xraw[1, 0, z] for z in range(zs)]
    for b in range(bin_blocks):
        for z in range(zs):
            row = b * zs + z
            nd[t, row : row + 1, :] = lead[z][:, b * blk : (b + 1) * blk]

    def nd_copy(a):
        return pltpu.make_async_remote_copy(
            src_ref=nd.at[t],
            dst_ref=nd.at[t],
            send_sem=nd_send.at[0],
            recv_sem=nd_recv.at[t],
            device_id=(p, a),
            device_id_type=MESH,
        )

    def nd_arrival(a):
        return pltpu.make_async_remote_copy(
            src_ref=nd.at[a],
            dst_ref=nd.at[a],
            send_sem=nd_send.at[0],
            recv_sem=nd_recv.at[a],
            device_id=(p, a),
            device_id_type=MESH,
        )

    @pl.loop(1, tile_count)
    def _(n):
        nd_copy(near(tile_count - n)).start()

    for c in range(mems):
        for z in range(zs):
            at = c * zs + z
            out_dual[c, z] = res[at : at + 1] + xraw[1, c, z]

    rows_all(lambda size: all_copy(size, row_send, row_recv).wait_recv())
    send_planes()


    together = 2

    for c in range(mems + 1):
        for kz in range(3):
            for ky in range(3):
                at = (kz * 3 + ky) * 8 + c
                taps = pk_ref[c, kz, ky]
                for kx in range(3):
                    moved[kx, at : at + 1, :hidden] = taps[kx : kx + 1]
    flatten(pkern)
    expand_new(pkern, ap, zs, rs, p_span)
    p_mix = mixing_matrix(pm_ref, p_rows, zs * rs)
    def backward(m, acc):
        picks = [near(m * together + i) for i in range(together)]
        for i, a in enumerate(picks):

            @pl.when(m * together + i > 0)
            def _():
                nd_arrival(a).wait_recv()

        for i, a in enumerate(picks):
            for b in range(bin_blocks):
                nd_pat[i, b] = pattern([nd[a, b * zs + z : b * zs + z + 1, :] for z in range(zs)])
        for i, a in enumerate(picks):
            left = []
            for s in range(slots):
                target = jnp.where(s < cnt_ref[0, a], pix_ref[0, a, s], -1)
                left.append(masked(nd_pat[i, bin_ref[t, a, s]], target, back_len))
            acc = acc + dot(jnp.concatenate(left, 1), wturn[a])
        return acc

    acc = lax.fori_loop(0, tile_count // together, backward, jnp.zeros((2 * back_len, 2 * blk), F32))
    back[CENTRE] = acc[:back_len, :blk] + acc[back_len:, :blk] + acc[:back_len, blk:]
    each_neighbour(lambda dp, dt: block_copy(back, back_send, back_recv, dp, dt, back_span).start())
    planes_all(lambda size: all_copy(size, xp_send, xp_recv).wait_recv())
    for c in range(mems):
        for zz in range(zs + 2):
            for rr in range(rs + 2):
                if 0 < rr <= rs:
                    r = slice(rr - 1, rr)
                    row = primal_ref[c, zz - 1, r, :] if 0 < zz <= zs else pplane[min(zz, 1), c, r, :]
                else:
                    side = 0 if rr == 0 else 1
                    row = prow_in[side, c, zz - 1] if 0 < zz <= zs else pprow[min(zz, 1), side, c]
                xp[zz, rr, c : c + 1, :] = row
    known_part(
        pkern, pb_ref, xp[...].reshape((zs + 2) * (rs + 2) * 8, cols), known_p, zs, rs
    )
    each_count(lambda i, j: all_copy(back_all(i, j), back_send, back_recv).wait_recv())
    for zz in range(zs + 2):
        dp, z = source_of(zz, zs)
        for rr in range(rs + 2):
            dt, r = source_of(rr, rs)
            k = (dp + 1) * 3 + dt + 1
            at = zz * (rs + 2) + rr
            for b in range(col_blocks):
                row = (r * col_blocks + b) * zs + z
                back_rows[at : at + 1, b * blk : (b + 1) * blk] = back[k, row : row + 1, :]

    res = finish(
        back_rows, ap, known_p, ps_ref, p_mix, ph_ref, hp_high, hp_low, zs * rs, p_span
    )
    for c in range(mems):
        for z in range(zs):
            at = (c * zs + z) * rs
            out_primal[c, z] = res[at : at + rs] + primal_ref[c, z]

    dual_all(lambda size: all_copy(size, xd_send, xd_recv).wait_send())
    dual_near().wait_send()
    rows_all(lambda size: all_copy(size, row_send, row_recv).wait_send())
    planes_all(lambda size: all_copy(size, xp_send, xp_recv).wait_send())
    each_count(lambda i, j: all_copy(proj_all(i, j), proj_send, proj_recv).wait_send())
    each_count(lambda i, j: all_copy(back_all(i, j), back_send, back_recv).wait_send())
    all_copy(got, part_send, part_recv).wait_send()
    all_copy(got, nd_send, part_recv).wait_send()


def store(a_ref, b_ref, a_hbm, b_hbm, sem):
    copies = [
        pltpu.make_async_copy(x, y, sem.at[i])
        for i, (x, y) in enumerate(((a_ref, a_hbm), (b_ref, b_hbm)))
    ]
    for copy in copies:
        copy.start()
    for copy in copies:
        copy.wait()


def per_device(plane_count, tile_count, *args):
    (primal, dual, measured, weights, pix, bins_of, count, dk, db, ds, dm, dh, pk, pb, ps, pm, ph) = args
    mems, zs, rs, cols = primal.shape
    bins = dual.shape[3]
    angles, slots, blk = weights.shape[1:4]
    assert dual.shape[2] == 1 and angles == tile_count and 8 % zs == 0 and mems == NEW
    assert plane_count % 2 == 0
    hidden = db.shape[0]
    proj_len = bins // blk * zs
    back_len = rs * cols // blk * zs
    d_span = -(-(zs + 2) * 3 // 8) * 8
    p_span = -(-(zs + 2) * (rs + 2) // 8) * 8
    cells = zs * rs
    most = max(
        (2 * zs + 3) * (mems + 1) * bins,
        2 * mems * (rs + 2) * cols,
        2 * mems * zs * cols,
        8 * proj_len * blk,
        (2 * back_len + 6 * cols // blk * zs) * blk,
    )
    vmem = pl.BlockSpec(memory_space=pltpu.VMEM)
    dma = pltpu.SemaphoreType.DMA
    operands = (
        primal, dual, measured, weights, pix, bins_of, count,
        jnp.transpose(dk, (2, 3, 4, 1, 0)), db[None], ds[None], dm, dh[None],
        jnp.transpose(pk, (1, 2, 3, 4, 0)), pb[None], ps[None], pm, ph[None],
    )
    held = pl.pallas_call(
        functools.partial(body, plane_count, tile_count),
        out_shape=(
            pltpu.VMEM(primal.shape, F32),
            pltpu.VMEM(dual.shape, F32),
        ),
        in_specs=[pl.BlockSpec(memory_space=pl.ANY)] * len(operands),
        out_specs=(vmem, vmem),
        scratch_shapes=[
            (pltpu.SMEM if x.dtype == jnp.int32 else pltpu.VMEM)(x.shape, x.dtype)
            for x in operands
            if not any(x is y for y in (weights, dual, measured))
        ]
        + [
            pltpu.VMEM((3 * hidden, 72), F32),
            pltpu.VMEM((3 * hidden, 72), F32),
            pltpu.VMEM((3, 72, 128), F32),
            dma((len(operands) - 1,)),
            pltpu.VMEM((angles, slots, blk, blk), F32),
            pltpu.VMEM((angles, 2 * blk, slots * blk), BF16),
            pltpu.VMEM((angles, slots * blk, 2 * blk), BF16),
            pltpu.VMEM((rs * cols // blk, 16, blk), F32),
            pltpu.VMEM((2, bins // blk, 16, blk), F32),
            pltpu.VMEM((tile_count, proj_len, blk), F32),
            pltpu.VMEM((tile_count - 1, proj_len, blk), F32),
            pltpu.VMEM((-(-most // (8 * blk)), 8, blk), F32),
            pltpu.VMEM((tile_count, proj_len, blk), F32),
            pltpu.VMEM((3, mems + 1, zs, 1, bins), F32),
            pltpu.VMEM((2, 3, mems + 1, 1, bins), F32),
            pltpu.VMEM((2, mems, zs, 1, cols), F32),
            pltpu.VMEM((2, mems, zs, 1, cols), F32),
            pltpu.VMEM((2, mems, rs, cols), F32),
            pltpu.VMEM((2, 2, mems, 1, cols), F32),
            pltpu.VMEM((zs + 2, 3, 8, bins), F32),
            pltpu.VMEM((zs + 2, rs + 2, 8, cols), F32),
            pltpu.VMEM((9, proj_len, blk), F32),
            pltpu.VMEM((9, back_len, blk), F32),
            pltpu.VMEM((d_span, bins), F32),
            pltpu.VMEM((p_span, cols), F32),
            pltpu.VMEM((zs * hidden, -(-9 * d_span // 128) * 128), BF16),
            pltpu.VMEM((cells * hidden, -(-9 * p_span // 128) * 128), BF16),
            pltpu.VMEM((zs * hidden, bins), F32),
            pltpu.VMEM((cells * hidden, cols), F32),
            pltpu.VMEM((zs * hidden, bins), BF16),
            pltpu.VMEM((zs * hidden, bins), BF16),
            pltpu.VMEM((cells * hidden, cols), BF16),
            pltpu.VMEM((cells * hidden, cols), BF16),
            dma((angles,)),
            dma((1,)),
            dma((1,)),
            dma((1,)),
            dma((tile_count,)),
        ]
        + [dma((1,))] * 12,
        compiler_params=pltpu.CompilerParams(
            collective_id=0, has_side_effects=True, vmem_limit_bytes=60 * 2**20
        ),
    )(*operands)
    hbm = pl.BlockSpec(memory_space=pl.ANY)
    return pl.pallas_call(
        store,
        out_shape=[jax.ShapeDtypeStruct(x.shape, F32) for x in held],
        in_specs=[vmem] * 2,
        out_specs=[hbm] * 2,
        scratch_shapes=[dma((2,))],
    )(*[pltpu.with_memory_space_constraint(x, pltpu.VMEM) for x in held])


def solution(mesh):
    in_specs = (
        P(None, "plane", "tile", None),
        P(None, "plane", "tile", None),
        P("plane", "tile", None),
        P("tile", None, None, None, None),
        P("tile", None, None),
        P(),
        P("tile", None),
    ) + (P(),) * 10
    out_specs = (P(None, "plane", "tile", None), P(None, "plane", "tile", None))
    return jax.shard_map(
        functools.partial(per_device, mesh.shape["plane"], mesh.shape["tile"]),
        mesh=mesh,
        in_specs=in_specs,
        out_specs=out_specs,
        check_vma=False,
    )
```

```python
import functools

import jax
import jax.numpy as jnp
from jax import lax
from jax.experimental import pallas as pl
from jax.experimental.pallas import tpu as pltpu
from jax.sharding import PartitionSpec as P

F32 = jnp.float32
BF16 = jnp.bfloat16
MESH = pl.DeviceIdType.MESH
NEIGHBOURS = [(dp, dt) for dp in (-1, 0, 1) for dt in (-1, 0, 1)]
CENTRE = 4
NEW = 5


def split(x):
    high = x.astype(BF16)
    return high, (x - high.astype(F32)).astype(BF16)


def dot(a, b):
    return jnp.dot(a, b, preferred_element_type=F32)


def iota(shape, dim):
    return lax.broadcasted_iota(jnp.int32, shape, dim)


def shifted_sum(y, hidden):
    width = y.shape[1]
    lane = iota((hidden, width), 1)
    left = jnp.where(lane == 0, 0.0, pltpu.roll(y[:hidden], 1, 1))
    right = jnp.where(lane == width - 1, 0.0, pltpu.roll(y[2 * hidden :], width - 1, 1))
    return left + y[hidden : 2 * hidden] + right


def column(row, rows, repeat):
    shape = (rows, row.shape[1])
    low = iota(shape, 1) * repeat
    at = iota(shape, 0)
    hit = (at >= low) & (at < low + repeat)
    return jnp.sum(jnp.where(hit, row, 0.0), axis=1, keepdims=True)


def row_code(rows, lanes, step_rows):
    at = iota((rows, lanes), 0)
    tap = lax.shift_right_logical(at, 3)
    kz = (tap >= 3).astype(jnp.int32) + (tap >= 6).astype(jnp.int32)
    return kz * step_rows + (tap - 3 * kz), at & 7


def expand_new(kern_ref, out_ref, zs, rs, span):
    kern = kern_ref[...]
    taps = kern.shape[0]
    hidden = taps // 3
    high, low = split(kern)
    lanes = out_ref.shape[1]
    code, chan = row_code(kern.shape[1], lanes, rs + 2)
    lane = iota((kern.shape[1], lanes), 1)
    keep = lax.rem(iota((hidden, lanes), 1), 3 * span) < 2 * span
    for i in range(zs * rs):
        spread = 0.0
        for kx in range(3):
            place = code + ((i // rs) * (rs + 2) + i % rs + 3 * kx * span)
            hit = (lane == place) | (lane == place + span) | (lane == place + 2 * span)
            own = slice(kx * hidden, (kx + 1) * hidden)
            spread += dot(
                jnp.concatenate([high[own], low[own]], 0),
                jnp.where(hit & (chan == NEW), 1.0, 0.0).astype(BF16),
            )
        out_ref[i * hidden : (i + 1) * hidden, :] = jnp.where(
            keep, spread[:hidden], spread[hidden:]
        ).astype(BF16)


def known_part(kern_ref, bias_ref, cells, known_ref, zs, rs):
    hidden = bias_ref.shape[1]
    kern = kern_ref[...]
    taps = kern.shape[0]
    depth = cells.shape[0]
    lanes = -(-depth // 128) * 128
    both = jnp.concatenate(split(kern), 0)
    code, chan = row_code(kern.shape[1], lanes, rs + 2)
    base = code * 8 + chan
    lane = iota((kern.shape[1], lanes), 1)
    high, low = split(cells)
    bias = column(bias_ref[...], hidden, 1)
    for i in range(zs * rs):
        place = base + ((i // rs) * (rs + 2) + i % rs) * 8
        a = dot(both, jnp.where(lane == place, 1.0, 0.0).astype(BF16))[:, :depth].astype(BF16)
        y = dot(a, high)
        y = y[:taps] + y[taps:] + dot(a[:taps], low)
        known_ref[i * hidden : (i + 1) * hidden, :] = shifted_sum(y, hidden) + bias


def mixing_matrix(mix_ref, rows, cells):
    outs, hidden = mix_ref.shape
    lanes = cells * hidden
    mix = jnp.concatenate([mix_ref[...], jnp.zeros((8 - outs, hidden), F32)], 0)
    both = jnp.concatenate(split(mix), 0)
    at = iota((hidden, lanes), 1)
    rep = jnp.where(lax.rem(at, hidden) == iota((hidden, lanes), 0), 1.0, 0.0).astype(BF16)
    wide = dot(both, rep)
    low_row = iota((rows, 8), 1) * cells
    at_row = iota((rows, 8), 0)
    pick = jnp.where((at_row >= low_row) & (at_row < low_row + cells), 1.0, 0.0).astype(BF16)
    cell_of_lane = lax.div(iota((rows, lanes), 1), hidden)
    own = lax.rem(iota((rows, lanes), 0), cells) == cell_of_lane
    high = jnp.where(own, dot(pick, wide[:8].astype(BF16)), 0.0).astype(BF16)
    low = jnp.where(own, dot(pick, wide[8:].astype(BF16)), 0.0).astype(BF16)
    return jnp.concatenate([high, low], 0)


def finish(new_ref, a_ref, known_ref, slope_ref, mix, shift_ref, hid_high, hid_low, cells, span):
    hidden = slope_ref.shape[1]
    new = new_ref[...]
    width = new.shape[1]
    lane = iota(new.shape, 1)
    left = jnp.where(lane == 0, 0.0, pltpu.roll(new, 1, 1))
    right = jnp.where(lane == width - 1, 0.0, pltpu.roll(new, width - 1, 1))
    pieces = []
    for piece in (left, new, right):
        high, low = split(piece)
        high, low = high.astype(F32), low.astype(F32)
        pieces += [high, low, high]
    stack = jnp.concatenate(pieces, 0).astype(BF16)
    y = dot(a_ref[:, : 9 * span], stack)
    slope = column(slope_ref[...], hidden, 1)
    for i in range(cells):
        h = known_ref[i * hidden : (i + 1) * hidden, :] + y[i * hidden : (i + 1) * hidden]
        h = jnp.where(h > 0, h, slope * h)
        hh, hl = split(h)
        hid_high[i * hidden : (i + 1) * hidden, :] = hh
        hid_low[i * hidden : (i + 1) * hidden, :] = hl
    rows = mix.shape[0] // 2
    first = dot(mix, hid_high[...])
    out = first[:rows] + first[rows:] + dot(mix[:rows], hid_low[...])
    return out + column(shift_ref[...], rows, cells)


def body(
    plane_count,
    tile_count,
    primal_hbm,
    dual_hbm,
    measured_hbm,
    w_hbm,
    pix_hbm,
    bin_hbm,
    cnt_hbm,
    dk_hbm,
    db_hbm,
    ds_hbm,
    dm_hbm,
    dh_hbm,
    pk_hbm,
    pb_hbm,
    ps_hbm,
    pm_hbm,
    ph_hbm,
    out_primal,
    out_dual,
    primal_ref,
    pix_ref,
    bin_ref,
    cnt_ref,
    dk_ref,
    db_ref,
    ds_ref,
    dm_ref,
    dh_ref,
    pk_ref,
    pb_ref,
    ps_ref,
    pm_ref,
    ph_ref,
    dkern,
    pkern,
    moved,
    in_sem,
    wbuf,
    wback,
    wturn,
    src_pat,
    nd_pat,
    part,
    got,
    size_ref,
    nd,
    xraw,
    xside,
    prow_out,
    prow_in,
    pplane,
    pprow,
    xd,
    xp,
    proj,
    back,
    proj_rows,
    back_rows,
    ad,
    ap,
    known_d,
    known_p,
    hd_high,
    hd_low,
    hp_high,
    hp_low,
    w_sem,
    part_send,
    part_recv,
    nd_send,
    nd_recv,
    xd_send,
    xd_recv,
    near_send,
    near_recv,
    row_send,
    row_recv,
    xp_send,
    xp_recv,
    proj_send,
    proj_recv,
    back_send,
    back_recv,
):
    mems, zs, rs, cols = primal_hbm.shape
    bins = dual_hbm.shape[3]
    angles, slots, blk = w_hbm.shape[1], w_hbm.shape[2], w_hbm.shape[3]
    pix_blocks = rs * cols // blk
    bin_blocks = bins // blk
    col_blocks = cols // blk
    p = lax.axis_index("plane")
    t = lax.axis_index("tile")

    def angle_at(n):
        return lax.rem(t + n, tile_count)

    def near(n):
        pair, pairs, m = lax.div(t, 2), tile_count // 2, lax.div(n, 2)
        inner = jnp.minimum(pair, pairs - 1 - pair)
        away = lax.div(m + 1, 2)
        either = jnp.where(lax.rem(m, 2) == 1, pair + away, pair - away)
        beyond = jnp.where(pair < pairs - 1 - pair, pair + m - inner, pair - m + inner)
        own = lax.rem(t, 2)
        return 2 * jnp.where(m <= 2 * inner, either, beyond) + jnp.where(
            lax.rem(n, 2) == 0, own, 1 - own
        )

    def far(n):
        return near(tile_count - 1 - n)

    def w_copy(a):
        return pltpu.make_async_copy(w_hbm.at[0, a], wbuf.at[a], w_sem.at[a])

    inputs = (
        (primal_hbm, primal_ref),
        (pix_hbm, pix_ref),
        (bin_hbm, bin_ref),
        (cnt_hbm, cnt_ref),
        (dual_hbm, xraw.at[1, pl.ds(0, mems)]),
        (measured_hbm, xraw.at[1, mems]),
        (dk_hbm, dk_ref),
        (db_hbm, db_ref),
        (ds_hbm, ds_ref),
        (dm_hbm, dm_ref),
        (dh_hbm, dh_ref),
        (pk_hbm, pk_ref),
        (pb_hbm, pb_ref),
        (ps_hbm, ps_ref),
        (pm_hbm, pm_ref),
        (ph_hbm, ph_ref),
    )
    loads = [pltpu.make_async_copy(a, b, in_sem.at[i]) for i, (a, b) in enumerate(inputs)]
    for load in loads[:4]:
        load.start()
    w_copy(far(0)).start()
    def exists(dp, dt):
        there = None
        for step, at, count in ((dp, p, plane_count), (dt, t, tile_count)):
            if step:
                ok = at > 0 if step < 0 else at < count - 1
                there = ok if there is None else there & ok
        return there

    barrier = pltpu.get_barrier_semaphore()

    @pl.loop(1, tile_count)
    def _(n):
        pl.semaphore_signal(barrier, inc=1, device_id=(p, near(tile_count - n)), device_id_type=MESH)

    for dp, dt in NEIGHBOURS:
        if dp:

            @pl.when(exists(dp, dt))
            def _():
                pl.semaphore_signal(
                    barrier, inc=1, device_id=(p + dp, t + dt), device_id_type=MESH
                )

    for load in loads[4:6]:
        load.start()

    @pl.loop(1, angles)
    def _(n):
        w_copy(far(n)).start()

    for load in loads[6:]:
        load.start()

    for ref in (xd, xp):
        ref[...] = jnp.zeros_like(ref)

    def clear(ref):
        ref[...] = jnp.zeros_like(ref)

    planes_near = (p > 0).astype(jnp.int32) + (p < plane_count - 1).astype(jnp.int32)
    tiles_near = 1 + (t > 0).astype(jnp.int32) + (t < tile_count - 1).astype(jnp.int32)
    odd = lax.rem(p, 2) == 1
    far_step = jnp.where(odd, 1, -1)
    far_edge = jnp.where(odd, zs - 1, 0)
    near_edge = jnp.where(odd, 0, zs - 1)
    far_there = (p + far_step >= 0) & (p + far_step < plane_count)

    def missing(there, *refs):
        @pl.when(jnp.logical_not(there))
        def _():
            for ref in refs:
                clear(ref)

    for dt in (-1, 1):
        missing(exists(0, dt), xraw.at[1 + dt], prow_in.at[(dt + 1) // 2])
        missing(far_there & exists(0, dt), xside.at[1, 1 + dt])
    missing(far_there, xside.at[1, 1])
    for dp in (-1, 1):
        missing(exists(dp, 0), pplane.at[(dp + 1) // 2], pprow.at[(dp + 1) // 2])
    for dp, dt in [x for x in NEIGHBOURS if x != (0, 0)]:
        k = (dp + 1) * 3 + dt + 1
        missing(exists(dp, dt), proj.at[k], back.at[k])

    for load in loads[:6]:
        load.wait()
    for z in range(zs):
        for c in range(mems):
            prow_out[0, c, z] = primal_ref[c, z, 0:1, :]
            prow_out[1, c, z] = primal_ref[c, z, rs - 1 : rs, :]

    def remote(src, dst, send, recv, device):
        return pltpu.make_async_remote_copy(
            src_ref=src,
            dst_ref=dst,
            send_sem=send.at[0],
            recv_sem=recv.at[0],
            device_id=device,
            device_id_type=MESH,
        )

    def dual_tile(dt):
        return remote(xraw.at[1], xraw.at[1 - dt], xd_send, xd_recv, (p, t + dt))

    def dual_far(dt):
        return remote(
            xraw.at[1, :, far_edge], xside.at[1, 1 - dt], xd_send, xd_recv, (p + far_step, t + dt)
        )

    def dual_near():
        return remote(
            xraw.at[:, :, near_edge], xside.at[0], near_send, near_recv, (p - far_step, t)
        )

    def row_tile(dt):
        side = (dt + 1) // 2
        return remote(prow_out.at[side], prow_in.at[1 - side], row_send, row_recv, (p, t + dt))

    def plane_copies(dp):
        z, side = (0, 1) if dp < 0 else (zs - 1, 0)
        to = (p + dp, t)
        return (
            remote(primal_ref.at[:, z], pplane.at[side], xp_send, xp_recv, to),
            remote(prow_in.at[:, :, z], pprow.at[side], xp_send, xp_recv, to),
        )

    def send_known():
        for dt in (-1, 1):
            pl.when(exists(0, dt))(lambda dt=dt: dual_tile(dt).start())
        pl.when(far_there)(lambda: dual_far(0).start())
        for dt in (-1, 1):
            pl.when(far_there & exists(0, dt))(lambda dt=dt: dual_far(dt).start())
        for dt in (-1, 1):
            pl.when(exists(0, dt))(lambda dt=dt: row_tile(dt).start())

    def send_planes():
        for dp in (-1, 1):

            @pl.when(exists(dp, 0))
            def _():
                for copy in plane_copies(dp):
                    copy.start()

    def block_copy(ref, send, recv, dp, dt, span):
        k = (dp + 1) * 3 + dt + 1
        return pltpu.make_async_remote_copy(
            src_ref=ref.at[CENTRE, span(dt, True)],
            dst_ref=ref.at[8 - k, span(dt, True)],
            send_sem=send.at[0],
            recv_sem=recv.at[0],
            device_id=(p + dp, t + dt),
            device_id_type=MESH,
        )

    def all_copy(size, send, recv):
        return pltpu.make_async_remote_copy(
            src_ref=size,
            dst_ref=size,
            send_sem=send.at[0],
            recv_sem=recv.at[0],
            device_id=(p, angle_at(1)),
            device_id_type=MESH,
        )

    def each_count(act):
        for i in range(min(plane_count, 3)):
            for j in range(min(tile_count, 3)):
                if (i or plane_count == 1) and (j or tile_count == 1):
                    pl.when((planes_near == i) & (tiles_near == j + 1))(
                        functools.partial(act, i, j)
                    )

    def tiles(n):
        return size_ref.at[pl.ds(0, n // (8 * blk))]

    def dual_all(act):
        for far in range(2):
            for j in range(1, min(tile_count, 3)):
                count = j * zs + far * (1 + j)
                pl.when((far_there == (far == 1)) & (tiles_near == j + 1))(
                    functools.partial(act, tiles(count * (mems + 1) * bins))
                )

    def rows_all(act):
        for j in range(1, min(tile_count, 3)):
            pl.when(tiles_near == j + 1)(functools.partial(act, tiles(j * mems * zs * cols)))

    def planes_all(act):
        for i in range(1, min(plane_count, 3)):
            pl.when(planes_near == i)(functools.partial(act, tiles(i * mems * (rs + 2) * cols)))

    def blocks_of(along, side, i, j):
        return size_ref.at[pl.ds(0, (i * along + (i + 1) * j * side) // 8)]

    proj_len = bin_blocks * zs
    back_len = pix_blocks * zs
    edge_len = col_blocks * zs

    def proj_span(dt, sending):
        return pl.ds(0, proj_len)

    def back_span(dt, sending):
        if dt == 0:
            return pl.ds(0, back_len)
        first = (dt < 0) == sending
        return pl.ds(0 if first else back_len - edge_len, edge_len)

    def each_neighbour(act):
        for dp, dt in NEIGHBOURS:
            if (dp, dt) != (0, 0):
                pl.when(exists(dp, dt))(functools.partial(act, dp, dt))


    row8 = iota((8, blk), 0)
    group = 8 // zs
    of_row = lax.div(row8, zs)
    z_row = lax.rem(row8, zs)

    def pattern(rows):
        out = jnp.broadcast_to(rows[0], (8, blk))
        for z in range(1, zs):
            out = jnp.where(z_row == z, jnp.broadcast_to(rows[z], (8, blk)), out)
        high, low = split(out)
        return jnp.concatenate([high.astype(F32), low.astype(F32)], 0)

    for q in range(pix_blocks):
        r, b = q // col_blocks, q % col_blocks
        src_pat[q] = pattern(
            [primal_ref[1, z, r : r + 1, b * blk : (b + 1) * blk] for z in range(zs)]
        )

    def masked(pat, target, total):
        pieces = []
        for half in (pat[:8], pat[8:]):
            for g in range(total // 8):
                pieces.append(jnp.where(of_row + g * group == target, half, 0.0))
        return jnp.concatenate(pieces, 0).astype(BF16)

    def part_copy(a):
        return pltpu.make_async_remote_copy(
            src_ref=part.at[a],
            dst_ref=got.at[lax.rem(t - a - 1 + 2 * tile_count, tile_count)],
            send_sem=part_send.at[0],
            recv_sem=part_recv.at[0],
            device_id=(p, a),
            device_id_type=MESH,
        )

    def forward(n, carry):
        a = far(n)
        w_copy(a).wait()
        high, low = split(wbuf[a].reshape(slots * blk, blk))
        for s in range(slots):
            rows = slice(s * blk, (s + 1) * blk)
            wback[a, :blk, rows] = high[rows]
            wback[a, blk:, rows] = low[rows]
        left = []
        for s in range(slots):
            target = jnp.where(s < cnt_ref[0, a], bin_ref[t, a, s], -1)
            left.append(masked(src_pat[pix_ref[0, a, s]], target, proj_len))
        o = dot(jnp.concatenate(left, 1), jnp.concatenate([high, low], 1))
        part[a] = o[:proj_len, :blk] + o[proj_len:, :blk] + o[:proj_len, blk:]

        @pl.when(n == ahead)
        def _():
            pl.semaphore_wait(barrier, tile_count - 1 + planes_near * tiles_near)
            for m in range(ahead):
                part_copy(far(m)).start()

        @pl.when((n >= ahead) & (n < tile_count - 1))
        def _():
            part_copy(a).start()

        return carry

    ahead = angles - 2
    lax.fori_loop(0, angles, forward, 0)

    send_known()

    for load in loads[6:]:
        load.wait()
    hidden = db_ref.shape[1]
    moved[...] = jnp.zeros_like(moved)

    def flatten(kern):
        for kx in range(3):
            kern[kx * hidden : (kx + 1) * hidden, :] = moved[kx].T[:hidden, :]

    for kz in range(3):
        for ky in range(3):
            for kx in range(3):
                at = (kz * 3 + ky) * 8
                moved[kx, at : at + mems + 2, :hidden] = dk_ref[kz, ky, kx]
    flatten(dkern)
    d_span = -(-(zs + 2) * 3 // 8) * 8
    p_span = -(-(zs + 2) * (rs + 2) // 8) * 8
    proj_rows[...] = jnp.zeros_like(proj_rows)
    back_rows[...] = jnp.zeros_like(back_rows)
    expand_new(dkern, ad, zs, 1, d_span)
    d_rows = -(-mems * zs // 8) * 8
    p_rows = -(-mems * zs * rs // 8) * 8
    d_mix = mixing_matrix(dm_ref, d_rows, zs)
    eye = jnp.where(iota((blk, blk), 0) == iota((blk, blk), 1), 1.0, 0.0).astype(BF16)

    def turn(first, last):
        @pl.loop(first, last)
        def _(n):
            a = near(n)
            for s in range(slots):
                rows = slice(s * blk, (s + 1) * blk)
                wturn[a, rows, :] = lax.dot_general(
                    eye, wback[a, :, rows], (((1,), (1,)), ((), ())), preferred_element_type=F32
                ).astype(BF16)

    turn(0, angles)
    total = part[t]
    all_copy(got, part_send, part_recv).wait_recv()
    for n in range(tile_count - 1):
        total = total + got[n]
    proj[CENTRE] = total
    each_neighbour(lambda dp, dt: block_copy(proj, proj_send, proj_recv, dp, dt, proj_span).start())
    dual_all(lambda size: all_copy(size, xd_send, xd_recv).wait_recv())
    dual_near().start()
    for z in range(zs):
        for aa in range(3):
            for c in range(mems + 1):
                at = c if c < mems else NEW + 1
                xd[1 + z, aa, at : at + 1, :] = xraw[aa, c, z]
    low_side = jnp.where(odd, 0, 1)
    dual_near().wait_recv()
    for zz, side in ((0, low_side), (zs + 1, 1 - low_side)):
        for aa in range(3):
            for c in range(mems + 1):
                at = c if c < mems else NEW + 1
                xd[zz, aa, at : at + 1, :] = xside[side, aa, c]
    known_part(dkern, db_ref, xd[...].reshape((zs + 2) * 3 * 8, bins), known_d, zs, 1)
    proj_all = functools.partial(blocks_of, proj_len, proj_len)
    back_all = functools.partial(blocks_of, back_len, edge_len)
    each_count(lambda i, j: all_copy(proj_all(i, j), proj_send, proj_recv).wait_recv())

    def source_of(at, count):
        if at == 0:
            return -1, count - 1
        if at == count + 1:
            return 1, 0
        return 0, at - 1

    for zz in range(zs + 2):
        dp, z = source_of(zz, zs)
        for aa in range(3):
            dt, _ = source_of(aa, 1)
            k = (dp + 1) * 3 + dt + 1
            at = zz * 3 + aa
            for b in range(bin_blocks):
                row = b * zs + z
                proj_rows[at : at + 1, b * blk : (b + 1) * blk] = proj[k, row : row + 1, :]

    res = finish(
        proj_rows, ad, known_d, ds_ref, d_mix, dh_ref, hd_high, hd_low, zs, d_span
    )
    lead = [res[z : z + 1] + xraw[1, 0, z] for z in range(zs)]
    for b in range(bin_blocks):
        for z in range(zs):
            row = b * zs + z
            nd[t, row : row + 1, :] = lead[z][:, b * blk : (b + 1) * blk]

    def nd_copy(a):
        return pltpu.make_async_remote_copy(
            src_ref=nd.at[t],
            dst_ref=nd.at[t],
            send_sem=nd_send.at[0],
            recv_sem=nd_recv.at[t],
            device_id=(p, a),
            device_id_type=MESH,
        )

    def nd_arrival(a):
        return pltpu.make_async_remote_copy(
            src_ref=nd.at[a],
            dst_ref=nd.at[a],
            send_sem=nd_send.at[0],
            recv_sem=nd_recv.at[a],
            device_id=(p, a),
            device_id_type=MESH,
        )

    @pl.loop(1, tile_count)
    def _(n):
        nd_copy(near(tile_count - n)).start()

    for c in range(mems):
        for z in range(zs):
            at = c * zs + z
            out_dual[c, z] = res[at : at + 1] + xraw[1, c, z]

    rows_all(lambda size: all_copy(size, row_send, row_recv).wait_recv())
    send_planes()


    together = 2

    for c in range(mems + 1):
        for kz in range(3):
            for ky in range(3):
                at = (kz * 3 + ky) * 8 + c
                taps = pk_ref[c, kz, ky]
                for kx in range(3):
                    moved[kx, at : at + 1, :hidden] = taps[kx : kx + 1]
    flatten(pkern)
    expand_new(pkern, ap, zs, rs, p_span)
    p_mix = mixing_matrix(pm_ref, p_rows, zs * rs)
    def backward(m, acc):
        picks = [near(m * together + i) for i in range(together)]
        for i, a in enumerate(picks):

            @pl.when(m * together + i > 0)
            def _():
                nd_arrival(a).wait_recv()

        for i, a in enumerate(picks):
            for b in range(bin_blocks):
                nd_pat[i, b] = pattern([nd[a, b * zs + z : b * zs + z + 1, :] for z in range(zs)])
        for i, a in enumerate(picks):
            left = []
            for s in range(slots):
                target = jnp.where(s < cnt_ref[0, a], pix_ref[0, a, s], -1)
                left.append(masked(nd_pat[i, bin_ref[t, a, s]], target, back_len))
            acc = acc + dot(jnp.concatenate(left, 1), wturn[a])
        return acc

    acc = lax.fori_loop(0, tile_count // together, backward, jnp.zeros((2 * back_len, 2 * blk), F32))
    back[CENTRE] = acc[:back_len, :blk] + acc[back_len:, :blk] + acc[:back_len, blk:]
    each_neighbour(lambda dp, dt: block_copy(back, back_send, back_recv, dp, dt, back_span).start())
    planes_all(lambda size: all_copy(size, xp_send, xp_recv).wait_recv())
    for c in range(mems):
        for zz in range(zs + 2):
            for rr in range(rs + 2):
                if 0 < rr <= rs:
                    r = slice(rr - 1, rr)
                    row = primal_ref[c, zz - 1, r, :] if 0 < zz <= zs else pplane[min(zz, 1), c, r, :]
                else:
                    side = 0 if rr == 0 else 1
                    row = prow_in[side, c, zz - 1] if 0 < zz <= zs else pprow[min(zz, 1), side, c]
                xp[zz, rr, c : c + 1, :] = row
    known_part(
        pkern, pb_ref, xp[...].reshape((zs + 2) * (rs + 2) * 8, cols), known_p, zs, rs
    )
    each_count(lambda i, j: all_copy(back_all(i, j), back_send, back_recv).wait_recv())
    for zz in range(zs + 2):
        dp, z = source_of(zz, zs)
        for rr in range(rs + 2):
            dt, r = source_of(rr, rs)
            k = (dp + 1) * 3 + dt + 1
            at = zz * (rs + 2) + rr
            for b in range(col_blocks):
                row = (r * col_blocks + b) * zs + z
                back_rows[at : at + 1, b * blk : (b + 1) * blk] = back[k, row : row + 1, :]

    res = finish(
        back_rows, ap, known_p, ps_ref, p_mix, ph_ref, hp_high, hp_low, zs * rs, p_span
    )
    for c in range(mems):
        for z in range(zs):
            at = (c * zs + z) * rs
            out_primal[c, z] = res[at : at + rs] + primal_ref[c, z]

    dual_all(lambda size: all_copy(size, xd_send, xd_recv).wait_send())
    dual_near().wait_send()
    rows_all(lambda size: all_copy(size, row_send, row_recv).wait_send())
    planes_all(lambda size: all_copy(size, xp_send, xp_recv).wait_send())
    each_count(lambda i, j: all_copy(proj_all(i, j), proj_send, proj_recv).wait_send())
    each_count(lambda i, j: all_copy(back_all(i, j), back_send, back_recv).wait_send())
    all_copy(got, part_send, part_recv).wait_send()
    all_copy(got, nd_send, part_recv).wait_send()


def store(a_ref, b_ref, a_hbm, b_hbm, sem):
    copies = [
        pltpu.make_async_copy(x, y, sem.at[i])
        for i, (x, y) in enumerate(((a_ref, a_hbm), (b_ref, b_hbm)))
    ]
    for copy in copies:
        copy.start()
    for copy in copies:
        copy.wait()


def per_device(plane_count, tile_count, *args):
    (primal, dual, measured, weights, pix, bins_of, count, dk, db, ds, dm, dh, pk, pb, ps, pm, ph) = args
    mems, zs, rs, cols = primal.shape
    bins = dual.shape[3]
    angles, slots, blk = weights.shape[1:4]
    assert dual.shape[2] == 1 and angles == tile_count and 8 % zs == 0 and mems == NEW
    assert plane_count % 2 == 0 and tile_count % 2 == 0
    hidden = db.shape[0]
    proj_len = bins // blk * zs
    back_len = rs * cols // blk * zs
    d_span = -(-(zs + 2) * 3 // 8) * 8
    p_span = -(-(zs + 2) * (rs + 2) // 8) * 8
    cells = zs * rs
    most = max(
        (2 * zs + 3) * (mems + 1) * bins,
        2 * mems * (rs + 2) * cols,
        2 * mems * zs * cols,
        8 * proj_len * blk,
        (2 * back_len + 6 * cols // blk * zs) * blk,
    )
    vmem = pl.BlockSpec(memory_space=pltpu.VMEM)
    dma = pltpu.SemaphoreType.DMA
    operands = (
        primal, dual, measured, weights, pix, bins_of, count,
        jnp.transpose(dk, (2, 3, 4, 1, 0)), db[None], ds[None], dm, dh[None],
        jnp.transpose(pk, (1, 2, 3, 4, 0)), pb[None], ps[None], pm, ph[None],
    )
    held = pl.pallas_call(
        functools.partial(body, plane_count, tile_count),
        out_shape=(
            pltpu.VMEM(primal.shape, F32),
            pltpu.VMEM(dual.shape, F32),
        ),
        in_specs=[pl.BlockSpec(memory_space=pl.ANY)] * len(operands),
        out_specs=(vmem, vmem),
        scratch_shapes=[
            (pltpu.SMEM if x.dtype == jnp.int32 else pltpu.VMEM)(x.shape, x.dtype)
            for x in operands
            if not any(x is y for y in (weights, dual, measured))
        ]
        + [
            pltpu.VMEM((3 * hidden, 72), F32),
            pltpu.VMEM((3 * hidden, 72), F32),
            pltpu.VMEM((3, 72, 128), F32),
            dma((len(operands) - 1,)),
            pltpu.VMEM((angles, slots, blk, blk), F32),
            pltpu.VMEM((angles, 2 * blk, slots * blk), BF16),
            pltpu.VMEM((angles, slots * blk, 2 * blk), BF16),
            pltpu.VMEM((rs * cols // blk, 16, blk), F32),
            pltpu.VMEM((2, bins // blk, 16, blk), F32),
            pltpu.VMEM((tile_count, proj_len, blk), F32),
            pltpu.VMEM((tile_count - 1, proj_len, blk), F32),
            pltpu.VMEM((-(-most // (8 * blk)), 8, blk), F32),
            pltpu.VMEM((tile_count, proj_len, blk), F32),
            pltpu.VMEM((3, mems + 1, zs, 1, bins), F32),
            pltpu.VMEM((2, 3, mems + 1, 1, bins), F32),
            pltpu.VMEM((2, mems, zs, 1, cols), F32),
            pltpu.VMEM((2, mems, zs, 1, cols), F32),
            pltpu.VMEM((2, mems, rs, cols), F32),
            pltpu.VMEM((2, 2, mems, 1, cols), F32),
            pltpu.VMEM((zs + 2, 3, 8, bins), F32),
            pltpu.VMEM((zs + 2, rs + 2, 8, cols), F32),
            pltpu.VMEM((9, proj_len, blk), F32),
            pltpu.VMEM((9, back_len, blk), F32),
            pltpu.VMEM((d_span, bins), F32),
            pltpu.VMEM((p_span, cols), F32),
            pltpu.VMEM((zs * hidden, -(-9 * d_span // 128) * 128), BF16),
            pltpu.VMEM((cells * hidden, -(-9 * p_span // 128) * 128), BF16),
            pltpu.VMEM((zs * hidden, bins), F32),
            pltpu.VMEM((cells * hidden, cols), F32),
            pltpu.VMEM((zs * hidden, bins), BF16),
            pltpu.VMEM((zs * hidden, bins), BF16),
            pltpu.VMEM((cells * hidden, cols), BF16),
            pltpu.VMEM((cells * hidden, cols), BF16),
            dma((angles,)),
            dma((1,)),
            dma((1,)),
            dma((1,)),
            dma((tile_count,)),
        ]
        + [dma((1,))] * 12,
        compiler_params=pltpu.CompilerParams(
            collective_id=0, has_side_effects=True, vmem_limit_bytes=60 * 2**20
        ),
    )(*operands)
    hbm = pl.BlockSpec(memory_space=pl.ANY)
    return pl.pallas_call(
        store,
        out_shape=[jax.ShapeDtypeStruct(x.shape, F32) for x in held],
        in_specs=[vmem] * 2,
        out_specs=[hbm] * 2,
        scratch_shapes=[dma((2,))],
    )(*[pltpu.with_memory_space_constraint(x, pltpu.VMEM) for x in held])


def solution(mesh):
    in_specs = (
        P(None, "plane", "tile", None),
        P(None, "plane", "tile", None),
        P("plane", "tile", None),
        P("tile", None, None, None, None),
        P("tile", None, None),
        P(),
        P("tile", None),
    ) + (P(),) * 10
    out_specs = (P(None, "plane", "tile", None), P(None, "plane", "tile", None))
    return jax.shard_map(
        functools.partial(per_device, mesh.shape["plane"], mesh.shape["tile"]),
        mesh=mesh,
        in_specs=in_specs,
        out_specs=out_specs,
        check_vma=False,
    )
```

```python
import functools

import jax
import jax.numpy as jnp
from jax import lax
from jax.experimental import pallas as pl
from jax.experimental.pallas import tpu as pltpu
from jax.sharding import PartitionSpec as P

F32 = jnp.float32
BF16 = jnp.bfloat16
MESH = pl.DeviceIdType.MESH
NEIGHBOURS = [(dp, dt) for dp in (-1, 0, 1) for dt in (-1, 0, 1)]
CENTRE = 4
NEW = 5


def split(x):
    high = x.astype(BF16)
    return high, (x - high.astype(F32)).astype(BF16)


def dot(a, b):
    return jnp.dot(a, b, preferred_element_type=F32)


def iota(shape, dim):
    return lax.broadcasted_iota(jnp.int32, shape, dim)


def shifted_sum(y, hidden):
    width = y.shape[1]
    lane = iota((hidden, width), 1)
    left = jnp.where(lane == 0, 0.0, pltpu.roll(y[:hidden], 1, 1))
    right = jnp.where(lane == width - 1, 0.0, pltpu.roll(y[2 * hidden :], width - 1, 1))
    return left + y[hidden : 2 * hidden] + right


def column(row, rows, repeat):
    shape = (rows, row.shape[1])
    low = iota(shape, 1) * repeat
    at = iota(shape, 0)
    hit = (at >= low) & (at < low + repeat)
    return jnp.sum(jnp.where(hit, row, 0.0), axis=1, keepdims=True)


def row_code(rows, lanes, step_rows):
    at = iota((rows, lanes), 0)
    tap = lax.shift_right_logical(at, 3)
    kz = (tap >= 3).astype(jnp.int32) + (tap >= 6).astype(jnp.int32)
    return kz * step_rows + (tap - 3 * kz), at & 7


def expand_new(kern_ref, out_ref, zs, rs, span):
    kern = kern_ref[...]
    taps = kern.shape[0]
    hidden = taps // 3
    high, low = split(kern)
    lanes = out_ref.shape[1]
    code, chan = row_code(kern.shape[1], lanes, rs + 2)
    lane = iota((kern.shape[1], lanes), 1)
    keep = lax.rem(iota((hidden, lanes), 1), 3 * span) < 2 * span
    for i in range(zs * rs):
        spread = 0.0
        for kx in range(3):
            place = code + ((i // rs) * (rs + 2) + i % rs + 3 * kx * span)
            hit = (lane == place) | (lane == place + span) | (lane == place + 2 * span)
            own = slice(kx * hidden, (kx + 1) * hidden)
            spread += dot(
                jnp.concatenate([high[own], low[own]], 0),
                jnp.where(hit & (chan == NEW), 1.0, 0.0).astype(BF16),
            )
        out_ref[i * hidden : (i + 1) * hidden, :] = jnp.where(
            keep, spread[:hidden], spread[hidden:]
        ).astype(BF16)


def known_part(kern_ref, bias_ref, cells, known_ref, zs, rs):
    hidden = bias_ref.shape[1]
    kern = kern_ref[...]
    taps = kern.shape[0]
    depth = cells.shape[0]
    lanes = -(-depth // 128) * 128
    both = jnp.concatenate(split(kern), 0)
    code, chan = row_code(kern.shape[1], lanes, rs + 2)
    base = code * 8 + chan
    lane = iota((kern.shape[1], lanes), 1)
    high, low = split(cells)
    bias = column(bias_ref[...], hidden, 1)
    for i in range(zs * rs):
        place = base + ((i // rs) * (rs + 2) + i % rs) * 8
        a = dot(both, jnp.where(lane == place, 1.0, 0.0).astype(BF16))[:, :depth].astype(BF16)
        y = dot(a, high)
        y = y[:taps] + y[taps:] + dot(a[:taps], low)
        known_ref[i * hidden : (i + 1) * hidden, :] = shifted_sum(y, hidden) + bias


def mixing_matrix(mix_ref, rows, cells):
    outs, hidden = mix_ref.shape
    lanes = cells * hidden
    mix = jnp.concatenate([mix_ref[...], jnp.zeros((8 - outs, hidden), F32)], 0)
    both = jnp.concatenate(split(mix), 0)
    at = iota((hidden, lanes), 1)
    rep = jnp.where(lax.rem(at, hidden) == iota((hidden, lanes), 0), 1.0, 0.0).astype(BF16)
    wide = dot(both, rep)
    low_row = iota((rows, 8), 1) * cells
    at_row = iota((rows, 8), 0)
    pick = jnp.where((at_row >= low_row) & (at_row < low_row + cells), 1.0, 0.0).astype(BF16)
    cell_of_lane = lax.div(iota((rows, lanes), 1), hidden)
    own = lax.rem(iota((rows, lanes), 0), cells) == cell_of_lane
    high = jnp.where(own, dot(pick, wide[:8].astype(BF16)), 0.0).astype(BF16)
    low = jnp.where(own, dot(pick, wide[8:].astype(BF16)), 0.0).astype(BF16)
    return jnp.concatenate([high, low], 0)


def finish(new_ref, a_ref, known_ref, slope_ref, mix, shift_ref, hid_high, hid_low, cells, span):
    hidden = slope_ref.shape[1]
    new = new_ref[...]
    width = new.shape[1]
    lane = iota(new.shape, 1)
    left = jnp.where(lane == 0, 0.0, pltpu.roll(new, 1, 1))
    right = jnp.where(lane == width - 1, 0.0, pltpu.roll(new, width - 1, 1))
    pieces = []
    for piece in (left, new, right):
        high, low = split(piece)
        high, low = high.astype(F32), low.astype(F32)
        pieces += [high, low, high]
    stack = jnp.concatenate(pieces, 0).astype(BF16)
    y = dot(a_ref[:, : 9 * span], stack)
    slope = column(slope_ref[...], hidden, 1)
    for i in range(cells):
        h = known_ref[i * hidden : (i + 1) * hidden, :] + y[i * hidden : (i + 1) * hidden]
        h = jnp.where(h > 0, h, slope * h)
        hh, hl = split(h)
        hid_high[i * hidden : (i + 1) * hidden, :] = hh
        hid_low[i * hidden : (i + 1) * hidden, :] = hl
    rows = mix.shape[0] // 2
    first = dot(mix, hid_high[...])
    out = first[:rows] + first[rows:] + dot(mix[:rows], hid_low[...])
    return out + column(shift_ref[...], rows, cells)


def body(
    plane_count,
    tile_count,
    primal_hbm,
    dual_hbm,
    measured_hbm,
    w_hbm,
    pix_hbm,
    bin_hbm,
    cnt_hbm,
    dk_hbm,
    db_hbm,
    ds_hbm,
    dm_hbm,
    dh_hbm,
    pk_hbm,
    pb_hbm,
    ps_hbm,
    pm_hbm,
    ph_hbm,
    out_primal,
    out_dual,
    primal_ref,
    pix_ref,
    bin_ref,
    cnt_ref,
    dk_ref,
    db_ref,
    ds_ref,
    dm_ref,
    dh_ref,
    pk_ref,
    pb_ref,
    ps_ref,
    pm_ref,
    ph_ref,
    dkern,
    pkern,
    moved,
    in_sem,
    wbuf,
    wback,
    wturn,
    src_pat,
    nd_pat,
    part,
    got,
    size_ref,
    nd,
    xraw,
    xside,
    prow_out,
    prow_in,
    pplane,
    pprow,
    xd,
    xp,
    proj,
    back,
    proj_rows,
    back_rows,
    ad,
    ap,
    known_d,
    known_p,
    hd_high,
    hd_low,
    hp_high,
    hp_low,
    w_sem,
    part_send,
    part_recv,
    nd_send,
    nd_recv,
    xd_send,
    xd_recv,
    near_send,
    near_recv,
    row_send,
    row_recv,
    xp_send,
    xp_recv,
    proj_send,
    proj_recv,
    back_send,
    back_recv,
):
    mems, zs, rs, cols = primal_hbm.shape
    bins = dual_hbm.shape[3]
    angles, slots, blk = w_hbm.shape[1], w_hbm.shape[2], w_hbm.shape[3]
    pix_blocks = rs * cols // blk
    bin_blocks = bins // blk
    col_blocks = cols // blk
    p = lax.axis_index("plane")
    t = lax.axis_index("tile")

    def angle_at(n):
        return lax.rem(t + n, tile_count)

    def near(n):
        pair, pairs, m = lax.div(t, 2), tile_count // 2, lax.div(n, 2)
        inner = jnp.minimum(pair, pairs - 1 - pair)
        away = lax.div(m + 1, 2)
        either = jnp.where(lax.rem(m, 2) == 1, pair + away, pair - away)
        beyond = jnp.where(pair < pairs - 1 - pair, pair + m - inner, pair - m + inner)
        own = lax.rem(t, 2)
        return 2 * jnp.where(m <= 2 * inner, either, beyond) + jnp.where(
            lax.rem(n, 2) == 0, own, 1 - own
        )

    def far(n):
        return near(tile_count - 1 - n)

    def w_copy(a):
        return pltpu.make_async_copy(w_hbm.at[0, a], wbuf.at[a], w_sem.at[a])

    inputs = (
        (primal_hbm, primal_ref),
        (pix_hbm, pix_ref),
        (bin_hbm, bin_ref),
        (cnt_hbm, cnt_ref),
        (dual_hbm, xraw.at[1, pl.ds(0, mems)]),
        (measured_hbm, xraw.at[1, mems]),
        (dk_hbm, dk_ref),
        (db_hbm, db_ref),
        (ds_hbm, ds_ref),
        (dm_hbm, dm_ref),
        (dh_hbm, dh_ref),
        (pk_hbm, pk_ref),
        (pb_hbm, pb_ref),
        (ps_hbm, ps_ref),
        (pm_hbm, pm_ref),
        (ph_hbm, ph_ref),
    )
    loads = [pltpu.make_async_copy(a, b, in_sem.at[i]) for i, (a, b) in enumerate(inputs)]
    for load in loads[:4]:
        load.start()
    w_copy(far(0)).start()
    def exists(dp, dt):
        there = None
        for step, at, count in ((dp, p, plane_count), (dt, t, tile_count)):
            if step:
                ok = at > 0 if step < 0 else at < count - 1
                there = ok if there is None else there & ok
        return there

    barrier = pltpu.get_barrier_semaphore()

    @pl.loop(1, tile_count)
    def _(n):
        pl.semaphore_signal(barrier, inc=1, device_id=(p, near(tile_count - n)), device_id_type=MESH)

    for dp, dt in NEIGHBOURS:
        if dp:

            @pl.when(exists(dp, dt))
            def _():
                pl.semaphore_signal(
                    barrier, inc=1, device_id=(p + dp, t + dt), device_id_type=MESH
                )

    for load in loads[4:6]:
        load.start()

    @pl.loop(1, angles)
    def _(n):
        w_copy(far(n)).start()

    for load in loads[6:]:
        load.start()

    for ref in (xd, xp):
        ref[...] = jnp.zeros_like(ref)

    def clear(ref):
        ref[...] = jnp.zeros_like(ref)

    planes_near = (p > 0).astype(jnp.int32) + (p < plane_count - 1).astype(jnp.int32)
    tiles_near = 1 + (t > 0).astype(jnp.int32) + (t < tile_count - 1).astype(jnp.int32)
    odd = lax.rem(p, 2) == 1
    far_step = jnp.where(odd, 1, -1)
    far_edge = jnp.where(odd, zs - 1, 0)
    near_edge = jnp.where(odd, 0, zs - 1)
    far_there = (p + far_step >= 0) & (p + far_step < plane_count)

    def missing(there, *refs):
        @pl.when(jnp.logical_not(there))
        def _():
            for ref in refs:
                clear(ref)

    for dt in (-1, 1):
        missing(exists(0, dt), xraw.at[1 + dt], prow_in.at[(dt + 1) // 2])
        missing(far_there & exists(0, dt), xside.at[1, 1 + dt])
    missing(far_there, xside.at[1, 1])
    for dp in (-1, 1):
        missing(exists(dp, 0), pplane.at[(dp + 1) // 2], pprow.at[(dp + 1) // 2])
    for dp, dt in [x for x in NEIGHBOURS if x != (0, 0)]:
        k = (dp + 1) * 3 + dt + 1
        missing(exists(dp, dt), proj.at[k], back.at[k])

    for load in loads[:6]:
        load.wait()
    for z in range(zs):
        for c in range(mems):
            prow_out[0, c, z] = primal_ref[c, z, 0:1, :]
            prow_out[1, c, z] = primal_ref[c, z, rs - 1 : rs, :]

    def remote(src, dst, send, recv, device):
        return pltpu.make_async_remote_copy(
            src_ref=src,
            dst_ref=dst,
            send_sem=send.at[0],
            recv_sem=recv.at[0],
            device_id=device,
            device_id_type=MESH,
        )

    def dual_tile(dt):
        return remote(xraw.at[1], xraw.at[1 - dt], xd_send, xd_recv, (p, t + dt))

    def dual_far(dt):
        return remote(
            xraw.at[1, :, far_edge], xside.at[1, 1 - dt], xd_send, xd_recv, (p + far_step, t + dt)
        )

    def dual_near():
        return remote(
            xraw.at[:, :, near_edge], xside.at[0], near_send, near_recv, (p - far_step, t)
        )

    def row_tile(dt):
        side = (dt + 1) // 2
        return remote(prow_out.at[side], prow_in.at[1 - side], row_send, row_recv, (p, t + dt))

    def plane_copies(dp):
        z, side = (0, 1) if dp < 0 else (zs - 1, 0)
        to = (p + dp, t)
        return (
            remote(primal_ref.at[:, z], pplane.at[side], xp_send, xp_recv, to),
            remote(prow_in.at[:, :, z], pprow.at[side], xp_send, xp_recv, to),
        )

    def send_known():
        for dt in (-1, 1):
            pl.when(exists(0, dt))(lambda dt=dt: dual_tile(dt).start())
        pl.when(far_there)(lambda: dual_far(0).start())
        for dt in (-1, 1):
            pl.when(far_there & exists(0, dt))(lambda dt=dt: dual_far(dt).start())
        for dt in (-1, 1):
            pl.when(exists(0, dt))(lambda dt=dt: row_tile(dt).start())

    def send_planes():
        for dp in (-1, 1):

            @pl.when(exists(dp, 0))
            def _():
                for copy in plane_copies(dp):
                    copy.start()

    def block_copy(ref, send, recv, dp, dt, span):
        k = (dp + 1) * 3 + dt + 1
        return pltpu.make_async_remote_copy(
            src_ref=ref.at[CENTRE, span(dt, True)],
            dst_ref=ref.at[8 - k, span(dt, True)],
            send_sem=send.at[0],
            recv_sem=recv.at[0],
            device_id=(p + dp, t + dt),
            device_id_type=MESH,
        )

    def all_copy(size, send, recv):
        return pltpu.make_async_remote_copy(
            src_ref=size,
            dst_ref=size,
            send_sem=send.at[0],
            recv_sem=recv.at[0],
            device_id=(p, angle_at(1)),
            device_id_type=MESH,
        )

    def each_count(act):
        for i in range(min(plane_count, 3)):
            for j in range(min(tile_count, 3)):
                if (i or plane_count == 1) and (j or tile_count == 1):
                    pl.when((planes_near == i) & (tiles_near == j + 1))(
                        functools.partial(act, i, j)
                    )

    def tiles(n):
        return size_ref.at[pl.ds(0, n // (8 * blk))]

    def dual_all(act):
        for far in range(2):
            for j in range(1, min(tile_count, 3)):
                count = j * zs + far * (1 + j)
                pl.when((far_there == (far == 1)) & (tiles_near == j + 1))(
                    functools.partial(act, tiles(count * (mems + 1) * bins))
                )

    def rows_all(act):
        for j in range(1, min(tile_count, 3)):
            pl.when(tiles_near == j + 1)(functools.partial(act, tiles(j * mems * zs * cols)))

    def planes_all(act):
        for i in range(1, min(plane_count, 3)):
            pl.when(planes_near == i)(functools.partial(act, tiles(i * mems * (rs + 2) * cols)))

    def blocks_of(along, side, i, j):
        return size_ref.at[pl.ds(0, (i * along + (i + 1) * j * side) // 8)]

    proj_len = bin_blocks * zs
    back_len = pix_blocks * zs
    edge_len = col_blocks * zs

    def proj_span(dt, sending):
        return pl.ds(0, proj_len)

    def back_span(dt, sending):
        if dt == 0:
            return pl.ds(0, back_len)
        first = (dt < 0) == sending
        return pl.ds(0 if first else back_len - edge_len, edge_len)

    def each_neighbour(act):
        for dp, dt in NEIGHBOURS:
            if (dp, dt) != (0, 0):
                pl.when(exists(dp, dt))(functools.partial(act, dp, dt))


    row8 = iota((8, blk), 0)
    group = 8 // zs
    of_row = lax.div(row8, zs)
    z_row = lax.rem(row8, zs)

    def pattern(rows):
        out = jnp.broadcast_to(rows[0], (8, blk))
        for z in range(1, zs):
            out = jnp.where(z_row == z, jnp.broadcast_to(rows[z], (8, blk)), out)
        high, low = split(out)
        return jnp.concatenate([high.astype(F32), low.astype(F32)], 0)

    for q in range(pix_blocks):
        r, b = q // col_blocks, q % col_blocks
        src_pat[q] = pattern(
            [primal_ref[1, z, r : r + 1, b * blk : (b + 1) * blk] for z in range(zs)]
        )

    def masked(pat, target, total):
        pieces = []
        for half in (pat[:8], pat[8:]):
            for g in range(total // 8):
                pieces.append(jnp.where(of_row + g * group == target, half, 0.0))
        return jnp.concatenate(pieces, 0).astype(BF16)

    def part_copy(a):
        return pltpu.make_async_remote_copy(
            src_ref=part.at[a],
            dst_ref=got.at[lax.rem(t - a - 1 + 2 * tile_count, tile_count)],
            send_sem=part_send.at[0],
            recv_sem=part_recv.at[0],
            device_id=(p, a),
            device_id_type=MESH,
        )

    def forward(n, carry):
        a = far(n)
        w_copy(a).wait()
        high, low = split(wbuf[a].reshape(slots * blk, blk))
        for s in range(slots):
            rows = slice(s * blk, (s + 1) * blk)
            wback[a, :blk, rows] = high[rows]
            wback[a, blk:, rows] = low[rows]
        left = []
        for s in range(slots):
            target = jnp.where(s < cnt_ref[0, a], bin_ref[t, a, s], -1)
            left.append(masked(src_pat[pix_ref[0, a, s]], target, proj_len))
        o = dot(jnp.concatenate(left, 1), jnp.concatenate([high, low], 1))
        part[a] = o[:proj_len, :blk] + o[proj_len:, :blk] + o[:proj_len, blk:]

        @pl.when(n == ahead)
        def _():
            pl.semaphore_wait(barrier, tile_count - 1 + planes_near * tiles_near)
            for m in range(ahead):
                part_copy(far(m)).start()

        @pl.when((n >= ahead) & (n < tile_count - 1))
        def _():
            part_copy(a).start()

        return carry

    ahead = angles - 3
    lax.fori_loop(0, angles, forward, 0)

    send_known()

    for load in loads[6:]:
        load.wait()
    hidden = db_ref.shape[1]
    moved[...] = jnp.zeros_like(moved)

    def flatten(kern):
        for kx in range(3):
            kern[kx * hidden : (kx + 1) * hidden, :] = moved[kx].T[:hidden, :]

    for kz in range(3):
        for ky in range(3):
            for kx in range(3):
                at = (kz * 3 + ky) * 8
                moved[kx, at : at + mems + 2, :hidden] = dk_ref[kz, ky, kx]
    flatten(dkern)
    d_span = -(-(zs + 2) * 3 // 8) * 8
    p_span = -(-(zs + 2) * (rs + 2) // 8) * 8
    proj_rows[...] = jnp.zeros_like(proj_rows)
    back_rows[...] = jnp.zeros_like(back_rows)
    expand_new(dkern, ad, zs, 1, d_span)
    d_rows = -(-mems * zs // 8) * 8
    p_rows = -(-mems * zs * rs // 8) * 8
    d_mix = mixing_matrix(dm_ref, d_rows, zs)
    eye = jnp.where(iota((blk, blk), 0) == iota((blk, blk), 1), 1.0, 0.0).astype(BF16)

    def turn(first, last):
        @pl.loop(first, last)
        def _(n):
            a = near(n)
            for s in range(slots):
                rows = slice(s * blk, (s + 1) * blk)
                wturn[a, rows, :] = lax.dot_general(
                    eye, wback[a, :, rows], (((1,), (1,)), ((), ())), preferred_element_type=F32
                ).astype(BF16)

    turn(0, angles)
    total = part[t]
    all_copy(got, part_send, part_recv).wait_recv()
    for n in range(tile_count - 1):
        total = total + got[n]
    proj[CENTRE] = total
    each_neighbour(lambda dp, dt: block_copy(proj, proj_send, proj_recv, dp, dt, proj_span).start())
    dual_all(lambda size: all_copy(size, xd_send, xd_recv).wait_recv())
    dual_near().start()
    for z in range(zs):
        for aa in range(3):
            for c in range(mems + 1):
                at = c if c < mems else NEW + 1
                xd[1 + z, aa, at : at + 1, :] = xraw[aa, c, z]
    low_side = jnp.where(odd, 0, 1)
    dual_near().wait_recv()
    for zz, side in ((0, low_side), (zs + 1, 1 - low_side)):
        for aa in range(3):
            for c in range(mems + 1):
                at = c if c < mems else NEW + 1
                xd[zz, aa, at : at + 1, :] = xside[side, aa, c]
    known_part(dkern, db_ref, xd[...].reshape((zs + 2) * 3 * 8, bins), known_d, zs, 1)
    proj_all = functools.partial(blocks_of, proj_len, proj_len)
    back_all = functools.partial(blocks_of, back_len, edge_len)
    each_count(lambda i, j: all_copy(proj_all(i, j), proj_send, proj_recv).wait_recv())

    def source_of(at, count):
        if at == 0:
            return -1, count - 1
        if at == count + 1:
            return 1, 0
        return 0, at - 1

    for zz in range(zs + 2):
        dp, z = source_of(zz, zs)
        for aa in range(3):
            dt, _ = source_of(aa, 1)
            k = (dp + 1) * 3 + dt + 1
            at = zz * 3 + aa
            for b in range(bin_blocks):
                row = b * zs + z
                proj_rows[at : at + 1, b * blk : (b + 1) * blk] = proj[k, row : row + 1, :]

    res = finish(
        proj_rows, ad, known_d, ds_ref, d_mix, dh_ref, hd_high, hd_low, zs, d_span
    )
    lead = [res[z : z + 1] + xraw[1, 0, z] for z in range(zs)]
    for b in range(bin_blocks):
        for z in range(zs):
            row = b * zs + z
            nd[t, row : row + 1, :] = lead[z][:, b * blk : (b + 1) * blk]

    def nd_copy(a):
        return pltpu.make_async_remote_copy(
            src_ref=nd.at[t],
            dst_ref=nd.at[t],
            send_sem=nd_send.at[0],
            recv_sem=nd_recv.at[t],
            device_id=(p, a),
            device_id_type=MESH,
        )

    def nd_arrival(a):
        return pltpu.make_async_remote_copy(
            src_ref=nd.at[a],
            dst_ref=nd.at[a],
            send_sem=nd_send.at[0],
            recv_sem=nd_recv.at[a],
            device_id=(p, a),
            device_id_type=MESH,
        )

    @pl.loop(1, tile_count)
    def _(n):
        nd_copy(near(tile_count - n)).start()

    for c in range(mems):
        for z in range(zs):
            at = c * zs + z
            out_dual[c, z] = res[at : at + 1] + xraw[1, c, z]

    rows_all(lambda size: all_copy(size, row_send, row_recv).wait_recv())
    send_planes()


    together = 2

    for c in range(mems + 1):
        for kz in range(3):
            for ky in range(3):
                at = (kz * 3 + ky) * 8 + c
                taps = pk_ref[c, kz, ky]
                for kx in range(3):
                    moved[kx, at : at + 1, :hidden] = taps[kx : kx + 1]
    flatten(pkern)
    expand_new(pkern, ap, zs, rs, p_span)
    p_mix = mixing_matrix(pm_ref, p_rows, zs * rs)
    def backward(m, acc):
        picks = [near(m * together + i) for i in range(together)]
        for i, a in enumerate(picks):

            @pl.when(m * together + i > 0)
            def _():
                nd_arrival(a).wait_recv()

        for i, a in enumerate(picks):
            for b in range(bin_blocks):
                nd_pat[i, b] = pattern([nd[a, b * zs + z : b * zs + z + 1, :] for z in range(zs)])
        for i, a in enumerate(picks):
            left = []
            for s in range(slots):
                target = jnp.where(s < cnt_ref[0, a], pix_ref[0, a, s], -1)
                left.append(masked(nd_pat[i, bin_ref[t, a, s]], target, back_len))
            acc = acc + dot(jnp.concatenate(left, 1), wturn[a])
        return acc

    acc = lax.fori_loop(0, tile_count // together, backward, jnp.zeros((2 * back_len, 2 * blk), F32))
    back[CENTRE] = acc[:back_len, :blk] + acc[back_len:, :blk] + acc[:back_len, blk:]
    each_neighbour(lambda dp, dt: block_copy(back, back_send, back_recv, dp, dt, back_span).start())
    planes_all(lambda size: all_copy(size, xp_send, xp_recv).wait_recv())
    for c in range(mems):
        for zz in range(zs + 2):
            for rr in range(rs + 2):
                if 0 < rr <= rs:
                    r = slice(rr - 1, rr)
                    row = primal_ref[c, zz - 1, r, :] if 0 < zz <= zs else pplane[min(zz, 1), c, r, :]
                else:
                    side = 0 if rr == 0 else 1
                    row = prow_in[side, c, zz - 1] if 0 < zz <= zs else pprow[min(zz, 1), side, c]
                xp[zz, rr, c : c + 1, :] = row
    known_part(
        pkern, pb_ref, xp[...].reshape((zs + 2) * (rs + 2) * 8, cols), known_p, zs, rs
    )
    each_count(lambda i, j: all_copy(back_all(i, j), back_send, back_recv).wait_recv())
    for zz in range(zs + 2):
        dp, z = source_of(zz, zs)
        for rr in range(rs + 2):
            dt, r = source_of(rr, rs)
            k = (dp + 1) * 3 + dt + 1
            at = zz * (rs + 2) + rr
            for b in range(col_blocks):
                row = (r * col_blocks + b) * zs + z
                back_rows[at : at + 1, b * blk : (b + 1) * blk] = back[k, row : row + 1, :]

    res = finish(
        back_rows, ap, known_p, ps_ref, p_mix, ph_ref, hp_high, hp_low, zs * rs, p_span
    )
    for c in range(mems):
        for z in range(zs):
            at = (c * zs + z) * rs
            out_primal[c, z] = res[at : at + rs] + primal_ref[c, z]

    dual_all(lambda size: all_copy(size, xd_send, xd_recv).wait_send())
    dual_near().wait_send()
    rows_all(lambda size: all_copy(size, row_send, row_recv).wait_send())
    planes_all(lambda size: all_copy(size, xp_send, xp_recv).wait_send())
    each_count(lambda i, j: all_copy(proj_all(i, j), proj_send, proj_recv).wait_send())
    each_count(lambda i, j: all_copy(back_all(i, j), back_send, back_recv).wait_send())
    all_copy(got, part_send, part_recv).wait_send()
    all_copy(got, nd_send, part_recv).wait_send()


def store(a_ref, b_ref, a_hbm, b_hbm, sem):
    copies = [
        pltpu.make_async_copy(x, y, sem.at[i])
        for i, (x, y) in enumerate(((a_ref, a_hbm), (b_ref, b_hbm)))
    ]
    for copy in copies:
        copy.start()
    for copy in copies:
        copy.wait()


def per_device(plane_count, tile_count, *args):
    (primal, dual, measured, weights, pix, bins_of, count, dk, db, ds, dm, dh, pk, pb, ps, pm, ph) = args
    mems, zs, rs, cols = primal.shape
    bins = dual.shape[3]
    angles, slots, blk = weights.shape[1:4]
    assert dual.shape[2] == 1 and angles == tile_count and 8 % zs == 0 and mems == NEW
    assert plane_count % 2 == 0 and tile_count % 2 == 0
    hidden = db.shape[0]
    proj_len = bins // blk * zs
    back_len = rs * cols // blk * zs
    d_span = -(-(zs + 2) * 3 // 8) * 8
    p_span = -(-(zs + 2) * (rs + 2) // 8) * 8
    cells = zs * rs
    most = max(
        (2 * zs + 3) * (mems + 1) * bins,
        2 * mems * (rs + 2) * cols,
        2 * mems * zs * cols,
        8 * proj_len * blk,
        (2 * back_len + 6 * cols // blk * zs) * blk,
    )
    vmem = pl.BlockSpec(memory_space=pltpu.VMEM)
    dma = pltpu.SemaphoreType.DMA
    operands = (
        primal, dual, measured, weights, pix, bins_of, count,
        jnp.transpose(dk, (2, 3, 4, 1, 0)), db[None], ds[None], dm, dh[None],
        jnp.transpose(pk, (1, 2, 3, 4, 0)), pb[None], ps[None], pm, ph[None],
    )
    held = pl.pallas_call(
        functools.partial(body, plane_count, tile_count),
        out_shape=(
            pltpu.VMEM(primal.shape, F32),
            pltpu.VMEM(dual.shape, F32),
        ),
        in_specs=[pl.BlockSpec(memory_space=pl.ANY)] * len(operands),
        out_specs=(vmem, vmem),
        scratch_shapes=[
            (pltpu.SMEM if x.dtype == jnp.int32 else pltpu.VMEM)(x.shape, x.dtype)
            for x in operands
            if not any(x is y for y in (weights, dual, measured))
        ]
        + [
            pltpu.VMEM((3 * hidden, 72), F32),
            pltpu.VMEM((3 * hidden, 72), F32),
            pltpu.VMEM((3, 72, 128), F32),
            dma((len(operands) - 1,)),
            pltpu.VMEM((angles, slots, blk, blk), F32),
            pltpu.VMEM((angles, 2 * blk, slots * blk), BF16),
            pltpu.VMEM((angles, slots * blk, 2 * blk), BF16),
            pltpu.VMEM((rs * cols // blk, 16, blk), F32),
            pltpu.VMEM((2, bins // blk, 16, blk), F32),
            pltpu.VMEM((tile_count, proj_len, blk), F32),
            pltpu.VMEM((tile_count - 1, proj_len, blk), F32),
            pltpu.VMEM((-(-most // (8 * blk)), 8, blk), F32),
            pltpu.VMEM((tile_count, proj_len, blk), F32),
            pltpu.VMEM((3, mems + 1, zs, 1, bins), F32),
            pltpu.VMEM((2, 3, mems + 1, 1, bins), F32),
            pltpu.VMEM((2, mems, zs, 1, cols), F32),
            pltpu.VMEM((2, mems, zs, 1, cols), F32),
            pltpu.VMEM((2, mems, rs, cols), F32),
            pltpu.VMEM((2, 2, mems, 1, cols), F32),
            pltpu.VMEM((zs + 2, 3, 8, bins), F32),
            pltpu.VMEM((zs + 2, rs + 2, 8, cols), F32),
            pltpu.VMEM((9, proj_len, blk), F32),
            pltpu.VMEM((9, back_len, blk), F32),
            pltpu.VMEM((d_span, bins), F32),
            pltpu.VMEM((p_span, cols), F32),
            pltpu.VMEM((zs * hidden, -(-9 * d_span // 128) * 128), BF16),
            pltpu.VMEM((cells * hidden, -(-9 * p_span // 128) * 128), BF16),
            pltpu.VMEM((zs * hidden, bins), F32),
            pltpu.VMEM((cells * hidden, cols), F32),
            pltpu.VMEM((zs * hidden, bins), BF16),
            pltpu.VMEM((zs * hidden, bins), BF16),
            pltpu.VMEM((cells * hidden, cols), BF16),
            pltpu.VMEM((cells * hidden, cols), BF16),
            dma((angles,)),
            dma((1,)),
            dma((1,)),
            dma((1,)),
            dma((tile_count,)),
        ]
        + [dma((1,))] * 12,
        compiler_params=pltpu.CompilerParams(
            collective_id=0, has_side_effects=True, vmem_limit_bytes=60 * 2**20
        ),
    )(*operands)
    hbm = pl.BlockSpec(memory_space=pl.ANY)
    return pl.pallas_call(
        store,
        out_shape=[jax.ShapeDtypeStruct(x.shape, F32) for x in held],
        in_specs=[vmem] * 2,
        out_specs=[hbm] * 2,
        scratch_shapes=[dma((2,))],
    )(*[pltpu.with_memory_space_constraint(x, pltpu.VMEM) for x in held])


def solution(mesh):
    in_specs = (
        P(None, "plane", "tile", None),
        P(None, "plane", "tile", None),
        P("plane", "tile", None),
        P("tile", None, None, None, None),
        P("tile", None, None),
        P(),
        P("tile", None),
    ) + (P(),) * 10
    out_specs = (P(None, "plane", "tile", None), P(None, "plane", "tile", None))
    return jax.shard_map(
        functools.partial(per_device, mesh.shape["plane"], mesh.shape["tile"]),
        mesh=mesh,
        in_specs=in_specs,
        out_specs=out_specs,
        check_vma=False,
    )
```
